32 devices in a mesh: gx: 4 (over y, core), gy: 8 (over z, x).
Axes of the slice: x: 2, y: 2, z: 4, core: 2. Of those that a mesh axis runs over, the one named last changes fastest.
Arguments:
- weighted_jacobian_strips: float32 [4096, 3, 768], P(('gx', 'gy')), may hold values from -0.3125 to 0.3125
- leading_pose_index: int32 [4096, 1], P(('gx', 'gy')), may hold values from 0 to 31; in each aligned block of 128 rows (0 to 127, 128 to 255, ...) at most 6 rows name the same one
- levenberg_shift: float32 [32, 768], P(('gx', 'gy')), may hold values from 0.05 to 0.5
- removal_flags: int32 [32], replicated, may hold values from 0 to 1, as said below
Outputs:
- schur: float32 [32, 3, 768, 768], P(('gx', 'gy'))
- coupling: float32 [32, 4, 768, 768], P(('gx', 'gy'))
The draws below stay inside these ranges and needn't reach their ends.
Inputs may be any that keep to these rules, and one draw needn't show every extreme that they name: `leading_pose_index`: within the 128 columns of one device no block is the base of more than 6 columns, and some device reaches 6. `removal_flags`: eliminated blocks lie 3 or more blocks apart around the cycle of 32 blocks.
All inputs are finite; a program needn't handle non-finite values.
Results may differ from the reference program's by a relative error of at most 0.0003.
Values sent between devices are 32-bit elements; how exact they have to be, the bound alone decides.
No kernel may reach another device: no remote copies, remote signals or barrier semaphores. Data moves between devices by JAX's collectives and lax.ppermute only.
A program may use at most 192 MiB of HBM per device.

```python
import math
import jax
import jax.numpy as jnp
import numpy as np
from jax import lax

B = 768
SURF_DEV = 128
NB = 32
SURFELS = 4096
MOST = 6
N_GX = 4
N_GY = 8


def draw_removal_flags(key, part):
    key_gaps, key_start = jax.random.split(jax.random.fold_in(key, 17))
    count_all = NB // 3
    spare_gaps = NB - 3 * count_all
    shuffled = jax.random.permutation(key_gaps, count_all)
    gap_sizes = jnp.where(shuffled < spare_gaps, 4, 3).astype(jnp.int32)
    anchor = jax.random.randint(key_start, (), 0, NB, dtype=jnp.int32)
    places = (anchor + jnp.cumsum(gap_sizes) - gap_sizes) % NB
    return jnp.zeros((NB,), jnp.int32).at[places].set(1)


def level_of(own_key, dims, pieces, low, largest):
    level = 1.0
    for axis_at, blocks in pieces:
        draws = jax.random.uniform(jax.random.fold_in(jax.random.fold_in(own_key, 6), axis_at), (blocks,), jnp.float32, low / len(pieces), largest / len(pieces))
        level = level * jnp.repeat(jnp.exp(draws), dims[axis_at] // blocks).reshape((-1,) + (1,) * (len(dims) - 1 - axis_at))
    return level


def assign_block(key, own, number, rows, amount, top, reach, lean):
    sequence = jax.random.permutation(key, amount)
    crowded, usual = shares(amount, rows * top, reach, lean, True), shares(amount, rows * top, reach, lean, False)
    places = jnp.arange(amount)

    def named(sizes, turn):
        used = int((sizes > 0).sum())
        fixed = max(1, used // 4)
        passed = fixed + (places - fixed + turn * (used - fixed)) % max(1, amount - fixed)
        return jnp.zeros((amount,), jnp.int32).at[sequence[jnp.where(places < fixed, places, passed)]].set(jnp.asarray(sizes, jnp.int32))

    sizes = jnp.where(number % 4 == 0, named(crowded, number // 4), named(usual, number - number // 4 - 1))
    mixed = jax.random.permutation(jax.random.fold_in(own, 3), amount)
    giver, sink = mixed[0:amount // 2 * 2:2], mixed[1:amount // 2 * 2:2]
    room = jnp.minimum(sizes[giver] - 1, reach - sizes[sink]) // 2
    room = jnp.where((giver == sequence[0]) | (sink == sequence[0]) | (sizes[sink] == 0), 0, jnp.maximum(room, 0))
    passed = jax.random.randint(jax.random.fold_in(own, 4), (amount // 2,), 0, 1 << 20) % (room + 1)
    sizes = sizes.at[giver].add(-passed).at[sink].add(passed)
    labels = jnp.searchsorted(jnp.cumsum(sizes), jnp.arange(rows * top), side="right").astype(jnp.int32)
    table = labels.reshape(top, rows).T
    table = table[jax.random.permutation(jax.random.fold_in(own, 1), rows)]
    turn = jax.random.randint(jax.random.fold_in(own, 2), (rows, 1), 0, top)
    return jnp.take_along_axis(table, (jnp.arange(top)[None, :] + turn) % top, axis=1)


def shares(count, total, limit, slope, full):
    portions = [(1 << 20) // math.isqrt(rank ** slope) + 1 for rank in range(1, count + 1)]
    largest = limit if full else min(limit, max(-(-total // count), total * portions[0] // sum(portions)))
    least = 1 if total - largest >= count - 1 else 0
    holding, spare = [largest] + [least] * (count - 1), total - largest - least * (count - 1)
    while spare > 0:
        free = [i for i in range(1, count) if holding[i] < largest] or [i for i in range(1, count) if holding[i] < limit]
        whole, budget = sum([portions[i] for i in free]), spare
        for i in free:
            more = min(limit - holding[i], max(1, budget * portions[i] // whole), spare)
            holding[i] = holding[i] + more
            spare = spare - more
    return np.array(holding)


def centred(key, shape, scale, reach, cuts=(), kind=jnp.bfloat16):
    result = scale * jax.random.normal(key, shape, jnp.float32)
    if cuts:
        result = result * level_of(key, shape, cuts, -0.22, 0.18)
    return jnp.clip(result, -reach, reach).astype(kind)


def setup_inputs(seed: int = 0) -> dict:
    key_of = jax.random.split(jax.random.key(seed), 5)
    weighted_jacobian_strips = centred(key_of[0], (SURFELS, 3, B), (3 * SURF_DEV) ** -0.5, 0.3125, ((0, 32),), jnp.float32)
    leading_pose_index_keys = jax.random.split(jax.random.fold_in(key_of[1], 1), SURFELS // SURF_DEV)
    leading_pose_index_turns = jax.random.permutation(jax.random.fold_in(key_of[1], 3), SURFELS // SURF_DEV)
    leading_pose_index = jax.vmap(lambda own, number: assign_block(jax.random.fold_in(key_of[1], 2), own, number, SURF_DEV, NB, 1, MOST, 2))(leading_pose_index_keys, leading_pose_index_turns).reshape((SURFELS, 1))
    levenberg_shift = jnp.clip(jnp.exp(math.log(0.5) - 2.3025851 * jax.random.uniform(key_of[2], (NB, B), jnp.float32) ** level_of(key_of[2], (NB, B), ((0, 32),), -0.2, 0.2)), 0.05, 0.5)
    removal_flags = draw_removal_flags(jax.random.fold_in(key_of[4], 71), 0)
    return dict(weighted_jacobian_strips=weighted_jacobian_strips, leading_pose_index=leading_pose_index, levenberg_shift=levenberg_shift, removal_flags=removal_flags)


def pair_gram(left_op, right_op):
    return jnp.dot(left_op.T.astype(jnp.float32), right_op.astype(jnp.float32), precision=lax.Precision.HIGHEST, preferred_element_type=jnp.float32)

def batch_gram(left_op, right_op):
    return jnp.einsum('nki,nkj->nij', left_op, right_op, precision=lax.Precision.HIGHEST)

def triangular(lower_tri, right_side):
    return jax.scipy.linalg.solve_triangular(lower_tri, right_side, lower=True)

def from_block(array, step):
    return jnp.roll(array, -step, axis=0)

def reference(weighted_jacobian_strips, leading_pose_index, levenberg_shift, removal_flags):
    count_all = weighted_jacobian_strips.shape[0]
    capacity = N_GX * N_GY * MOST
    blocks = leading_pose_index[:, 0].astype(jnp.int32)
    shuffled = jnp.argsort(blocks, stable=True).astype(jnp.int32)
    sorted_blocks = blocks[shuffled]
    first_seen = jnp.searchsorted(sorted_blocks, sorted_blocks, side='left').astype(jnp.int32)
    within = jnp.arange(count_all, dtype=jnp.int32) - first_seen
    padded = jnp.zeros((NB, capacity, 3, B), jnp.float32).at[sorted_blocks, within].set(weighted_jacobian_strips[shuffled])

    def assemble(block_id):
        own_rows = padded[block_id]
        one_back = padded[(block_id - 1) % NB]
        two_back = padded[(block_id - 2) % NB]
        diag_tile = pair_gram(own_rows[:, 0], own_rows[:, 0]) + pair_gram(one_back[:, 1], one_back[:, 1])
        diag_tile = diag_tile + pair_gram(two_back[:, 2], two_back[:, 2]) + jnp.diag(levenberg_shift[block_id])
        near_tile = pair_gram(one_back[:, 0], one_back[:, 1]) + pair_gram(two_back[:, 1], two_back[:, 2])
        far_tile = pair_gram(two_back[:, 0], two_back[:, 2])
        return jnp.stack([far_tile, near_tile, diag_tile])
    tiles = lax.map(assemble, jnp.arange(NB, dtype=jnp.int32))
    far_all = tiles[:, 0]
    near_all = tiles[:, 1]
    diagonal_blocks_full = tiles[:, 2]
    factor = jnp.linalg.cholesky(diagonal_blocks_full)
    next_all = jnp.roll(near_all, -1, axis=0)
    after_all = jnp.roll(far_all, -2, axis=0)
    right_sides = jnp.concatenate([jnp.swapaxes(far_all, 1, 2), jnp.swapaxes(near_all, 1, 2), next_all, after_all], axis=2)
    solved = jax.vmap(triangular)(factor, right_sides)
    panels = [solved[:, :, member * B:(member + 1) * B] for member in range(4)]
    coupling = jnp.stack([from_block(panels[0], 2), from_block(panels[1], 1), from_block(panels[2], -1), from_block(panels[3], -2)], axis=1)
    flag_strip = removal_flags.astype(jnp.float32)[:, None, None]
    lower_two, lower_one, upper_one, upper_two = [flag_strip * system_matrix for system_matrix in panels]
    new_diag = diagonal_blocks_full - batch_gram(from_block(lower_two, 2), from_block(lower_two, 2))
    new_diag = new_diag - batch_gram(from_block(lower_one, 1), from_block(lower_one, 1))
    new_diag = new_diag - batch_gram(from_block(upper_one, -1), from_block(upper_one, -1))
    new_diag = new_diag - batch_gram(from_block(upper_two, -2), from_block(upper_two, -2))
    new_near = near_all - batch_gram(from_block(lower_two, 1), from_block(lower_one, 1))
    new_near = new_near - batch_gram(from_block(upper_one, -2), from_block(upper_two, -2))
    new_far = far_all - batch_gram(from_block(lower_one, -1), from_block(upper_one, -1))
    prior_pose_tile_single = (jnp.roll(removal_flags, 1) > 0)[:, None, None]
    prior_pose_tile_double = (jnp.roll(removal_flags, 2) > 0)[:, None, None]
    new_near = jnp.where(prior_pose_tile_single, from_block(upper_one, -1), new_near)
    new_far = jnp.where(prior_pose_tile_double, from_block(upper_two, -2), new_far)
    current_pose_tile = (removal_flags > 0)[:, None, None]
    schur = jnp.stack([jnp.where(current_pose_tile, jnp.swapaxes(panels[0], 1, 2), new_far), jnp.where(current_pose_tile, jnp.swapaxes(panels[1], 1, 2), new_near), jnp.where(current_pose_tile, factor, new_diag)], axis=1)
    return (schur, coupling)
```

```python
import functools
import math

import jax
import jax.numpy as jnp
from jax import lax
from jax.experimental import pallas as pl
from jax.experimental.pallas import tpu as pltpu
from jax.sharding import PartitionSpec as P

AXES = ("gx", "gy")
TILE = 128
GROUP = 8
WIDE = 256
NT = (((1,), (1,)), ((), ()))
TN = (((0,), (0,)), ((), ()))
NN = (((1,), (0,)), ((), ()))
VMEM_SPEC = pl.BlockSpec(memory_space=pltpu.VMEM)


def passed_along(value, steps):
    count = lax.axis_size(AXES)
    pairs = [(source, (source + steps) % count) for source in range(count)]
    return lax.ppermute(value, AXES, pairs)


def product(left, right, dims, precision=lax.Precision.HIGHEST):
    return lax.dot_general(
        left, right, dims, precision=precision, preferred_element_type=jnp.float32
    )


def bucket_kernel(count, capacity, index_ref, strips_ref, out_ref, rows_ref):
    surfels = strips_ref.shape[1]
    width = strips_ref.shape[2]
    lane_tiles = width // WIDE
    index = index_ref[...]
    base = lax.broadcasted_iota(jnp.int32, (count, surfels), 0)
    hot = (base == index).astype(jnp.float32)
    first = lax.broadcasted_iota(jnp.int32, (surfels, surfels), 0)
    second = lax.broadcasted_iota(jnp.int32, (surfels, surfels), 1)
    ahead = (first < second).astype(jnp.float32)
    earlier = product(hot, ahead, NN)
    within = jnp.sum(earlier * hot, axis=0, keepdims=True).astype(jnp.int32)
    period = GROUP // math.gcd(capacity, GROUP)
    for piece in range(3):
        moved = index + piece
        moved = jnp.where(moved >= count, moved - count, moved)
        slot = moved * capacity + within
        row = lax.broadcasted_iota(jnp.int32, (count * capacity, surfels), 0)
        pick = (row == slot).astype(jnp.bfloat16)
        values = strips_ref[piece]
        high = values.astype(jnp.bfloat16)
        rest = values - high.astype(jnp.float32)
        middle = rest.astype(jnp.bfloat16)
        low = (rest - middle.astype(jnp.float32)).astype(jnp.bfloat16)
        rows_ref[...] = product(
            jnp.concatenate([pick, pick, pick], axis=1),
            jnp.concatenate([high, middle, low], axis=0),
            NN,
            lax.Precision.DEFAULT,
        )

        def spread(turn, carry, piece=piece):
            start = pl.multiple_of(turn * (period * capacity), GROUP)
            for tile in range(lane_tiles):
                block = rows_ref[pl.ds(start, period * capacity), WIDE * tile : WIDE * (tile + 1)]
                for member in range(period):
                    begin = (piece * lane_tiles + tile) * capacity
                    out_ref[turn * period + member, begin : begin + capacity, :] = block[
                        member * capacity : (member + 1) * capacity
                    ]
            return carry

        lax.fori_loop(0, count // period, spread, 0)


def bucketed(index_row, strips, count, capacity):
    width = strips.shape[2]
    return pl.pallas_call(
        functools.partial(bucket_kernel, count, capacity),
        out_shape=jax.ShapeDtypeStruct(
            (count, 3 * (width // WIDE) * capacity, WIDE), jnp.float32
        ),
        in_specs=[VMEM_SPEC, VMEM_SPEC],
        out_specs=VMEM_SPEC,
        scratch_shapes=[pltpu.VMEM((count * capacity, width), jnp.float32)],
        name="bucket",
    )(index_row, strips)


def regroup_kernel(capacity, in_ref, out_ref):
    count = in_ref.shape[0]
    width = out_ref.shape[1]
    lane_tiles = width // WIDE
    period = GROUP // math.gcd(capacity, GROUP)

    def gather(turn, carry):
        for piece in range(3):
            for tile in range(lane_tiles):
                begin = (piece * lane_tiles + tile) * capacity
                block = jnp.concatenate(
                    [
                        in_ref[turn * period + member, begin : begin + capacity, :]
                        for member in range(period)
                    ],
                    axis=0,
                )
                start = pl.multiple_of(
                    piece * count * capacity + turn * (period * capacity), GROUP
                )
                out_ref[
                    pl.ds(start, period * capacity), WIDE * tile : WIDE * (tile + 1)
                ] = block
        return carry

    lax.fori_loop(0, count // period, gather, 0)


def regrouped(chunks, capacity, width):
    count = chunks.shape[0]
    return pl.pallas_call(
        functools.partial(regroup_kernel, capacity),
        out_shape=jax.ShapeDtypeStruct((3 * count * capacity, width), jnp.float32),
        in_specs=[VMEM_SPEC],
        out_specs=VMEM_SPEC,
        name="regroup",
    )(chunks)


def full(value):
    return jnp.broadcast_to(value, (GROUP, TILE))


def tile_factor(rows):
    groups = len(rows)
    sub = lax.broadcasted_iota(jnp.int32, (GROUP, TILE), 0)
    lane = lax.broadcasted_iota(jnp.int32, (GROUP, TILE), 1)
    unit = [
        jnp.where(lane == sub + GROUP * g, 1.0, 0.0).astype(jnp.float32) for g in range(groups)
    ]
    uppers = []
    inverses = []
    eight = range(GROUP)
    for p in range(groups):
        strip, mark = rows[p], unit[p]
        cols = [full(strip[:, GROUP * p + k : GROUP * p + k + 1]) for k in eight]
        m = [[full(cols[k][i : i + 1, :]) if k <= i else None for k in eight] for i in eight]
        r = [None] * GROUP
        for j in eight:
            r[j] = lax.rsqrt(m[j][j])
            for i in range(j + 1, GROUP):
                m[i][j] = m[i][j] * r[j]
            for k in range(j + 1, GROUP):
                for i in range(k, GROUP):
                    m[i][k] = m[i][k] - m[i][j] * m[k][j]

        def forward(block):
            done = []
            for j in eight:
                x = full(block[j : j + 1, :])
                for i in range(j):
                    x = x - m[j][i] * done[i]
                done.append(x * r[j])
            return done

        def backward(given):
            done = [None] * GROUP
            for j in reversed(eight):
                x = given[j]
                for i in range(j + 1, GROUP):
                    x = x - m[i][j] * done[i]
                done[j] = x * r[j]
            return done

        def joined(given):
            x = given[0]
            for j in range(1, GROUP):
                x = jnp.where(sub == j, given[j], x)
            return x

        u = forward(strip)
        t = forward(mark)
        uppers.append(joined(u))
        inverses.append(joined(t))
        if p == groups - 1:
            break
        v = backward(u)
        w = backward(t)
        for g in range(p + 1, groups):
            x, y = rows[g], unit[g]
            for k in eight:
                c = full(rows[g][:, GROUP * p + k : GROUP * p + k + 1])
                x = x - c * v[k]
                y = y - c * w[k]
            rows[g], unit[g] = x, y
    return uppers, inverses


def factor_kernel(side, x_ref, shift_ref, low_ref, y_ref, gram_ref, turned_ref, inv_ref):
    width = x_ref.shape[1]
    depth = x_ref.shape[0]
    tiles = width // TILE
    row = lax.broadcasted_iota(jnp.int32, (TILE, TILE), 0)
    col = lax.broadcasted_iota(jnp.int32, (TILE, TILE), 1)
    turned_ref[...] = x_ref[...].T
    y_ref[...] = x_ref[...]

    def tile_at(number):
        return pl.ds(pl.multiple_of(number * TILE, TILE), TILE)

    for i in range(tiles):
        rows = slice(i * TILE, (i + 1) * TILE)
        ahead = slice(0, (i + 1) * TILE)
        low_ref[rows, ahead] = product(turned_ref[rows, :], x_ref[:, ahead], NN)
        low_ref[rows, rows] = low_ref[rows, rows] + jnp.where(
            row == col, jnp.broadcast_to(shift_ref[:, rows], (TILE, TILE)), 0.0
        )
        if i + 1 < tiles:
            low_ref[rows, (i + 1) * TILE :] = jnp.zeros(
                (TILE, width - (i + 1) * TILE), jnp.float32
            )

    def step(j, carry):
        cols = tile_at(j)

        def reduced(ref, rows):
            def less(k, value):
                return value - product(ref[rows, tile_at(k)], low_ref[cols, tile_at(k)], NT)

            return lax.fori_loop(0, j, less, ref[rows, cols])

        tile = reduced(low_ref, cols)
        uppers, inverses = tile_factor(
            [tile[GROUP * g : GROUP * (g + 1)] for g in range(TILE // GROUP)]
        )
        for g, piece in enumerate(inverses):
            inv_ref[GROUP * g : GROUP * (g + 1), :] = piece
        upper = jnp.concatenate(uppers, axis=0)
        low_ref[cols, cols] = jnp.where(col <= row, upper.T, 0.0)

        def below(i, inner):
            rows = tile_at(i)
            low_ref[rows, cols] = product(reduced(low_ref, rows), inv_ref[...], NT)
            return inner

        lax.fori_loop(j + 1, tiles, below, 0)

        def sides(i, inner):
            rows = pl.ds(pl.multiple_of(i * side, GROUP), side)
            y_ref[rows, cols] = product(reduced(y_ref, rows), inv_ref[...], NT)
            return inner

        lax.fori_loop(0, depth // side, sides, 0)
        return carry

    lax.fori_loop(0, tiles, step, 0)
    gram_ref[...] = product(y_ref[side:, :], y_ref[: 2 * side, :], NT)


def factored(x, shift, side):
    depth, width = x.shape
    return pl.pallas_call(
        functools.partial(factor_kernel, side),
        out_shape=(
            jax.ShapeDtypeStruct((width, width), jnp.float32),
            jax.ShapeDtypeStruct((depth, width), jnp.float32),
            jax.ShapeDtypeStruct((2 * side, 2 * side), jnp.float32),
        ),
        in_specs=[VMEM_SPEC, VMEM_SPEC],
        out_specs=(VMEM_SPEC, VMEM_SPEC, VMEM_SPEC),
        scratch_shapes=[
            pltpu.VMEM((width, depth), jnp.float32),
            pltpu.VMEM((TILE, TILE), jnp.float32),
        ],
        compiler_params=pltpu.CompilerParams(vmem_limit_bytes=48 << 20),
        cost_estimate=pl.CostEstimate(
            flops=40_000_000_000, bytes_accessed=3 * depth * width * 4, transcendentals=0
        ),
        name="factor",
    )(x, shift)


def local(weighted_jacobian_strips, leading_pose_index, levenberg_shift, removal_flags):
    count = lax.axis_size(AXES)
    own = lax.axis_index(AXES)
    surfels, _, width = weighted_jacobian_strips.shape
    capacity = max(2, (3 * surfels + 2 * count - 1) // (2 * count))
    side = count * capacity

    chunks = bucketed(
        leading_pose_index.reshape(1, surfels),
        weighted_jacobian_strips.transpose(1, 0, 2),
        count,
        capacity,
    )
    chunks = lax.all_to_all(chunks, AXES, split_axis=0, concat_axis=0, tiled=True)
    x = regrouped(chunks, capacity, width)

    flags = removal_flags.astype(jnp.float32)

    def flag_at(shift_by):
        return lax.dynamic_index_in_dim(flags, (own + shift_by) % count, keepdims=False)

    below = passed_along(x[: 2 * side], 1)
    second_below = passed_along(x[:side], 2)
    low, y, gram = factored(x, levenberg_shift, side)
    extra = passed_along(jnp.where(flag_at(0) > 0, below[side:], x[2 * side :]), 1)
    y_below = passed_along(y[: 2 * side], 1)
    y_above = passed_along(y[side:], -1)
    y_second_below = passed_along(y[:side], 2)
    y_second_above = passed_along(y[2 * side :], -2)
    gram_below = passed_along(gram[side:], 1)
    gram_second_below = passed_along(gram[:side, :side], 2)

    high = lax.Precision.HIGH
    couple = [
        product(y_second_above, x[:side], TN, high),
        product(y_above, x[: 2 * side], TN, high),
        product(y_below, x[side:], TN, high),
        product(y_second_below, x[2 * side :], TN, high),
    ]

    def weighed(part, rows, flag):
        return flag * product(product(part, part, NT, high), rows, NN, high)

    from_second_above = weighed(y_second_above, x[:side], flag_at(2))
    from_above = weighed(y_above, x[: 2 * side], flag_at(1))
    from_below = weighed(y_below, x[side:], flag_at(-1))
    from_second_below = weighed(y_second_below, x[2 * side :], flag_at(-2))
    rest = jnp.concatenate(
        [
            x[:side] - from_second_above - from_above[:side],
            x[side : 2 * side] - from_above[side:] - from_below[:side],
            x[2 * side :] - from_below[side:] - from_second_below,
        ],
        axis=0,
    )
    new_diag = product(x, rest, TN, high) + jnp.diag(levenberg_shift[0])
    chosen = jnp.where(flag_at(0) > 0, y, x)
    near = product(
        jnp.concatenate([below, extra], axis=0),
        jnp.concatenate(
            [
                chosen[side : 2 * side] - from_above[side:],
                chosen[2 * side :] - from_second_below,
                -flag_at(-2) * product(gram_second_below, x[2 * side :], NN, high),
            ],
            axis=0,
        ),
        TN,
        high,
    )
    far = product(
        jnp.concatenate([second_below, extra], axis=0),
        jnp.concatenate(
            [
                chosen[2 * side :] - from_below[side:],
                -flag_at(-1) * product(gram_below, x[side:], NN, high),
            ],
            axis=0,
        ),
        TN,
        high,
    )
    schur = jnp.stack(
        [
            jnp.where(flag_at(-2) > 0, couple[3], far),
            jnp.where(flag_at(-1) > 0, couple[2], near),
            jnp.where(flag_at(0) > 0, low, new_diag),
        ]
    )
    return schur[None], jnp.stack(couple)[None]


def solution(mesh):
    in_specs = (P(AXES, None, None), P(AXES, None), P(AXES, None), P())
    out_specs = (P(AXES, None, None, None), P(AXES, None, None, None))
    return jax.shard_map(local, mesh=mesh, in_specs=in_specs, out_specs=out_specs, check_vma=False)
```

```python
import functools
import math

import jax
import jax.numpy as jnp
from jax import lax
from jax.experimental import pallas as pl
from jax.experimental.pallas import tpu as pltpu
from jax.sharding import PartitionSpec as P


AXES = ("gx", "gy")
TILE = 128
GROUP = 8
WIDE = 256
NT = (((1,), (1,)), ((), ()))
NN = (((1,), (0,)), ((), ()))
VMEM_SPEC = pl.BlockSpec(memory_space=pltpu.VMEM)
SMEM_SPEC = pl.BlockSpec(memory_space=pltpu.SMEM)
ANY_SPEC = pl.BlockSpec(memory_space=pl.ANY)
PIECES = ((0, 2), (1, 3), (0, 1), (2, 3))


def passed_along(value, steps):
    count = lax.axis_size(AXES)
    pairs = [(source, (source + steps) % count) for source in range(count)]
    return lax.ppermute(value, AXES, pairs)


def product(left, right, dims, precision=lax.Precision.HIGHEST):
    return lax.dot_general(
        left, right, dims, precision=precision, preferred_element_type=jnp.float32
    )


def bucket_kernel(count, capacity, index_ref, strips_ref, out_ref, rows_ref):
    surfels = strips_ref.shape[1]
    width = strips_ref.shape[2]
    lane_tiles = width // WIDE
    index = index_ref[...]
    base = lax.broadcasted_iota(jnp.int32, (count, surfels), 0)
    hot = (base == index).astype(jnp.float32)
    first = lax.broadcasted_iota(jnp.int32, (surfels, surfels), 0)
    second = lax.broadcasted_iota(jnp.int32, (surfels, surfels), 1)
    ahead = (first < second).astype(jnp.float32)
    earlier = product(hot, ahead, NN)
    within = jnp.sum(earlier * hot, axis=0, keepdims=True).astype(jnp.int32)
    period = GROUP // math.gcd(capacity, GROUP)
    for piece in range(3):
        moved = index + piece
        moved = jnp.where(moved >= count, moved - count, moved)
        slot = moved * capacity + within
        row = lax.broadcasted_iota(jnp.int32, (count * capacity, surfels), 0)
        pick = (row == slot).astype(jnp.bfloat16)
        values = strips_ref[piece]
        high = values.astype(jnp.bfloat16)
        rest = values - high.astype(jnp.float32)
        middle = rest.astype(jnp.bfloat16)
        low = (rest - middle.astype(jnp.float32)).astype(jnp.bfloat16)
        rows_ref[...] = product(
            jnp.concatenate([pick, pick, pick], axis=1),
            jnp.concatenate([high, middle, low], axis=0),
            NN,
            lax.Precision.DEFAULT,
        )

        def spread(turn, carry, piece=piece):
            start = pl.multiple_of(turn * (period * capacity), GROUP)
            for tile in range(lane_tiles):
                block = rows_ref[pl.ds(start, period * capacity), WIDE * tile : WIDE * (tile + 1)]
                for member in range(period):
                    begin = (piece * lane_tiles + tile) * capacity
                    out_ref[turn * period + member, begin : begin + capacity, :] = block[
                        member * capacity : (member + 1) * capacity
                    ]
            return carry

        lax.fori_loop(0, count // period, spread, 0)


def bucketed(index_row, strips, count, capacity):
    width = strips.shape[2]
    return pl.pallas_call(
        functools.partial(bucket_kernel, count, capacity),
        out_shape=jax.ShapeDtypeStruct(
            (count, 3 * (width // WIDE) * capacity, WIDE), jnp.float32
        ),
        in_specs=[VMEM_SPEC, VMEM_SPEC],
        out_specs=VMEM_SPEC,
        scratch_shapes=[pltpu.VMEM((count * capacity, width), jnp.float32)],
        name="bucket",
    )(index_row, strips)


def regroup_kernel(capacity, in_ref, out_ref, two_ref, one_ref):
    count = in_ref.shape[0]
    width = out_ref.shape[1]
    lane_tiles = width // WIDE
    period = GROUP // math.gcd(capacity, GROUP)

    def gather(turn, carry):
        for piece in range(3):
            for tile in range(lane_tiles):
                begin = (piece * lane_tiles + tile) * capacity
                block = jnp.concatenate(
                    [
                        in_ref[turn * period + member, begin : begin + capacity, :]
                        for member in range(period)
                    ],
                    axis=0,
                )
                start = pl.multiple_of(
                    piece * count * capacity + turn * (period * capacity), GROUP
                )
                out_ref[
                    pl.ds(start, period * capacity), WIDE * tile : WIDE * (tile + 1)
                ] = block
        return carry

    lax.fori_loop(0, count // period, gather, 0)
    side = count * capacity
    two_ref[...] = out_ref[: 2 * side, :]
    one_ref[...] = out_ref[:side, :]


def regrouped(chunks, capacity, width):
    side = chunks.shape[0] * capacity
    return pl.pallas_call(
        functools.partial(regroup_kernel, capacity),
        out_shape=tuple(
            jax.ShapeDtypeStruct((parts * side, width), jnp.float32) for parts in (3, 2, 1)
        ),
        in_specs=[VMEM_SPEC],
        out_specs=(VMEM_SPEC,) * 3,
        name="regroup",
    )(chunks)


def full(value):
    return jnp.broadcast_to(value, (GROUP, TILE))


def tile_factor(rows):
    groups = len(rows)
    sub = lax.broadcasted_iota(jnp.int32, (GROUP, TILE), 0)
    lane = lax.broadcasted_iota(jnp.int32, (GROUP, TILE), 1)
    unit = [
        jnp.where(lane == sub + GROUP * g, 1.0, 0.0).astype(jnp.float32) for g in range(groups)
    ]
    uppers = []
    inverses = []
    eight = range(GROUP)
    for p in range(groups):
        strip, mark = rows[p], unit[p]
        cols = [full(strip[:, GROUP * p + k : GROUP * p + k + 1]) for k in eight]
        m = [[full(cols[k][i : i + 1, :]) if k <= i else None for k in eight] for i in eight]
        r = [None] * GROUP
        for j in eight:
            r[j] = lax.rsqrt(m[j][j])
            for i in range(j + 1, GROUP):
                m[i][j] = m[i][j] * r[j]
            for k in range(j + 1, GROUP):
                for i in range(k, GROUP):
                    m[i][k] = m[i][k] - m[i][j] * m[k][j]

        def forward(block):
            done = []
            for j in eight:
                x = full(block[j : j + 1, :])
                for i in range(j):
                    x = x - m[j][i] * done[i]
                done.append(x * r[j])
            return done

        def backward(given):
            done = [None] * GROUP
            for j in reversed(eight):
                x = given[j]
                for i in range(j + 1, GROUP):
                    x = x - m[i][j] * done[i]
                done[j] = x * r[j]
            return done

        def joined(given):
            x = given[0]
            for j in range(1, GROUP):
                x = jnp.where(sub == j, given[j], x)
            return x

        u = forward(strip)
        t = forward(mark)
        uppers.append(joined(u))
        inverses.append(joined(t))
        if p == groups - 1:
            break
        v = backward(u)
        w = backward(t)
        for g in range(p + 1, groups):
            x, y = rows[g], unit[g]
            for k in eight:
                c = full(rows[g][:, GROUP * p + k : GROUP * p + k + 1])
                x = x - c * v[k]
                y = y - c * w[k]
            rows[g], unit[g] = x, y
    return uppers, inverses


def factor_steps(side, low_ref, y_ref, inv_ref, first, last):
    width = low_ref.shape[1]
    depth = y_ref.shape[0]
    tiles = width // TILE
    row = lax.broadcasted_iota(jnp.int32, (TILE, TILE), 0)
    col = lax.broadcasted_iota(jnp.int32, (TILE, TILE), 1)

    def tile_at(number):
        return pl.ds(pl.multiple_of(number * TILE, TILE), TILE)

    def step(j, carry):
        cols = tile_at(j)

        def reduced(ref, rows):
            def less(k, value):
                return value - product(ref[rows, tile_at(k)], low_ref[cols, tile_at(k)], NT)

            return lax.fori_loop(0, j, less, ref[rows, cols])

        tile = reduced(low_ref, cols)
        uppers, inverses = tile_factor(
            [tile[GROUP * g : GROUP * (g + 1)] for g in range(TILE // GROUP)]
        )
        for g, piece in enumerate(inverses):
            inv_ref[GROUP * g : GROUP * (g + 1), :] = piece
        upper = jnp.concatenate(uppers, axis=0)
        low_ref[cols, cols] = jnp.where(col <= row, upper.T, 0.0)

        def below(i, inner):
            rows = tile_at(i)
            low_ref[rows, cols] = product(reduced(low_ref, rows), inv_ref[...], NT)
            return inner

        lax.fori_loop(j + 1, tiles, below, 0)

        def sides(i, inner):
            rows = pl.ds(pl.multiple_of(i * side, GROUP), side)
            y_ref[rows, cols] = product(reduced(y_ref, rows), inv_ref[...], NT)
            return inner

        lax.fori_loop(0, depth // side, sides, 0)
        return carry

    lax.fori_loop(first, last, step, 0)


def put_pieces(side, work_ref, lanes, outs):
    for out_ref, (start, stop) in zip(outs, PIECES):
        out_ref[...] = work_ref[start * side : stop * side, lanes]


def piece_shapes(side, lanes):
    return tuple(
        jax.ShapeDtypeStruct(((stop - start) * side, lanes), jnp.float32) for start, stop in PIECES
    )


def first_factor_kernel(side, cut, x_ref, shift_ref, low_ref, y_ref, *rest):
    outs, (work_ref, turned_ref, inv_ref) = rest[:4], rest[4:]
    width = x_ref.shape[1]
    tiles = width // TILE
    row = lax.broadcasted_iota(jnp.int32, (TILE, TILE), 0)
    col = lax.broadcasted_iota(jnp.int32, (TILE, TILE), 1)
    turned_ref[...] = x_ref[...].T
    work_ref[...] = x_ref[...]
    for i in range(tiles):
        rows = slice(i * TILE, (i + 1) * TILE)
        ahead = slice(0, (i + 1) * TILE)
        low_ref[rows, ahead] = product(turned_ref[rows, :], x_ref[:, ahead], NN)
        low_ref[rows, rows] = low_ref[rows, rows] + jnp.where(
            row == col, jnp.broadcast_to(shift_ref[:, rows], (TILE, TILE)), 0.0
        )
        if i + 1 < tiles:
            low_ref[rows, (i + 1) * TILE :] = jnp.zeros(
                (TILE, width - (i + 1) * TILE), jnp.float32
            )
    factor_steps(side, low_ref, work_ref, inv_ref, 0, cut // TILE)
    y_ref[...] = work_ref[:, :cut]
    put_pieces(side, work_ref, slice(0, cut), outs)


def second_factor_kernel(side, cut, x_ref, part_ref, y_in_ref, low_ref, *rest):
    outs, (gram_one_ref, gram_two_ref, work_ref, inv_ref) = rest[:4], rest[4:]
    width = x_ref.shape[1]
    low_ref[...] = part_ref[...]
    work_ref[:, :cut] = y_in_ref[...]
    work_ref[:, cut:] = x_ref[:, cut:]
    factor_steps(side, low_ref, work_ref, inv_ref, cut // TILE, width // TILE)
    put_pieces(side, work_ref, slice(cut, width), outs)
    gram_one_ref[...] = product(work_ref[2 * side :, :], work_ref[: 2 * side, :], NT)
    gram_two_ref[...] = product(work_ref[side : 2 * side, :], work_ref[:side, :], NT)


def first_factored(x, shift, side, cut):
    depth, width = x.shape
    return pl.pallas_call(
        functools.partial(first_factor_kernel, side, cut),
        out_shape=(
            jax.ShapeDtypeStruct((width, width), jnp.float32),
            jax.ShapeDtypeStruct((depth, cut), jnp.float32),
            *piece_shapes(side, cut),
        ),
        in_specs=[VMEM_SPEC, VMEM_SPEC],
        out_specs=(VMEM_SPEC,) * 6,
        scratch_shapes=[
            pltpu.VMEM((depth, width), jnp.float32),
            pltpu.VMEM((width, depth), jnp.float32),
            pltpu.VMEM((TILE, TILE), jnp.float32),
        ],
        compiler_params=pltpu.CompilerParams(vmem_limit_bytes=40 << 20),
        cost_estimate=pl.CostEstimate(
            flops=20_000_000_000, bytes_accessed=3 * depth * width * 4, transcendentals=0
        ),
        name="first_factor",
    )(x, shift)


def second_factored(x, part, y, side, cut):
    depth, width = x.shape
    return pl.pallas_call(
        functools.partial(second_factor_kernel, side, cut),
        out_shape=(
            jax.ShapeDtypeStruct((width, width), jnp.float32),
            *piece_shapes(side, width - cut),
            jax.ShapeDtypeStruct((side, 2 * side), jnp.float32),
            jax.ShapeDtypeStruct((side, side), jnp.float32),
        ),
        in_specs=[VMEM_SPEC, VMEM_SPEC, VMEM_SPEC],
        out_specs=(VMEM_SPEC,) * 7,
        scratch_shapes=[
            pltpu.VMEM((depth, width), jnp.float32),
            pltpu.VMEM((TILE, TILE), jnp.float32),
        ],
        compiler_params=pltpu.CompilerParams(vmem_limit_bytes=40 << 20),
        cost_estimate=pl.CostEstimate(
            flops=20_000_000_000, bytes_accessed=3 * depth * width * 4, transcendentals=0
        ),
        name="second_factor",
    )(x, part, y)


def halves(value):
    high = value.astype(jnp.bfloat16)
    return high, (value - high.astype(jnp.float32)).astype(jnp.bfloat16)


def product_of_halves(left, right, dims):
    total = product(left[0], right[0], dims, lax.Precision.DEFAULT)
    total = total + product(left[0], right[1], dims, lax.Precision.DEFAULT)
    return total + product(left[1], right[0], dims, lax.Precision.DEFAULT)


def near_product(left, right, dims):
    return product_of_halves(halves(left), halves(right), dims)


def put_coupling(side, start, y_refs, x_ref, buffer_ref, out_ref, sems):
    rows = buffer_ref.shape[1]
    width = x_ref.shape[1]
    copies = []
    for place, (number, begin, end) in enumerate(((3, 0, 1), (1, 0, 2), (0, 1, 3), (2, 2, 3))):
        left = halves(y_refs[number][...].T)
        for lanes in range(0, width, WIDE):
            right = halves(x_ref[begin * side : end * side, lanes : lanes + WIDE])
            buffer_ref[place, :, lanes : lanes + WIDE] = product_of_halves(left, right, NN)
        copy = pltpu.make_async_copy(
            buffer_ref.at[place], out_ref.at[place, pl.ds(start, rows), :], sems.at[place]
        )
        copy.start()
        copies.append(copy)
    return copies


def early_kernel(side, x_ref, y0_ref, y1_ref, y2_ref, y3_ref, out_ref, buffer_ref, sems):
    for copy in put_coupling(side, 0, (y0_ref, y1_ref, y2_ref, y3_ref), x_ref, buffer_ref, out_ref, sems):
        copy.wait()


def early(x, y_parts, side):
    width = x.shape[1]
    cut = y_parts[0].shape[1]
    return pl.pallas_call(
        functools.partial(early_kernel, side),
        out_shape=jax.ShapeDtypeStruct((4, width, width), jnp.float32),
        in_specs=[VMEM_SPEC] * 5,
        out_specs=ANY_SPEC,
        scratch_shapes=[
            pltpu.VMEM((4, cut, width), jnp.float32),
            pltpu.SemaphoreType.DMA((4,)),
        ],
        compiler_params=pltpu.CompilerParams(vmem_limit_bytes=32 << 20),
        cost_estimate=pl.CostEstimate(
            flops=8_000_000_000, bytes_accessed=4 * width * width * 4, transcendentals=0
        ),
        name="early",
    )(x, *y_parts)


def late_kernel(side, flags_ref, *refs):
    (
        x_ref,
        shift_ref,
        below_ref,
        second_ref,
        extra_ref,
        low_ref,
        gram_one_ref,
        gram_two_ref,
    ) = refs[:8]
    mine = refs[8:10]
    firsts, lasts = refs[10:14], refs[14:18]
    partial_ref, schur_ref, coupling_ref = refs[18:21]
    buffer_ref, tile_ref, rest_ref, near_ref, far_ref, sems, outs = refs[21:]
    width = x_ref.shape[1]
    cut = firsts[0].shape[1]
    copies = put_coupling(side, cut, lasts, x_ref, buffer_ref, coupling_ref, sems)
    own, above, second_above, under, second_under = [flags_ref[k] > 0 for k in range(5)]
    one, two, three = slice(0, side), slice(side, 2 * side), slice(2 * side, 3 * side)
    pair, tail = slice(0, 2 * side), slice(side, 3 * side)
    rest_ref[...] = x_ref[...]
    near_ref[three, :] = jnp.zeros((side, width), jnp.float32)
    far_ref[two, :] = jnp.zeros((side, width), jnp.float32)

    @pl.when(own)
    def _():
        near_ref[pair, :cut] = mine[0][...]
        near_ref[pair, cut:] = mine[1][...]
        far_ref[one, :cut] = mine[0][side:, :]
        far_ref[one, cut:] = mine[1][side:, :]

    @pl.when(jnp.logical_not(own))
    def _():
        near_ref[pair, :] = x_ref[tail, :]
        far_ref[one, :] = x_ref[three, :]

    def weighed(number, rows):
        gram = near_product(firsts[number][...], firsts[number][...], NT)
        gram = gram + near_product(lasts[number][...], lasts[number][...], NT)
        return near_product(gram, x_ref[rows, :], NN)

    @pl.when(second_above)
    def _():
        rest_ref[one, :] = rest_ref[one, :] - weighed(3, one)

    @pl.when(above)
    def _():
        term = weighed(1, pair)
        rest_ref[pair, :] = rest_ref[pair, :] - term
        near_ref[one, :] = near_ref[one, :] - term[side:]

    @pl.when(under)
    def _():
        term = weighed(0, tail)
        rest_ref[tail, :] = rest_ref[tail, :] - term
        far_ref[one, :] = far_ref[one, :] - term[side:]
        far_ref[two, :] = -near_product(gram_one_ref[...], x_ref[tail, :], NN)

    @pl.when(second_under)
    def _():
        term = weighed(2, three)
        rest_ref[three, :] = rest_ref[three, :] - term
        near_ref[two, :] = near_ref[two, :] - term
        near_ref[three, :] = -near_product(gram_two_ref[...], x_ref[three, :], NN)

    def put(place):
        copy = pltpu.make_async_copy(tile_ref.at[place], schur_ref.at[place], outs.at[place])
        copy.start()
        return copy

    def fill(place, left, right_ref):
        left = halves(left.T)
        for lanes in range(0, width, WIDE):
            tile_ref[place, :, lanes : lanes + WIDE] = product_of_halves(
                left, halves(right_ref[:, lanes : lanes + WIDE]), NN
            )

    def from_coupling(place, member):
        copy = pltpu.make_async_copy(
            partial_ref.at[member, pl.ds(0, cut), :],
            tile_ref.at[place, pl.ds(0, cut), :],
            outs.at[place],
        )
        copy.start()
        tile_ref[place, cut:, :] = buffer_ref[member]
        copy.wait()

    @pl.when(own)
    def _():
        tile_ref[2] = low_ref[...]

    @pl.when(jnp.logical_not(own))
    def _():
        fill(2, x_ref[...], rest_ref)
        for i in range(width // TILE):
            rows = slice(i * TILE, (i + 1) * TILE)
            row = lax.broadcasted_iota(jnp.int32, (TILE, TILE), 0)
            col = lax.broadcasted_iota(jnp.int32, (TILE, TILE), 1)
            tile_ref[2, rows, rows] = tile_ref[2, rows, rows] + jnp.where(
                row == col, jnp.broadcast_to(shift_ref[:, rows], (TILE, TILE)), 0.0
            )

    copies.append(put(2))

    @pl.when(under)
    def _():
        from_coupling(1, 2)

    @pl.when(jnp.logical_not(under))
    def _():
        fill(1, jnp.concatenate([below_ref[...], extra_ref[...]], axis=0), near_ref)

    copies.append(put(1))

    @pl.when(second_under)
    def _():
        from_coupling(0, 3)

    @pl.when(jnp.logical_not(second_under))
    def _():
        fill(0, jnp.concatenate([second_ref[...], extra_ref[...]], axis=0), far_ref)

    copies.append(put(0))
    for copy in copies:
        copy.wait()


def late(flags, x, shift, below, second_below, extra, low, grams, mine, firsts, lasts, partial, side):
    depth, width = x.shape
    rest = lasts[0].shape[1]
    return pl.pallas_call(
        functools.partial(late_kernel, side),
        out_shape=(
            jax.ShapeDtypeStruct((3, width, width), jnp.float32),
            jax.ShapeDtypeStruct((4, width, width), jnp.float32),
        ),
        in_specs=[SMEM_SPEC] + [VMEM_SPEC] * 18 + [ANY_SPEC],
        out_specs=(ANY_SPEC, ANY_SPEC),
        input_output_aliases={19: 1},
        scratch_shapes=[
            pltpu.VMEM((4, rest, width), jnp.float32),
            pltpu.VMEM((3, width, width), jnp.float32),
            pltpu.VMEM((depth, width), jnp.float32),
            pltpu.VMEM((depth, width), jnp.float32),
            pltpu.VMEM((2 * side, width), jnp.float32),
            pltpu.SemaphoreType.DMA((4,)),
            pltpu.SemaphoreType.DMA((3,)),
        ],
        compiler_params=pltpu.CompilerParams(vmem_limit_bytes=56 << 20),
        cost_estimate=pl.CostEstimate(
            flops=12_000_000_000, bytes_accessed=7 * width * width * 4, transcendentals=0
        ),
        name="late",
    )(flags, x, shift, below, second_below, extra, low, *grams, *mine, *firsts, *lasts, partial)


def pick_kernel(flags_ref, first_ref, second_ref, out_ref):
    side = out_ref.shape[0]

    @pl.when(flags_ref[0] > 0)
    def _():
        out_ref[...] = first_ref[side:, :]

    @pl.when(flags_ref[0] <= 0)
    def _():
        out_ref[...] = second_ref[2 * side :, :]


def picked(flags, below, x, side):
    return pl.pallas_call(
        pick_kernel,
        out_shape=jax.ShapeDtypeStruct((side, x.shape[1]), jnp.float32),
        in_specs=[SMEM_SPEC, VMEM_SPEC, VMEM_SPEC],
        out_specs=VMEM_SPEC,
        name="pick",
    )(flags, below, x)


def local(weighted_jacobian_strips, leading_pose_index, levenberg_shift, removal_flags):
    count = lax.axis_size(AXES)
    own = lax.axis_index(AXES)
    surfels, _, width = weighted_jacobian_strips.shape
    capacity = max(2, (3 * surfels + 2 * count - 1) // (2 * count))
    side = count * capacity
    cut = width // TILE // 2 * TILE
    flags = removal_flags[(own + jnp.array((0, 1, 2, -1, -2), jnp.int32)) % count]

    chunks = bucketed(
        leading_pose_index.reshape(1, surfels),
        weighted_jacobian_strips.transpose(1, 0, 2),
        count,
        capacity,
    )
    chunks = lax.all_to_all(chunks, AXES, split_axis=0, concat_axis=0, tiled=True)
    x, two, one = regrouped(chunks, capacity, width)

    def sent_parts(parts):
        return [passed_along(part, steps) for part, steps in zip(parts, (1, -1, 2, -2))]

    below = passed_along(two, 1)
    second_below = passed_along(one, 2)
    part, y_first, *first_pieces = first_factored(x, levenberg_shift, side, cut)
    extra = picked(flags, below, x, side)
    extra = passed_along(extra, 1)
    firsts = sent_parts(first_pieces)
    low, *last_pieces, gram_one, gram_two = second_factored(x, part, y_first, side, cut)
    lasts = sent_parts(last_pieces)
    grams = (passed_along(gram_one, 1), passed_along(gram_two, 2))
    partial = early(x, firsts, side)
    schur, coupling = late(
        flags,
        x,
        levenberg_shift,
        below,
        second_below,
        extra,
        low,
        grams,
        (first_pieces[1], last_pieces[1]),
        firsts,
        lasts,
        partial,
        side,
    )
    return schur[None], coupling[None]


def solution(mesh):
    in_specs = (P(AXES, None, None), P(AXES, None), P(AXES, None), P())
    out_specs = (P(AXES, None, None, None), P(AXES, None, None, None))

    return jax.shard_map(local, mesh=mesh, in_specs=in_specs, out_specs=out_specs, check_vma=False)
```

```python
import functools
import math

import jax
import jax.numpy as jnp
from jax import lax
from jax.experimental import pallas as pl
from jax.experimental.pallas import tpu as pltpu
from jax.sharding import PartitionSpec as P


AXES = ("gx", "gy")
TILE = 128
GROUP = 8
WIDE = 256
NT = (((1,), (1,)), ((), ()))
NN = (((1,), (0,)), ((), ()))
VMEM_SPEC = pl.BlockSpec(memory_space=pltpu.VMEM)
SMEM_SPEC = pl.BlockSpec(memory_space=pltpu.SMEM)
ANY_SPEC = pl.BlockSpec(memory_space=pl.ANY)
PIECES = ((0, 2), (1, 3), (0, 1), (2, 3))


def passed_along(value, steps):
    count = lax.axis_size(AXES)
    pairs = [(source, (source + steps) % count) for source in range(count)]
    return lax.ppermute(value, AXES, pairs)


def product(left, right, dims, precision=lax.Precision.HIGHEST):
    return lax.dot_general(
        left, right, dims, precision=precision, preferred_element_type=jnp.float32
    )


def bucket_kernel(count, capacity, index_ref, strips_ref, out_ref, rows_ref):
    surfels = strips_ref.shape[1]
    width = strips_ref.shape[2]
    lane_tiles = width // WIDE
    index = index_ref[...]
    base = lax.broadcasted_iota(jnp.int32, (count, surfels), 0)
    hot = (base == index).astype(jnp.float32)
    first = lax.broadcasted_iota(jnp.int32, (surfels, surfels), 0)
    second = lax.broadcasted_iota(jnp.int32, (surfels, surfels), 1)
    ahead = (first < second).astype(jnp.float32)
    earlier = product(hot, ahead, NN)
    within = jnp.sum(earlier * hot, axis=0, keepdims=True).astype(jnp.int32)
    period = GROUP // math.gcd(capacity, GROUP)
    for piece in range(3):
        moved = index + piece
        moved = jnp.where(moved >= count, moved - count, moved)
        slot = moved * capacity + within
        row = lax.broadcasted_iota(jnp.int32, (count * capacity, surfels), 0)
        pick = (row == slot).astype(jnp.bfloat16)
        values = strips_ref[piece]
        high = values.astype(jnp.bfloat16)
        rest = values - high.astype(jnp.float32)
        middle = rest.astype(jnp.bfloat16)
        low = (rest - middle.astype(jnp.float32)).astype(jnp.bfloat16)
        rows_ref[...] = product(
            jnp.concatenate([pick, pick, pick], axis=1),
            jnp.concatenate([high, middle, low], axis=0),
            NN,
            lax.Precision.DEFAULT,
        )

        def spread(turn, carry, piece=piece):
            start = pl.multiple_of(turn * (period * capacity), GROUP)
            for tile in range(lane_tiles):
                block = rows_ref[pl.ds(start, period * capacity), WIDE * tile : WIDE * (tile + 1)]
                for member in range(period):
                    begin = (piece * lane_tiles + tile) * capacity
                    out_ref[turn * period + member, begin : begin + capacity, :] = block[
                        member * capacity : (member + 1) * capacity
                    ]
            return carry

        lax.fori_loop(0, count // period, spread, 0)


def bucketed(index_row, strips, count, capacity):
    width = strips.shape[2]
    return pl.pallas_call(
        functools.partial(bucket_kernel, count, capacity),
        out_shape=jax.ShapeDtypeStruct(
            (count, 3 * (width // WIDE) * capacity, WIDE), jnp.float32
        ),
        in_specs=[VMEM_SPEC, VMEM_SPEC],
        out_specs=VMEM_SPEC,
        scratch_shapes=[pltpu.VMEM((count * capacity, width), jnp.float32)],
        name="bucket",
    )(index_row, strips)


def regroup_kernel(capacity, in_ref, out_ref, two_ref, one_ref):
    count = in_ref.shape[0]
    width = out_ref.shape[1]
    lane_tiles = width // WIDE
    period = GROUP // math.gcd(capacity, GROUP)

    def gather(turn, carry):
        for piece in range(3):
            for tile in range(lane_tiles):
                begin = (piece * lane_tiles + tile) * capacity
                block = jnp.concatenate(
                    [
                        in_ref[turn * period + member, begin : begin + capacity, :]
                        for member in range(period)
                    ],
                    axis=0,
                )
                start = pl.multiple_of(
                    piece * count * capacity + turn * (period * capacity), GROUP
                )
                out_ref[
                    pl.ds(start, period * capacity), WIDE * tile : WIDE * (tile + 1)
                ] = block
        return carry

    lax.fori_loop(0, count // period, gather, 0)
    side = count * capacity
    two_ref[...] = out_ref[: 2 * side, :]
    one_ref[...] = out_ref[2 * side :, :]


def regrouped(chunks, capacity, width):
    side = chunks.shape[0] * capacity
    return pl.pallas_call(
        functools.partial(regroup_kernel, capacity),
        out_shape=tuple(
            jax.ShapeDtypeStruct((parts * side, width), jnp.float32) for parts in (3, 2, 1)
        ),
        in_specs=[VMEM_SPEC],
        out_specs=(VMEM_SPEC,) * 3,
        compiler_params=pltpu.CompilerParams(vmem_limit_bytes=16 << 20),
        name="regroup",
    )(chunks)


def full(value):
    return jnp.broadcast_to(value, (GROUP, TILE))


def tile_factor(rows):
    groups = len(rows)
    sub = lax.broadcasted_iota(jnp.int32, (GROUP, TILE), 0)
    lane = lax.broadcasted_iota(jnp.int32, (GROUP, TILE), 1)
    unit = [
        jnp.where(lane == sub + GROUP * g, 1.0, 0.0).astype(jnp.float32) for g in range(groups)
    ]
    uppers = []
    inverses = []
    eight = range(GROUP)
    for p in range(groups):
        strip, mark = rows[p], unit[p]
        cols = [full(strip[:, GROUP * p + k : GROUP * p + k + 1]) for k in eight]
        m = [[full(cols[k][i : i + 1, :]) if k <= i else None for k in eight] for i in eight]
        r = [None] * GROUP
        for j in eight:
            r[j] = lax.rsqrt(m[j][j])
            for i in range(j + 1, GROUP):
                m[i][j] = m[i][j] * r[j]
            for k in range(j + 1, GROUP):
                for i in range(k, GROUP):
                    m[i][k] = m[i][k] - m[i][j] * m[k][j]

        def forward(block):
            done = []
            for j in eight:
                x = full(block[j : j + 1, :])
                for i in range(j):
                    x = x - m[j][i] * done[i]
                done.append(x * r[j])
            return done

        def backward(given):
            done = [None] * GROUP
            for j in reversed(eight):
                x = given[j]
                for i in range(j + 1, GROUP):
                    x = x - m[i][j] * done[i]
                done[j] = x * r[j]
            return done

        def joined(given):
            x = given[0]
            for j in range(1, GROUP):
                x = jnp.where(sub == j, given[j], x)
            return x

        u = forward(strip)
        t = forward(mark)
        uppers.append(joined(u))
        inverses.append(joined(t))
        if p == groups - 1:
            break
        v = backward(u)
        w = backward(t)
        for g in range(p + 1, groups):
            x, y = rows[g], unit[g]
            for k in eight:
                c = full(rows[g][:, GROUP * p + k : GROUP * p + k + 1])
                x = x - c * v[k]
                y = y - c * w[k]
            rows[g], unit[g] = x, y
    return uppers, inverses


def factor_steps(side, low_ref, y_ref, inv_ref, first, last):
    width = low_ref.shape[1]
    depth = y_ref.shape[0]
    tiles = width // TILE
    row = lax.broadcasted_iota(jnp.int32, (TILE, TILE), 0)
    col = lax.broadcasted_iota(jnp.int32, (TILE, TILE), 1)

    def tile_at(number):
        return pl.ds(pl.multiple_of(number * TILE, TILE), TILE)

    def step(j, carry):
        cols = tile_at(j)

        def reduced(ref, rows):
            def less(k, value):
                return value - product(ref[rows, tile_at(k)], low_ref[cols, tile_at(k)], NT)

            return lax.fori_loop(0, j, less, ref[rows, cols])

        tile = reduced(low_ref, cols)
        uppers, inverses = tile_factor(
            [tile[GROUP * g : GROUP * (g + 1)] for g in range(TILE // GROUP)]
        )
        for g, piece in enumerate(inverses):
            inv_ref[GROUP * g : GROUP * (g + 1), :] = piece
        upper = jnp.concatenate(uppers, axis=0)
        low_ref[cols, cols] = jnp.where(col <= row, upper.T, 0.0)

        def below(i, inner):
            rows = tile_at(i)
            low_ref[rows, cols] = product(reduced(low_ref, rows), inv_ref[...], NT)
            return inner

        lax.fori_loop(j + 1, tiles, below, 0)

        def sides(i, inner):
            rows = pl.ds(pl.multiple_of(i * side, GROUP), side)
            y_ref[rows, cols] = product(reduced(y_ref, rows), inv_ref[...], NT)
            return inner

        lax.fori_loop(0, depth // side, sides, 0)
        return carry

    lax.fori_loop(first, last, step, 0)


def put_pieces(side, work_ref, lanes, outs):
    for out_ref, (start, stop) in zip(outs, PIECES):
        out_ref[...] = work_ref[start * side : stop * side, lanes]


def piece_shapes(side, lanes):
    return tuple(
        jax.ShapeDtypeStruct(((stop - start) * side, lanes), jnp.float32) for start, stop in PIECES
    )


def first_factor_kernel(side, cut, x_ref, shift_ref, low_ref, y_ref, *rest):
    outs, (work_ref, turned_ref, inv_ref) = rest[:4], rest[4:]
    width = x_ref.shape[1]
    tiles = width // TILE
    row = lax.broadcasted_iota(jnp.int32, (TILE, TILE), 0)
    col = lax.broadcasted_iota(jnp.int32, (TILE, TILE), 1)
    turned_ref[...] = x_ref[...].T
    work_ref[...] = x_ref[...]
    for i in range(tiles):
        rows = slice(i * TILE, (i + 1) * TILE)
        ahead = slice(0, (i + 1) * TILE)
        low_ref[rows, ahead] = product(turned_ref[rows, :], x_ref[:, ahead], NN)
        low_ref[rows, rows] = low_ref[rows, rows] + jnp.where(
            row == col, jnp.broadcast_to(shift_ref[:, rows], (TILE, TILE)), 0.0
        )
        if i + 1 < tiles:
            low_ref[rows, (i + 1) * TILE :] = jnp.zeros(
                (TILE, width - (i + 1) * TILE), jnp.float32
            )
    factor_steps(side, low_ref, work_ref, inv_ref, 0, cut // TILE)
    y_ref[...] = work_ref[:, :cut]
    put_pieces(side, work_ref, slice(0, cut), outs)


def second_factor_kernel(side, cut, x_ref, part_ref, y_in_ref, low_ref, *rest):
    outs, (gram_one_ref, gram_two_ref, work_ref, inv_ref) = rest[:4], rest[4:]
    width = x_ref.shape[1]
    low_ref[...] = part_ref[...]
    work_ref[:, :cut] = y_in_ref[...]
    work_ref[:, cut:] = x_ref[:, cut:]
    factor_steps(side, low_ref, work_ref, inv_ref, cut // TILE, width // TILE)
    put_pieces(side, work_ref, slice(cut, width), outs)
    gram_one_ref[...] = product(work_ref[2 * side :, :], work_ref[: 2 * side, :], NT)
    gram_two_ref[...] = product(work_ref[side : 2 * side, :], work_ref[:side, :], NT)


def first_factored(x, shift, side, cut):
    depth, width = x.shape
    return pl.pallas_call(
        functools.partial(first_factor_kernel, side, cut),
        out_shape=(
            jax.ShapeDtypeStruct((width, width), jnp.float32),
            jax.ShapeDtypeStruct((depth, cut), jnp.float32),
            *piece_shapes(side, cut),
        ),
        in_specs=[VMEM_SPEC, VMEM_SPEC],
        out_specs=(VMEM_SPEC,) * 6,
        scratch_shapes=[
            pltpu.VMEM((depth, width), jnp.float32),
            pltpu.VMEM((width, depth), jnp.float32),
            pltpu.VMEM((TILE, TILE), jnp.float32),
        ],
        compiler_params=pltpu.CompilerParams(vmem_limit_bytes=24 << 20),
        cost_estimate=pl.CostEstimate(
            flops=20_000_000_000, bytes_accessed=3 * depth * width * 4, transcendentals=0
        ),
        name="first_factor",
    )(x, shift)


def second_factored(x, part, y, side, cut):
    depth, width = x.shape
    return pl.pallas_call(
        functools.partial(second_factor_kernel, side, cut),
        out_shape=(
            jax.ShapeDtypeStruct((width, width), jnp.float32),
            *piece_shapes(side, width - cut),
            jax.ShapeDtypeStruct((side, 2 * side), jnp.float32),
            jax.ShapeDtypeStruct((side, side), jnp.float32),
        ),
        in_specs=[VMEM_SPEC, VMEM_SPEC, VMEM_SPEC],
        out_specs=(VMEM_SPEC,) * 7,
        scratch_shapes=[
            pltpu.VMEM((depth, width), jnp.float32),
            pltpu.VMEM((TILE, TILE), jnp.float32),
        ],
        compiler_params=pltpu.CompilerParams(vmem_limit_bytes=24 << 20),
        cost_estimate=pl.CostEstimate(
            flops=20_000_000_000, bytes_accessed=3 * depth * width * 4, transcendentals=0
        ),
        name="second_factor",
    )(x, part, y)


def halves(value):
    high = value.astype(jnp.bfloat16)
    return high, (value - high.astype(jnp.float32)).astype(jnp.bfloat16)


def product_of_halves(left, right, dims):
    total = product(left[0], right[0], dims, lax.Precision.DEFAULT)
    total = total + product(left[0], right[1], dims, lax.Precision.DEFAULT)
    return total + product(left[1], right[0], dims, lax.Precision.DEFAULT)


def near_product(left, right, dims):
    return product_of_halves(halves(left), halves(right), dims)


def lanes_at(number):
    return pl.ds(pl.multiple_of(number * WIDE, WIDE), WIDE)


def tall_product(left_refs, rows, depth, right_at, put, width):
    left = tuple(ref[:rows, :depth] for ref in left_refs)

    def block(number, carry):
        put(lanes_at(number), product_of_halves(left, halves(right_at(lanes_at(number))), NN))
        return carry

    lax.fori_loop(0, width // WIDE, block, 0)


def keep_halves(left_refs, value):
    rows, depth = value.shape
    high, low = halves(value)
    left_refs[0][:rows, :depth] = high
    left_refs[1][:rows, :depth] = low


def put_coupling(side, start, y_refs, x_ref, buffer_ref, left_refs, out_ref, sems):
    rows = buffer_ref.shape[1]
    width = x_ref.shape[1]
    copies = []
    for place, (number, begin, end) in enumerate(((3, 0, 1), (1, 0, 2), (0, 1, 3), (2, 2, 3))):
        keep_halves(left_refs, y_refs[number][...].T)

        def put(lanes, value, place=place):
            buffer_ref[place, :, lanes] = value

        tall_product(
            left_refs,
            rows,
            (end - begin) * side,
            lambda lanes, begin=begin, end=end: x_ref[begin * side : end * side, lanes],
            put,
            width,
        )
        copy = pltpu.make_async_copy(
            buffer_ref.at[place], out_ref.at[place, pl.ds(start, rows), :], sems.at[place]
        )
        copy.start()
        copies.append(copy)
    return copies


def early_kernel(side, x_ref, y0_ref, y1_ref, y2_ref, y3_ref, out_ref, buffer_ref, high_ref, less_ref, sems):
    y_refs = (y0_ref, y1_ref, y2_ref, y3_ref)
    left_refs = (high_ref, less_ref)
    for copy in put_coupling(side, 0, y_refs, x_ref, buffer_ref, left_refs, out_ref, sems):
        copy.wait()


def early(x, y_parts, side):
    width = x.shape[1]
    cut = y_parts[0].shape[1]
    return pl.pallas_call(
        functools.partial(early_kernel, side),
        out_shape=jax.ShapeDtypeStruct((4, width, width), jnp.float32),
        in_specs=[VMEM_SPEC] * 5,
        out_specs=ANY_SPEC,
        scratch_shapes=[
            pltpu.VMEM((4, cut, width), jnp.float32),
            pltpu.VMEM((cut, 2 * side), jnp.bfloat16),
            pltpu.VMEM((cut, 2 * side), jnp.bfloat16),
            pltpu.SemaphoreType.DMA((4,)),
        ],
        compiler_params=pltpu.CompilerParams(vmem_limit_bytes=24 << 20),
        cost_estimate=pl.CostEstimate(
            flops=8_000_000_000, bytes_accessed=4 * width * width * 4, transcendentals=0
        ),
        name="early",
    )(x, *y_parts)


def late_kernel(side, flags_ref, *refs):
    (
        x_ref,
        shift_ref,
        direct_ref,
        onward_ref,
        second_ref,
        extra_ref,
        low_ref,
        gram_one_ref,
        gram_two_ref,
    ) = refs[:9]
    mine = refs[9:11]
    firsts, lasts = refs[11:15], refs[15:19]
    partial_ref, schur_ref, coupling_ref = refs[19:22]
    buffer_ref, tile_ref, rest_ref, near_ref, far_ref, high_ref, less_ref, sems, outs = refs[22:]
    left_refs = (high_ref, less_ref)
    width = x_ref.shape[1]
    cut = firsts[0].shape[1]
    copies = put_coupling(side, cut, lasts, x_ref, buffer_ref, left_refs, coupling_ref, sems)
    own, above, second_above, under, second_under = [flags_ref[k] > 0 for k in range(5)]
    one, two, three = slice(0, side), slice(side, 2 * side), slice(2 * side, 3 * side)
    pair, tail = slice(0, 2 * side), slice(side, 3 * side)
    rest_ref[...] = x_ref[...]
    near_ref[three, :] = jnp.zeros((side, width), jnp.float32)
    far_ref[two, :] = jnp.zeros((side, width), jnp.float32)

    @pl.when(own)
    def _():
        near_ref[pair, :cut] = mine[0][...]
        near_ref[pair, cut:] = mine[1][...]
        far_ref[one, :cut] = mine[0][side:, :]
        far_ref[one, cut:] = mine[1][side:, :]

    @pl.when(jnp.logical_not(own))
    def _():
        near_ref[pair, :] = x_ref[tail, :]
        far_ref[one, :] = x_ref[three, :]

    def weighed(number, rows):
        gram = near_product(firsts[number][...], firsts[number][...], NT)
        gram = gram + near_product(lasts[number][...], lasts[number][...], NT)
        return near_product(gram, x_ref[rows, :], NN)

    @pl.when(second_above)
    def _():
        rest_ref[one, :] = rest_ref[one, :] - weighed(3, one)

    @pl.when(above)
    def _():
        term = weighed(1, pair)
        rest_ref[pair, :] = rest_ref[pair, :] - term
        near_ref[one, :] = near_ref[one, :] - term[side:]

    @pl.when(under)
    def _():
        term = weighed(0, tail)
        rest_ref[tail, :] = rest_ref[tail, :] - term
        far_ref[one, :] = far_ref[one, :] - term[side:]
        far_ref[two, :] = -near_product(gram_one_ref[...], x_ref[tail, :], NN)

    @pl.when(second_under)
    def _():
        term = weighed(2, three)
        rest_ref[three, :] = rest_ref[three, :] - term
        near_ref[two, :] = near_ref[two, :] - term
        near_ref[three, :] = -near_product(gram_two_ref[...], x_ref[three, :], NN)

    def put(place):
        copy = pltpu.make_async_copy(tile_ref.at[place], schur_ref.at[place], outs.at[place])
        copy.start()
        return copy

    def fill(place, left, right_ref):
        keep_halves(left_refs, left.T)

        def put(lanes, value):
            tile_ref[place, :, lanes] = value

        tall_product(
            left_refs, width, left.shape[0], lambda lanes: right_ref[:, lanes], put, width
        )

    def from_coupling(place, member):
        copy = pltpu.make_async_copy(
            partial_ref.at[member, pl.ds(0, cut), :],
            tile_ref.at[place, pl.ds(0, cut), :],
            outs.at[place],
        )
        copy.start()
        tile_ref[place, cut:, :] = buffer_ref[member]
        copy.wait()

    @pl.when(own)
    def _():
        tile_ref[2] = low_ref[...]

    @pl.when(jnp.logical_not(own))
    def _():
        fill(2, x_ref[...], rest_ref)
        for i in range(width // TILE):
            rows = slice(i * TILE, (i + 1) * TILE)
            row = lax.broadcasted_iota(jnp.int32, (TILE, TILE), 0)
            col = lax.broadcasted_iota(jnp.int32, (TILE, TILE), 1)
            tile_ref[2, rows, rows] = tile_ref[2, rows, rows] + jnp.where(
                row == col, jnp.broadcast_to(shift_ref[:, rows], (TILE, TILE)), 0.0
            )

    copies.append(put(2))

    @pl.when(under)
    def _():
        from_coupling(1, 2)

    @pl.when(jnp.logical_not(under))
    def _():
        below = direct_ref[...] + onward_ref[...]
        fill(1, jnp.concatenate([below, extra_ref[...]], axis=0), near_ref)

    copies.append(put(1))

    @pl.when(second_under)
    def _():
        from_coupling(0, 3)

    @pl.when(jnp.logical_not(second_under))
    def _():
        fill(0, second_ref[...], far_ref)

    copies.append(put(0))
    for copy in copies:
        copy.wait()


def late(flags, x, shift, received, low, grams, mine, firsts, lasts, partial, side):
    depth, width = x.shape
    rest = lasts[0].shape[1]
    return pl.pallas_call(
        functools.partial(late_kernel, side),
        out_shape=(
            jax.ShapeDtypeStruct((3, width, width), jnp.float32),
            jax.ShapeDtypeStruct((4, width, width), jnp.float32),
        ),
        in_specs=[SMEM_SPEC] + [VMEM_SPEC] * 19 + [ANY_SPEC],
        out_specs=(ANY_SPEC, ANY_SPEC),
        input_output_aliases={20: 1},
        scratch_shapes=[
            pltpu.VMEM((4, rest, width), jnp.float32),
            pltpu.VMEM((3, width, width), jnp.float32),
            pltpu.VMEM((depth, width), jnp.float32),
            pltpu.VMEM((depth, width), jnp.float32),
            pltpu.VMEM((2 * side, width), jnp.float32),
            pltpu.VMEM((width, depth), jnp.bfloat16),
            pltpu.VMEM((width, depth), jnp.bfloat16),
            pltpu.SemaphoreType.DMA((4,)),
            pltpu.SemaphoreType.DMA((3,)),
        ],
        compiler_params=pltpu.CompilerParams(vmem_limit_bytes=40 << 20),
        cost_estimate=pl.CostEstimate(
            flops=12_000_000_000, bytes_accessed=7 * width * width * 4, transcendentals=0
        ),
        name="late",
    )(flags, x, shift, *received, low, *grams, *mine, *firsts, *lasts, partial)


def local(weighted_jacobian_strips, leading_pose_index, levenberg_shift, removal_flags):
    count = lax.axis_size(AXES)
    own = lax.axis_index(AXES)
    surfels, _, width = weighted_jacobian_strips.shape
    capacity = max(2, (3 * surfels + 2 * count - 1) // (2 * count))
    side = count * capacity
    cut = width // TILE // 2 * TILE
    flags = removal_flags[(own + jnp.array((0, 1, 2, -1, -2), jnp.int32)) % count]

    chunks = bucketed(
        leading_pose_index.reshape(1, surfels),
        weighted_jacobian_strips.transpose(1, 0, 2),
        count,
        capacity,
    )
    chunks = lax.all_to_all(chunks, AXES, split_axis=0, concat_axis=0, tiled=True)
    x, two, last = regrouped(chunks, capacity, width)

    def sent_parts(parts):
        return [passed_along(part, steps) for part, steps in zip(parts, (1, -1, 2, -2))]

    direct = lax.ppermute(two, AXES, [(k, k + 1) for k in range(0, count, 2)])
    second = passed_along(two, 2)
    part, y_first, *first_pieces = first_factored(x, levenberg_shift, side, cut)
    onward = lax.ppermute(second, AXES, [(k + 1, k) for k in range(0, count, 2)])
    extra = passed_along(last, 1)
    firsts = sent_parts(first_pieces)
    low, *last_pieces, gram_one, gram_two = second_factored(x, part, y_first, side, cut)
    lasts = sent_parts(last_pieces)
    grams = (passed_along(gram_one, 1), passed_along(gram_two, 2))
    partial = early(x, firsts, side)
    schur, coupling = late(
        flags,
        x,
        levenberg_shift,
        (direct, onward, second, extra),
        low,
        grams,
        (first_pieces[1], last_pieces[1]),
        firsts,
        lasts,
        partial,
        side,
    )
    return schur[None], coupling[None]


def solution(mesh):
    in_specs = (P(AXES, None, None), P(AXES, None), P(AXES, None), P())
    out_specs = (P(AXES, None, None, None), P(AXES, None, None, None))

    return jax.shard_map(local, mesh=mesh, in_specs=in_specs, out_specs=out_specs, check_vma=False)
```

```python
import functools
import math

import jax
import jax.numpy as jnp
from jax import lax
from jax.experimental import pallas as pl
from jax.experimental.pallas import tpu as pltpu
from jax.sharding import PartitionSpec as P


AXES = ("gx", "gy")
TILE = 128
GROUP = 8
WIDE = 256
PARTS = 3
NT = (((1,), (1,)), ((), ()))
NN = (((1,), (0,)), ((), ()))
VMEM_SPEC = pl.BlockSpec(memory_space=pltpu.VMEM)
SMEM_SPEC = pl.BlockSpec(memory_space=pltpu.SMEM)
ANY_SPEC = pl.BlockSpec(memory_space=pl.ANY)
PIECES = ((0, 2), (1, 3), (0, 1), (2, 3))


def passed_along(value, steps):
    count = lax.axis_size(AXES)
    pairs = [(source, (source + steps) % count) for source in range(count)]
    return lax.ppermute(value, AXES, pairs)


def product(left, right, dims, precision=lax.Precision.HIGHEST):
    return lax.dot_general(
        left, right, dims, precision=precision, preferred_element_type=jnp.float32
    )


def bucket_kernel(count, capacity, index_ref, strips_ref, out_ref, rows_ref):
    surfels = strips_ref.shape[1]
    width = strips_ref.shape[2]
    lane_tiles = width // WIDE
    index = index_ref[...]
    base = lax.broadcasted_iota(jnp.int32, (count, surfels), 0)
    hot = (base == index).astype(jnp.float32)
    first = lax.broadcasted_iota(jnp.int32, (surfels, surfels), 0)
    second = lax.broadcasted_iota(jnp.int32, (surfels, surfels), 1)
    ahead = (first < second).astype(jnp.float32)
    earlier = product(hot, ahead, NN)
    within = jnp.sum(earlier * hot, axis=0, keepdims=True).astype(jnp.int32)
    period = GROUP // math.gcd(capacity, GROUP)
    for piece in range(3):
        moved = index + piece
        moved = jnp.where(moved >= count, moved - count, moved)
        slot = moved * capacity + within
        row = lax.broadcasted_iota(jnp.int32, (count * capacity, surfels), 0)
        pick = (row == slot).astype(jnp.bfloat16)
        values = strips_ref[piece]
        high = values.astype(jnp.bfloat16)
        rest = values - high.astype(jnp.float32)
        middle = rest.astype(jnp.bfloat16)
        low = (rest - middle.astype(jnp.float32)).astype(jnp.bfloat16)
        rows_ref[...] = product(
            jnp.concatenate([pick, pick, pick], axis=1),
            jnp.concatenate([high, middle, low], axis=0),
            NN,
            lax.Precision.DEFAULT,
        )

        def spread(turn, carry, piece=piece):
            start = pl.multiple_of(turn * (period * capacity), GROUP)
            for tile in range(lane_tiles):
                block = rows_ref[pl.ds(start, period * capacity), WIDE * tile : WIDE * (tile + 1)]
                for member in range(period):
                    begin = (piece * lane_tiles + tile) * capacity
                    out_ref[turn * period + member, begin : begin + capacity, :] = block[
                        member * capacity : (member + 1) * capacity
                    ]
            return carry

        lax.fori_loop(0, count // period, spread, 0)


def bucketed(index_row, strips, count, capacity):
    width = strips.shape[2]
    return pl.pallas_call(
        functools.partial(bucket_kernel, count, capacity),
        out_shape=jax.ShapeDtypeStruct(
            (count, 3 * (width // WIDE) * capacity, WIDE), jnp.float32
        ),
        in_specs=[VMEM_SPEC, VMEM_SPEC],
        out_specs=VMEM_SPEC,
        scratch_shapes=[pltpu.VMEM((count * capacity, width), jnp.float32)],
        name="bucket",
    )(index_row, strips)


def regroup_kernel(capacity, in_ref, out_ref, two_ref, one_ref):
    count = in_ref.shape[0]
    width = out_ref.shape[1]
    lane_tiles = width // WIDE
    period = GROUP // math.gcd(capacity, GROUP)

    def gather(turn, carry):
        for piece in range(3):
            for tile in range(lane_tiles):
                begin = (piece * lane_tiles + tile) * capacity
                block = jnp.concatenate(
                    [
                        in_ref[turn * period + member, begin : begin + capacity, :]
                        for member in range(period)
                    ],
                    axis=0,
                )
                start = pl.multiple_of(
                    piece * count * capacity + turn * (period * capacity), GROUP
                )
                out_ref[
                    pl.ds(start, period * capacity), WIDE * tile : WIDE * (tile + 1)
                ] = block
        return carry

    lax.fori_loop(0, count // period, gather, 0)
    side = count * capacity
    two_ref[...] = out_ref[: 2 * side, :]
    one_ref[...] = out_ref[2 * side :, :]


def regrouped(chunks, capacity, width):
    side = chunks.shape[0] * capacity
    return pl.pallas_call(
        functools.partial(regroup_kernel, capacity),
        out_shape=tuple(
            jax.ShapeDtypeStruct((parts * side, width), jnp.float32) for parts in (3, 2, 1)
        ),
        in_specs=[VMEM_SPEC],
        out_specs=(VMEM_SPEC,) * 3,
        compiler_params=pltpu.CompilerParams(vmem_limit_bytes=16 << 20),
        name="regroup",
    )(chunks)


def full(value):
    return jnp.broadcast_to(value, (GROUP, TILE))


def tile_factor(rows):
    groups = len(rows)
    sub = lax.broadcasted_iota(jnp.int32, (GROUP, TILE), 0)
    lane = lax.broadcasted_iota(jnp.int32, (GROUP, TILE), 1)
    unit = [
        jnp.where(lane == sub + GROUP * g, 1.0, 0.0).astype(jnp.float32) for g in range(groups)
    ]
    uppers = []
    inverses = []
    eight = range(GROUP)
    for p in range(groups):
        strip, mark = rows[p], unit[p]
        cols = [full(strip[:, GROUP * p + k : GROUP * p + k + 1]) for k in eight]
        m = [[full(cols[k][i : i + 1, :]) if k <= i else None for k in eight] for i in eight]
        r = [None] * GROUP
        for j in eight:
            r[j] = lax.rsqrt(m[j][j])
            for i in range(j + 1, GROUP):
                m[i][j] = m[i][j] * r[j]
            for k in range(j + 1, GROUP):
                for i in range(k, GROUP):
                    m[i][k] = m[i][k] - m[i][j] * m[k][j]

        def forward(block):
            done = []
            for j in eight:
                x = full(block[j : j + 1, :])
                for i in range(j):
                    x = x - m[j][i] * done[i]
                done.append(x * r[j])
            return done

        def backward(given):
            done = [None] * GROUP
            for j in reversed(eight):
                x = given[j]
                for i in range(j + 1, GROUP):
                    x = x - m[i][j] * done[i]
                done[j] = x * r[j]
            return done

        def joined(given):
            x = given[0]
            for j in range(1, GROUP):
                x = jnp.where(sub == j, given[j], x)
            return x

        u = forward(strip)
        t = forward(mark)
        uppers.append(joined(u))
        inverses.append(joined(t))
        if p == groups - 1:
            break
        v = backward(u)
        w = backward(t)
        for g in range(p + 1, groups):
            x, y = rows[g], unit[g]
            for k in eight:
                c = full(rows[g][:, GROUP * p + k : GROUP * p + k + 1])
                x = x - c * v[k]
                y = y - c * w[k]
            rows[g], unit[g] = x, y
    return uppers, inverses


def halves(value):
    high = value.astype(jnp.bfloat16)
    return high, (value - high.astype(jnp.float32)).astype(jnp.bfloat16)


def product_of_halves(left, right, dims):
    total = product(left[0], right[0], dims, lax.Precision.DEFAULT)
    total = total + product(left[0], right[1], dims, lax.Precision.DEFAULT)
    return total + product(left[1], right[0], dims, lax.Precision.DEFAULT)


def lanes_at(number):
    return pl.ds(pl.multiple_of(number * WIDE, WIDE), WIDE)


def tall_product(left_refs, rows, depth, right_at, put, width):
    left = tuple(ref[:rows, :depth] for ref in left_refs)

    def block(number, carry):
        put(lanes_at(number), product_of_halves(left, halves(right_at(lanes_at(number))), NN))
        return carry

    lax.fori_loop(0, width // WIDE, block, 0)


def keep_halves(left_refs, value):
    rows, depth = value.shape
    high, low = halves(value)
    left_refs[0][:rows, :depth] = high
    left_refs[1][:rows, :depth] = low


def piece_shapes(side, lanes):
    return tuple(
        jax.ShapeDtypeStruct(((stop - start) * side, lanes), jnp.float32) for start, stop in PIECES
    )


def part_kernel(side, bounds, number, *refs):
    first, last = bounds[number], bounds[number + 1]
    final = number == len(bounds) - 2
    x_ref, start_ref = refs[:2]
    before = refs[2 : 2 + 2 * number]
    refs = refs[2 + 2 * number :]
    low_ref, outs = refs[0], refs[1:5]
    gram_refs, refs = (refs[5:7], refs[7:]) if final else ((), refs[5:])
    inv_ref, low_high_ref, low_less_ref, y_high_ref, y_less_ref = refs[:5]
    depth, width = x_ref.shape
    begin, end = first * TILE, last * TILE
    reach = end - TILE
    row = lax.broadcasted_iota(jnp.int32, (TILE, TILE), 0)
    col = lax.broadcasted_iota(jnp.int32, (TILE, TILE), 1)

    if number == 0:
        turned = refs[5:7]
        keep_halves(turned, x_ref[...].T)

        def gram(lanes, value):
            low_ref[:, lanes] = value

        tall_product(turned, width, depth, lambda lanes: x_ref[:, lanes], gram, width)
        for i in range(width // TILE):
            rows = slice(i * TILE, (i + 1) * TILE)
            low_ref[rows, rows] = low_ref[rows, rows] + jnp.where(
                row == col, jnp.broadcast_to(start_ref[:, rows], (TILE, TILE)), 0.0
            )
    else:
        low_ref[...] = start_ref[...]
        high, less = halves(start_ref[:, :begin])
        low_high_ref[:, :begin] = high
        low_less_ref[:, :begin] = less
        for k in range(number):
            lanes = slice(bounds[k] * TILE, bounds[k + 1] * TILE)
            for ref, rows in ((before[2 * k], slice(0, 2 * side)), (before[2 * k + 1], slice(2 * side, 3 * side))):
                high, less = halves(ref[...])
                y_high_ref[rows, lanes] = high
                y_less_ref[rows, lanes] = less
    for ref in (low_high_ref, low_less_ref):
        ref[:, begin:] = jnp.zeros((width, end - begin), jnp.bfloat16)
    for ref in (y_high_ref, y_less_ref):
        ref[:, begin:] = jnp.zeros((depth, end - begin), jnp.bfloat16)

    def step(j, carry):
        start = pl.multiple_of(j * TILE, TILE)
        cols = pl.ds(start, TILE)
        local = pl.ds(pl.multiple_of((j - first) * TILE, TILE), TILE)

        def reduced(value, high_ref, less_ref, rows):
            if reach == 0:
                return value
            return value - product_of_halves(
                (high_ref[rows, :reach], less_ref[rows, :reach]),
                (low_high_ref[cols, :reach], low_less_ref[cols, :reach]),
                NT,
            )

        tile = reduced(low_ref[cols, cols], low_high_ref, low_less_ref, cols)
        uppers, inverses = tile_factor(
            [tile[GROUP * g : GROUP * (g + 1)] for g in range(TILE // GROUP)]
        )
        for g, piece in enumerate(inverses):
            inv_ref[GROUP * g : GROUP * (g + 1), :] = piece
        inverse = halves(inv_ref[...])
        for i in range(depth // side):
            rows = slice(i * side, (i + 1) * side)
            value = reduced(x_ref[rows, cols], y_high_ref, y_less_ref, rows)
            value = product_of_halves(halves(value), inverse, NT)
            for out_ref, (head, tail) in zip(outs, PIECES):
                if head <= i < tail:
                    out_ref[(i - head) * side : (i - head + 1) * side, local] = value
            high, less = halves(value)
            y_high_ref[rows, cols] = high
            y_less_ref[rows, cols] = less
        for i in range(first * TILE // WIDE, width // WIDE):
            rows = slice(i * WIDE, (i + 1) * WIDE)
            value = reduced(low_ref[rows, cols], low_high_ref, low_less_ref, rows)
            value = product_of_halves(halves(value), inverse, NT)
            place = lax.broadcasted_iota(jnp.int32, (WIDE, TILE), 0) + i * WIDE
            value = jnp.where(place >= start + TILE, value, 0.0)
            low_ref[rows, cols] = value
            high, less = halves(value)
            low_high_ref[rows, cols] = high
            low_less_ref[rows, cols] = less
        upper = jnp.concatenate(uppers, axis=0)
        low_ref[cols, cols] = jnp.where(col <= row, upper.T, 0.0)
        return carry

    lax.fori_loop(first, last, step, 0)
    if number > 0:
        for i in range(first * TILE // WIDE):
            rows = slice(i * WIDE, (i + 1) * WIDE)
            low_ref[rows, begin:end] = jnp.zeros((WIDE, end - begin), jnp.float32)
    if final:
        for gram_ref, left, right in (
            (gram_refs[0], slice(2 * side, 3 * side), slice(0, 2 * side)),
            (gram_refs[1], slice(side, 2 * side), slice(0, side)),
        ):
            gram_ref[...] = product_of_halves(
                (y_high_ref[left, :], y_less_ref[left, :]),
                (y_high_ref[right, :], y_less_ref[right, :]),
                NT,
            )


def factored_part(x, start, before, side, bounds, number):
    depth, width = x.shape
    first, last = bounds[number], bounds[number + 1]
    final = number == len(bounds) - 2
    end = last * TILE
    shapes = [jax.ShapeDtypeStruct((width, width), jnp.float32)]
    shapes += piece_shapes(side, (last - first) * TILE)
    if final:
        shapes += [
            jax.ShapeDtypeStruct((side, 2 * side), jnp.float32),
            jax.ShapeDtypeStruct((side, side), jnp.float32),
        ]
    scratch = [pltpu.VMEM((TILE, TILE), jnp.float32)]
    scratch += [pltpu.VMEM((width, end), jnp.bfloat16)] * 2
    scratch += [pltpu.VMEM((depth, end), jnp.bfloat16)] * 2
    if number == 0:
        scratch += [pltpu.VMEM((width, depth), jnp.bfloat16)] * 2
    return pl.pallas_call(
        functools.partial(part_kernel, side, bounds, number),
        out_shape=tuple(shapes),
        in_specs=[VMEM_SPEC] * (2 + len(before)),
        out_specs=(VMEM_SPEC,) * len(shapes),
        scratch_shapes=scratch,
        compiler_params=pltpu.CompilerParams(vmem_limit_bytes=24 << 20),
        cost_estimate=pl.CostEstimate(
            flops=20_000_000_000, bytes_accessed=3 * depth * width * 4, transcendentals=0
        ),
        name="factor_part",
    )(x, start, *before)


def near_product(left, right, dims):
    return product_of_halves(halves(left), halves(right), dims)


def put_coupling(side, start, y_refs, x_ref, buffer_ref, left_refs, out_ref, sems):
    rows = buffer_ref.shape[1]
    width = x_ref.shape[1]
    copies = []
    for place, (number, begin, end) in enumerate(((3, 0, 1), (1, 0, 2), (0, 1, 3), (2, 2, 3))):
        keep_halves(left_refs, y_refs[number][...].T)

        def put(lanes, value, place=place):
            buffer_ref[place, :, lanes] = value

        tall_product(
            left_refs,
            rows,
            (end - begin) * side,
            lambda lanes, begin=begin, end=end: x_ref[begin * side : end * side, lanes],
            put,
            width,
        )
        copy = pltpu.make_async_copy(
            buffer_ref.at[place], out_ref.at[place, pl.ds(start, rows), :], sems.at[place]
        )
        copy.start()
        copies.append(copy)
    return copies


def early_kernel(side, starts, x_ref, *refs):
    parts = len(starts)
    y_refs, refs = refs[: 4 * parts], refs[4 * parts :]
    out_ref, refs = refs[0], refs[1:]
    buffers, (high_ref, less_ref, sems) = refs[:parts], refs[parts:]
    copies = []
    for number, start in enumerate(starts):
        copies += put_coupling(
            side,
            start,
            y_refs[4 * number : 4 * number + 4],
            x_ref,
            buffers[number],
            (high_ref, less_ref),
            out_ref,
            sems.at[number],
        )
    for copy in copies:
        copy.wait()


def early(x, parts, starts, side):
    width = x.shape[1]
    heights = [part[0].shape[1] for part in parts]
    most = max(heights)
    return pl.pallas_call(
        functools.partial(early_kernel, side, starts),
        out_shape=jax.ShapeDtypeStruct((4, width, width), jnp.float32),
        in_specs=[VMEM_SPEC] * (1 + 4 * len(parts)),
        out_specs=ANY_SPEC,
        scratch_shapes=[pltpu.VMEM((4, height, width), jnp.float32) for height in heights]
        + [
            pltpu.VMEM((most, 2 * side), jnp.bfloat16),
            pltpu.VMEM((most, 2 * side), jnp.bfloat16),
            pltpu.SemaphoreType.DMA((len(parts), 4)),
        ],
        compiler_params=pltpu.CompilerParams(vmem_limit_bytes=24 << 20),
        cost_estimate=pl.CostEstimate(
            flops=8_000_000_000, bytes_accessed=4 * width * width * 4, transcendentals=0
        ),
        name="early",
    )(x, *[piece for part in parts for piece in part])


def late_kernel(side, starts, flags_ref, *refs):
    (
        x_ref,
        shift_ref,
        direct_ref,
        onward_ref,
        second_ref,
        extra_ref,
        low_ref,
        gram_one_ref,
        gram_two_ref,
    ) = refs[:9]
    parts = len(starts)
    refs = refs[9:]
    mine, refs = refs[:parts], refs[parts:]
    pieces, refs = [refs[4 * k : 4 * k + 4] for k in range(parts)], refs[4 * parts :]
    lasts = pieces[-1]
    partial_ref, schur_ref, coupling_ref = refs[:3]
    buffer_ref, tile_ref, rest_ref, near_ref, far_ref, high_ref, less_ref, sems, outs = refs[3:]
    left_refs = (high_ref, less_ref)
    width = x_ref.shape[1]
    cut = starts[-1]
    copies = put_coupling(side, cut, lasts, x_ref, buffer_ref, left_refs, coupling_ref, sems)
    own, above, second_above, under, second_under = [flags_ref[k] > 0 for k in range(5)]
    one, two, three = slice(0, side), slice(side, 2 * side), slice(2 * side, 3 * side)
    pair, tail = slice(0, 2 * side), slice(side, 3 * side)
    rest_ref[...] = x_ref[...]
    near_ref[three, :] = jnp.zeros((side, width), jnp.float32)
    far_ref[two, :] = jnp.zeros((side, width), jnp.float32)

    @pl.when(own)
    def _():
        for start, ref in zip(starts, mine):
            lanes = slice(start, start + ref.shape[1])
            near_ref[pair, lanes] = ref[...]
            far_ref[one, lanes] = ref[side:, :]

    @pl.when(jnp.logical_not(own))
    def _():
        near_ref[pair, :] = x_ref[tail, :]
        far_ref[one, :] = x_ref[three, :]

    def weighed(number, rows):
        gram = 0.0
        for part in pieces:
            both = halves(part[number][...])
            gram = gram + product_of_halves(both, both, NT)
        return near_product(gram, x_ref[rows, :], NN)

    @pl.when(second_above)
    def _():
        rest_ref[one, :] = rest_ref[one, :] - weighed(3, one)

    @pl.when(above)
    def _():
        term = weighed(1, pair)
        rest_ref[pair, :] = rest_ref[pair, :] - term
        near_ref[one, :] = near_ref[one, :] - term[side:]

    @pl.when(under)
    def _():
        term = weighed(0, tail)
        rest_ref[tail, :] = rest_ref[tail, :] - term
        far_ref[one, :] = far_ref[one, :] - term[side:]
        far_ref[two, :] = -near_product(gram_one_ref[...], x_ref[tail, :], NN)

    @pl.when(second_under)
    def _():
        term = weighed(2, three)
        rest_ref[three, :] = rest_ref[three, :] - term
        near_ref[two, :] = near_ref[two, :] - term
        near_ref[three, :] = -near_product(gram_two_ref[...], x_ref[three, :], NN)

    def put(place):
        copy = pltpu.make_async_copy(tile_ref.at[place], schur_ref.at[place], outs.at[place])
        copy.start()
        return copy

    def fill(place, left, right_ref):
        keep_halves(left_refs, left.T)

        def put(lanes, value):
            tile_ref[place, :, lanes] = value

        tall_product(
            left_refs, width, left.shape[0], lambda lanes: right_ref[:, lanes], put, width
        )

    def from_coupling(place, member):
        copy = pltpu.make_async_copy(
            partial_ref.at[member, pl.ds(0, cut), :],
            tile_ref.at[place, pl.ds(0, cut), :],
            outs.at[place],
        )
        copy.start()
        tile_ref[place, cut:, :] = buffer_ref[member]
        copy.wait()

    @pl.when(own)
    def _():
        tile_ref[2] = low_ref[...]

    @pl.when(jnp.logical_not(own))
    def _():
        fill(2, x_ref[...], rest_ref)
        for i in range(width // TILE):
            rows = slice(i * TILE, (i + 1) * TILE)
            row = lax.broadcasted_iota(jnp.int32, (TILE, TILE), 0)
            col = lax.broadcasted_iota(jnp.int32, (TILE, TILE), 1)
            tile_ref[2, rows, rows] = tile_ref[2, rows, rows] + jnp.where(
                row == col, jnp.broadcast_to(shift_ref[:, rows], (TILE, TILE)), 0.0
            )

    copies.append(put(2))

    @pl.when(under)
    def _():
        from_coupling(1, 2)

    @pl.when(jnp.logical_not(under))
    def _():
        below = direct_ref[...] + onward_ref[...]
        fill(1, jnp.concatenate([below, extra_ref[...]], axis=0), near_ref)

    copies.append(put(1))

    @pl.when(second_under)
    def _():
        from_coupling(0, 3)

    @pl.when(jnp.logical_not(second_under))
    def _():
        fill(0, second_ref[...], far_ref)

    copies.append(put(0))
    for copy in copies:
        copy.wait()


def late(flags, x, shift, received, low, grams, mine, parts, partial, starts, side):
    depth, width = x.shape
    rest = parts[-1][0].shape[1]
    inputs = [x, shift, *received, low, *grams, *mine] + [piece for part in parts for piece in part]
    return pl.pallas_call(
        functools.partial(late_kernel, side, starts),
        out_shape=(
            jax.ShapeDtypeStruct((3, width, width), jnp.float32),
            jax.ShapeDtypeStruct((4, width, width), jnp.float32),
        ),
        in_specs=[SMEM_SPEC] + [VMEM_SPEC] * len(inputs) + [ANY_SPEC],
        out_specs=(ANY_SPEC, ANY_SPEC),
        input_output_aliases={1 + len(inputs): 1},
        scratch_shapes=[
            pltpu.VMEM((4, rest, width), jnp.float32),
            pltpu.VMEM((3, width, width), jnp.float32),
            pltpu.VMEM((depth, width), jnp.float32),
            pltpu.VMEM((depth, width), jnp.float32),
            pltpu.VMEM((2 * side, width), jnp.float32),
            pltpu.VMEM((width, depth), jnp.bfloat16),
            pltpu.VMEM((width, depth), jnp.bfloat16),
            pltpu.SemaphoreType.DMA((4,)),
            pltpu.SemaphoreType.DMA((3,)),
        ],
        compiler_params=pltpu.CompilerParams(vmem_limit_bytes=40 << 20),
        cost_estimate=pl.CostEstimate(
            flops=12_000_000_000, bytes_accessed=7 * width * width * 4, transcendentals=0
        ),
        name="late",
    )(flags, *inputs, partial)


def local(weighted_jacobian_strips, leading_pose_index, levenberg_shift, removal_flags):
    count = lax.axis_size(AXES)
    own = lax.axis_index(AXES)
    surfels, _, width = weighted_jacobian_strips.shape
    capacity = max(2, (3 * surfels + 2 * count - 1) // (2 * count))
    side = count * capacity
    tiles = width // TILE
    bounds = tuple(tiles * k // PARTS for k in range(PARTS + 1))
    starts = tuple(bound * TILE for bound in bounds[:-1])
    flags = removal_flags[(own + jnp.array((0, 1, 2, -1, -2), jnp.int32)) % count]

    chunks = bucketed(
        leading_pose_index.reshape(1, surfels),
        weighted_jacobian_strips.transpose(1, 0, 2),
        count,
        capacity,
    )
    chunks = lax.all_to_all(chunks, AXES, split_axis=0, concat_axis=0, tiled=True)
    x, two, last = regrouped(chunks, capacity, width)

    def sent_parts(parts):
        return [passed_along(part, steps) for part, steps in zip(parts, (1, -1, 2, -2))]

    direct = lax.ppermute(two, AXES, [(k, k + 1) for k in range(0, count, 2)])
    second = passed_along(two, 2)

    def solved(number, start, known):
        before = [part[k] for part in known for k in (0, 3)]
        return factored_part(x, start, before, side, bounds, number)

    low, *part = solved(0, levenberg_shift, ())
    known = [part]
    parts = [sent_parts(part)]
    for number in range(1, PARTS - 1):
        low, *part = solved(number, low, known)
        known.append(part)
        parts.append(sent_parts(part))
    onward = lax.ppermute(second, AXES, [(k + 1, k) for k in range(0, count, 2)])
    extra = passed_along(last, 1)
    low, *part, gram_one, gram_two = solved(PARTS - 1, low, known)
    known.append(part)
    parts.append(sent_parts(part))
    grams = (passed_along(gram_one, 1), passed_along(gram_two, 2))
    partial = early(x, parts[:-1], starts[:-1], side)
    schur, coupling = late(
        flags,
        x,
        levenberg_shift,
        (direct, onward, second, extra),
        low,
        grams,
        [part[1] for part in known],
        parts,
        partial,
        starts,
        side,
    )
    return schur[None], coupling[None]


def solution(mesh):
    in_specs = (P(AXES, None, None), P(AXES, None), P(AXES, None), P())
    out_specs = (P(AXES, None, None, None), P(AXES, None, None, None))

    return jax.shard_map(local, mesh=mesh, in_specs=in_specs, out_specs=out_specs, check_vma=False)
```

```python
import functools
import math

import jax
import jax.numpy as jnp
from jax import lax
from jax.experimental import pallas as pl
from jax.experimental.pallas import tpu as pltpu
from jax.sharding import PartitionSpec as P


AXES = ("gx", "gy")
TILE = 128
GROUP = 8
WIDE = 256
PARTS = 3
NT = (((1,), (1,)), ((), ()))
TN = (((0,), (0,)), ((), ()))
NN = (((1,), (0,)), ((), ()))
VMEM_SPEC = pl.BlockSpec(memory_space=pltpu.VMEM)
SMEM_SPEC = pl.BlockSpec(memory_space=pltpu.SMEM)
ANY_SPEC = pl.BlockSpec(memory_space=pl.ANY)
PIECES = ((0, 2), (1, 3), (0, 1), (2, 3))


def passed_along(value, steps):
    count = lax.axis_size(AXES)
    pairs = [(source, (source + steps) % count) for source in range(count)]
    return lax.ppermute(value, AXES, pairs)


def product(left, right, dims, precision=lax.Precision.HIGHEST):
    return lax.dot_general(
        left, right, dims, precision=precision, preferred_element_type=jnp.float32
    )


def bucket_kernel(count, capacity, index_ref, strips_ref, out_ref, rows_ref):
    surfels = strips_ref.shape[1]
    width = strips_ref.shape[2]
    lane_tiles = width // WIDE
    index = index_ref[...]
    base = lax.broadcasted_iota(jnp.int32, (count, surfels), 0)
    hot = (base == index).astype(jnp.float32)
    first = lax.broadcasted_iota(jnp.int32, (surfels, surfels), 0)
    second = lax.broadcasted_iota(jnp.int32, (surfels, surfels), 1)
    ahead = (first < second).astype(jnp.float32)
    earlier = product(hot, ahead, NN)
    within = jnp.sum(earlier * hot, axis=0, keepdims=True).astype(jnp.int32)
    period = GROUP // math.gcd(capacity, GROUP)
    for piece in range(3):
        moved = index + piece
        moved = jnp.where(moved >= count, moved - count, moved)
        slot = moved * capacity + within
        row = lax.broadcasted_iota(jnp.int32, (count * capacity, surfels), 0)
        pick = (row == slot).astype(jnp.bfloat16)
        values = strips_ref[piece]
        high = values.astype(jnp.bfloat16)
        rest = values - high.astype(jnp.float32)
        middle = rest.astype(jnp.bfloat16)
        low = (rest - middle.astype(jnp.float32)).astype(jnp.bfloat16)
        rows_ref[...] = product(
            jnp.concatenate([pick, pick, pick], axis=1),
            jnp.concatenate([high, middle, low], axis=0),
            NN,
            lax.Precision.DEFAULT,
        )

        def spread(turn, carry, piece=piece):
            start = pl.multiple_of(turn * (period * capacity), GROUP)
            for tile in range(lane_tiles):
                block = rows_ref[pl.ds(start, period * capacity), WIDE * tile : WIDE * (tile + 1)]
                for member in range(period):
                    begin = (piece * lane_tiles + tile) * capacity
                    out_ref[turn * period + member, begin : begin + capacity, :] = block[
                        member * capacity : (member + 1) * capacity
                    ]
            return carry

        lax.fori_loop(0, count // period, spread, 0)


def bucketed(index_row, strips, count, capacity):
    width = strips.shape[2]
    return pl.pallas_call(
        functools.partial(bucket_kernel, count, capacity),
        out_shape=jax.ShapeDtypeStruct(
            (count, 3 * (width // WIDE) * capacity, WIDE), jnp.float32
        ),
        in_specs=[VMEM_SPEC, VMEM_SPEC],
        out_specs=VMEM_SPEC,
        scratch_shapes=[pltpu.VMEM((count * capacity, width), jnp.float32)],
        name="bucket",
    )(index_row, strips)


def regroup_kernel(capacity, in_ref, out_ref, two_ref, one_ref):
    count = in_ref.shape[0]
    width = out_ref.shape[1]
    lane_tiles = width // WIDE
    period = GROUP // math.gcd(capacity, GROUP)

    def gather(turn, carry):
        for piece in range(3):
            for tile in range(lane_tiles):
                begin = (piece * lane_tiles + tile) * capacity
                block = jnp.concatenate(
                    [
                        in_ref[turn * period + member, begin : begin + capacity, :]
                        for member in range(period)
                    ],
                    axis=0,
                )
                start = pl.multiple_of(
                    piece * count * capacity + turn * (period * capacity), GROUP
                )
                out_ref[
                    pl.ds(start, period * capacity), WIDE * tile : WIDE * (tile + 1)
                ] = block
        return carry

    lax.fori_loop(0, count // period, gather, 0)
    side = count * capacity
    two_ref[...] = out_ref[: 2 * side, :]
    one_ref[...] = out_ref[2 * side :, :]


def regrouped(chunks, capacity, width):
    side = chunks.shape[0] * capacity
    return pl.pallas_call(
        functools.partial(regroup_kernel, capacity),
        out_shape=tuple(
            jax.ShapeDtypeStruct((parts * side, width), jnp.float32) for parts in (3, 2, 1)
        ),
        in_specs=[VMEM_SPEC],
        out_specs=(VMEM_SPEC,) * 3,
        compiler_params=pltpu.CompilerParams(vmem_limit_bytes=16 << 20),
        name="regroup",
    )(chunks)


def full(value):
    return jnp.broadcast_to(value, (GROUP, TILE))


def half_factor(pair_ref, done_ref, start):
    groups = pair_ref.shape[0] // GROUP
    sub = lax.broadcasted_iota(jnp.int32, (GROUP, TILE), 0)
    rows = [pair_ref[GROUP * g : GROUP * (g + 1), :] for g in range(groups)]
    eight = range(GROUP)
    for p in range(groups):
        strip = rows[p]
        cols = [full(strip[:, GROUP * p + k : GROUP * p + k + 1]) for k in eight]
        m = [[full(cols[k][i : i + 1, :]) if k <= i else None for k in eight] for i in eight]
        r = [None] * GROUP
        u = [full(strip[j : j + 1, :]) for j in eight]
        for j in eight:
            r[j] = lax.rsqrt(m[j][j])
            for i in range(j + 1, GROUP):
                m[i][j] = m[i][j] * r[j]
            for k in range(j + 1, GROUP):
                for i in range(k, GROUP):
                    m[i][k] = m[i][k] - m[i][j] * m[k][j]
            u[j] = u[j] * r[j]
            for i in range(j + 1, GROUP):
                u[i] = u[i] - m[i][j] * u[j]
        joined = u[0]
        for j in range(1, GROUP):
            joined = jnp.where(sub == j, u[j], joined)
        done_ref[pl.ds(start + GROUP * p, GROUP), :] = joined
        for g in range(p + 1, groups):
            side = [full(rows[g][:, GROUP * p + k : GROUP * p + k + 1]) for k in eight]
            x = rows[g]
            for j in eight:
                side[j] = side[j] * r[j]
                for i in range(j + 1, GROUP):
                    side[i] = side[i] - m[i][j] * side[j]
                x = x - side[j] * u[j]
            rows[g] = x


def tile_factor(tile, pair_ref, done_ref, cross_ref, corner_ref):
    half = TILE // 2
    row = lax.broadcasted_iota(jnp.int32, (half, half), 0)
    col = lax.broadcasted_iota(jnp.int32, (half, half), 1)
    unit = jnp.where(row == col, 1.0, 0.0).astype(jnp.float32)
    zero = jnp.zeros((half, half), jnp.float32)
    pair_ref[...] = jnp.concatenate([tile[:half, :half], unit], axis=1)
    cross_ref[...] = tile[:half, half:]
    corner_ref[...] = tile[half:, half:]

    def turn(number, carry):
        half_factor(pair_ref, done_ref, pl.multiple_of(number * half, half))

        @pl.when(number == 0)
        def _():
            cross = near_product(done_ref[:half, half:], cross_ref[...], NN)
            cross_ref[...] = cross
            both = halves(cross)
            rest = corner_ref[...] - product_of_halves(both, both, TN)
            pair_ref[...] = jnp.concatenate([rest, unit], axis=1)

        return carry

    lax.fori_loop(0, 2, turn, 0)
    first, second = done_ref[:half, half:], done_ref[half:, half:]
    middle = near_product(cross_ref[...], first, TN)
    upper = jnp.concatenate(
        [
            jnp.concatenate([done_ref[:half, :half], cross_ref[...]], axis=1),
            jnp.concatenate([zero, done_ref[half:, :half]], axis=1),
        ],
        axis=0,
    )
    inverse = jnp.concatenate(
        [
            jnp.concatenate([first, zero], axis=1),
            jnp.concatenate([-near_product(second, middle, NN), second], axis=1),
        ],
        axis=0,
    )
    return upper, inverse


def halves(value):
    high = value.astype(jnp.bfloat16)
    return high, (value - high.astype(jnp.float32)).astype(jnp.bfloat16)


def product_of_halves(left, right, dims):
    total = product(left[0], right[0], dims, lax.Precision.DEFAULT)
    total = total + product(left[0], right[1], dims, lax.Precision.DEFAULT)
    return total + product(left[1], right[0], dims, lax.Precision.DEFAULT)


def lanes_at(number):
    return pl.ds(pl.multiple_of(number * WIDE, WIDE), WIDE)


def tall_product(left_refs, rows, depth, right_at, put, width):
    left = tuple(ref[:rows, :depth] for ref in left_refs)

    def block(number, carry):
        put(lanes_at(number), product_of_halves(left, halves(right_at(lanes_at(number))), NN))
        return carry

    lax.fori_loop(0, width // WIDE, block, 0)


def keep_halves(left_refs, value):
    rows, depth = value.shape
    high, low = halves(value)
    left_refs[0][:rows, :depth] = high
    left_refs[1][:rows, :depth] = low


def piece_shapes(side, lanes):
    return tuple(
        jax.ShapeDtypeStruct(((stop - start) * side, lanes), jnp.float32) for start, stop in PIECES
    )


def part_kernel(side, bounds, number, *refs):
    first, last = bounds[number], bounds[number + 1]
    final = number == len(bounds) - 2
    x_ref, start_ref = refs[:2]
    before = refs[2 : 2 + 2 * number]
    refs = refs[2 + 2 * number :]
    low_ref, outs = refs[0], refs[1:5]
    gram_refs, refs = (refs[5:7], refs[7:]) if final else ((), refs[5:])
    small_refs, refs = refs[:4], refs[4:]
    low_high_ref, low_less_ref, y_high_ref, y_less_ref = refs[:4]
    depth, width = x_ref.shape
    begin, end = first * TILE, last * TILE
    reach = end - TILE
    row = lax.broadcasted_iota(jnp.int32, (TILE, TILE), 0)
    col = lax.broadcasted_iota(jnp.int32, (TILE, TILE), 1)

    if number == 0:
        turned = refs[4:6]
        keep_halves(turned, x_ref[...].T)

        def gram(lanes, value):
            low_ref[:, lanes] = value

        tall_product(turned, width, depth, lambda lanes: x_ref[:, lanes], gram, width)
        for i in range(width // TILE):
            rows = slice(i * TILE, (i + 1) * TILE)
            low_ref[rows, rows] = low_ref[rows, rows] + jnp.where(
                row == col, jnp.broadcast_to(start_ref[:, rows], (TILE, TILE)), 0.0
            )
    else:
        low_ref[...] = start_ref[...]
        high, less = halves(start_ref[:, :begin])
        low_high_ref[:, :begin] = high
        low_less_ref[:, :begin] = less
        for k in range(number):
            lanes = slice(bounds[k] * TILE, bounds[k + 1] * TILE)
            for ref, rows in ((before[2 * k], slice(0, 2 * side)), (before[2 * k + 1], slice(2 * side, 3 * side))):
                high, less = halves(ref[...])
                y_high_ref[rows, lanes] = high
                y_less_ref[rows, lanes] = less
    for ref in (low_high_ref, low_less_ref):
        ref[:, begin:] = jnp.zeros((width, end - begin), jnp.bfloat16)
    for ref in (y_high_ref, y_less_ref):
        ref[:, begin:] = jnp.zeros((depth, end - begin), jnp.bfloat16)

    def step(j, carry):
        start = pl.multiple_of(j * TILE, TILE)
        cols = pl.ds(start, TILE)
        local = pl.ds(pl.multiple_of((j - first) * TILE, TILE), TILE)

        def reduced(value, high_ref, less_ref, rows):
            if reach == 0:
                return value
            return value - product_of_halves(
                (high_ref[rows, :reach], less_ref[rows, :reach]),
                (low_high_ref[cols, :reach], low_less_ref[cols, :reach]),
                NT,
            )

        tile = reduced(low_ref[cols, cols], low_high_ref, low_less_ref, cols)
        upper, inverse = tile_factor(tile, *small_refs)
        inverse = halves(inverse)
        for i in range(depth // side):
            rows = slice(i * side, (i + 1) * side)
            value = reduced(x_ref[rows, cols], y_high_ref, y_less_ref, rows)
            value = product_of_halves(halves(value), inverse, NT)
            for out_ref, (head, tail) in zip(outs, PIECES):
                if head <= i < tail:
                    out_ref[(i - head) * side : (i - head + 1) * side, local] = value
            high, less = halves(value)
            y_high_ref[rows, cols] = high
            y_less_ref[rows, cols] = less
        for i in range(first * TILE // WIDE, width // WIDE):
            rows = slice(i * WIDE, (i + 1) * WIDE)
            value = reduced(low_ref[rows, cols], low_high_ref, low_less_ref, rows)
            value = product_of_halves(halves(value), inverse, NT)
            place = lax.broadcasted_iota(jnp.int32, (WIDE, TILE), 0) + i * WIDE
            value = jnp.where(place >= start + TILE, value, 0.0)
            low_ref[rows, cols] = value
            high, less = halves(value)
            low_high_ref[rows, cols] = high
            low_less_ref[rows, cols] = less
        low_ref[cols, cols] = jnp.where(col <= row, upper.T, 0.0)
        return carry

    lax.fori_loop(first, last, step, 0)
    if number > 0:
        for i in range(first * TILE // WIDE):
            rows = slice(i * WIDE, (i + 1) * WIDE)
            low_ref[rows, begin:end] = jnp.zeros((WIDE, end - begin), jnp.float32)
    if final:
        for gram_ref, left, right in (
            (gram_refs[0], slice(2 * side, 3 * side), slice(0, 2 * side)),
            (gram_refs[1], slice(side, 2 * side), slice(0, side)),
        ):
            gram_ref[...] = product_of_halves(
                (y_high_ref[left, :], y_less_ref[left, :]),
                (y_high_ref[right, :], y_less_ref[right, :]),
                NT,
            )


def factored_part(x, start, before, side, bounds, number):
    depth, width = x.shape
    first, last = bounds[number], bounds[number + 1]
    final = number == len(bounds) - 2
    end = last * TILE
    shapes = [jax.ShapeDtypeStruct((width, width), jnp.float32)]
    shapes += piece_shapes(side, (last - first) * TILE)
    if final:
        shapes += [
            jax.ShapeDtypeStruct((side, 2 * side), jnp.float32),
            jax.ShapeDtypeStruct((side, side), jnp.float32),
        ]
    half = TILE // 2
    scratch = [pltpu.VMEM((half, TILE), jnp.float32), pltpu.VMEM((TILE, TILE), jnp.float32)]
    scratch += [pltpu.VMEM((half, half), jnp.float32)] * 2
    scratch += [pltpu.VMEM((width, end), jnp.bfloat16)] * 2
    scratch += [pltpu.VMEM((depth, end), jnp.bfloat16)] * 2
    if number == 0:
        scratch += [pltpu.VMEM((width, depth), jnp.bfloat16)] * 2
    return pl.pallas_call(
        functools.partial(part_kernel, side, bounds, number),
        out_shape=tuple(shapes),
        in_specs=[VMEM_SPEC] * (2 + len(before)),
        out_specs=(VMEM_SPEC,) * len(shapes),
        scratch_shapes=scratch,
        compiler_params=pltpu.CompilerParams(vmem_limit_bytes=24 << 20),
        cost_estimate=pl.CostEstimate(
            flops=20_000_000_000, bytes_accessed=3 * depth * width * 4, transcendentals=0
        ),
        name="factor_part",
    )(x, start, *before)


def near_product(left, right, dims):
    return product_of_halves(halves(left), halves(right), dims)


def put_coupling(side, start, y_refs, x_ref, buffer_ref, left_refs, out_ref, sems):
    rows = buffer_ref.shape[1]
    width = x_ref.shape[1]
    copies = []
    for place, (number, begin, end) in enumerate(((3, 0, 1), (1, 0, 2), (0, 1, 3), (2, 2, 3))):
        keep_halves(left_refs, y_refs[number][...].T)

        def put(lanes, value, place=place):
            buffer_ref[place, :, lanes] = value

        tall_product(
            left_refs,
            rows,
            (end - begin) * side,
            lambda lanes, begin=begin, end=end: x_ref[begin * side : end * side, lanes],
            put,
            width,
        )
        copy = pltpu.make_async_copy(
            buffer_ref.at[place], out_ref.at[place, pl.ds(start, rows), :], sems.at[place]
        )
        copy.start()
        copies.append(copy)
    return copies


def early_kernel(side, starts, x_ref, *refs):
    parts = len(starts)
    y_refs, refs = refs[: 4 * parts], refs[4 * parts :]
    out_ref, refs = refs[0], refs[1:]
    buffers, (high_ref, less_ref, sems) = refs[:parts], refs[parts:]
    copies = []
    for number, start in enumerate(starts):
        copies += put_coupling(
            side,
            start,
            y_refs[4 * number : 4 * number + 4],
            x_ref,
            buffers[number],
            (high_ref, less_ref),
            out_ref,
            sems.at[number],
        )
    for copy in copies:
        copy.wait()


def early(x, parts, starts, side):
    width = x.shape[1]
    heights = [part[0].shape[1] for part in parts]
    most = max(heights)
    return pl.pallas_call(
        functools.partial(early_kernel, side, starts),
        out_shape=jax.ShapeDtypeStruct((4, width, width), jnp.float32),
        in_specs=[VMEM_SPEC] * (1 + 4 * len(parts)),
        out_specs=ANY_SPEC,
        scratch_shapes=[pltpu.VMEM((4, height, width), jnp.float32) for height in heights]
        + [
            pltpu.VMEM((most, 2 * side), jnp.bfloat16),
            pltpu.VMEM((most, 2 * side), jnp.bfloat16),
            pltpu.SemaphoreType.DMA((len(parts), 4)),
        ],
        compiler_params=pltpu.CompilerParams(vmem_limit_bytes=24 << 20),
        cost_estimate=pl.CostEstimate(
            flops=8_000_000_000, bytes_accessed=4 * width * width * 4, transcendentals=0
        ),
        name="early",
    )(x, *[piece for part in parts for piece in part])


def late_kernel(side, starts, flags_ref, *refs):
    (
        x_ref,
        shift_ref,
        direct_ref,
        onward_ref,
        second_ref,
        extra_ref,
        low_ref,
        gram_one_ref,
        gram_two_ref,
    ) = refs[:9]
    parts = len(starts)
    refs = refs[9:]
    mine, refs = refs[:parts], refs[parts:]
    pieces, refs = [refs[4 * k : 4 * k + 4] for k in range(parts)], refs[4 * parts :]
    lasts = pieces[-1]
    partial_ref, schur_ref, coupling_ref = refs[:3]
    buffer_ref, tile_ref, rest_ref, near_ref, far_ref, high_ref, less_ref, sems, outs = refs[3:]
    left_refs = (high_ref, less_ref)
    width = x_ref.shape[1]
    cut = starts[-1]
    copies = put_coupling(side, cut, lasts, x_ref, buffer_ref, left_refs, coupling_ref, sems)
    own, above, second_above, under, second_under = [flags_ref[k] > 0 for k in range(5)]
    one, two, three = slice(0, side), slice(side, 2 * side), slice(2 * side, 3 * side)
    pair, tail = slice(0, 2 * side), slice(side, 3 * side)
    rest_ref[...] = x_ref[...]
    near_ref[three, :] = jnp.zeros((side, width), jnp.float32)
    far_ref[two, :] = jnp.zeros((side, width), jnp.float32)

    @pl.when(own)
    def _():
        for start, ref in zip(starts, mine):
            lanes = slice(start, start + ref.shape[1])
            near_ref[pair, lanes] = ref[...]
            far_ref[one, lanes] = ref[side:, :]

    @pl.when(jnp.logical_not(own))
    def _():
        near_ref[pair, :] = x_ref[tail, :]
        far_ref[one, :] = x_ref[three, :]

    def weighed(number, rows):
        gram = 0.0
        for part in pieces:
            both = halves(part[number][...])
            gram = gram + product_of_halves(both, both, NT)
        return near_product(gram, x_ref[rows, :], NN)

    @pl.when(second_above)
    def _():
        rest_ref[one, :] = rest_ref[one, :] - weighed(3, one)

    @pl.when(above)
    def _():
        term = weighed(1, pair)
        rest_ref[pair, :] = rest_ref[pair, :] - term
        near_ref[one, :] = near_ref[one, :] - term[side:]

    @pl.when(under)
    def _():
        term = weighed(0, tail)
        rest_ref[tail, :] = rest_ref[tail, :] - term
        far_ref[one, :] = far_ref[one, :] - term[side:]
        far_ref[two, :] = -near_product(gram_one_ref[...], x_ref[tail, :], NN)

    @pl.when(second_under)
    def _():
        term = weighed(2, three)
        rest_ref[three, :] = rest_ref[three, :] - term
        near_ref[two, :] = near_ref[two, :] - term
        near_ref[three, :] = -near_product(gram_two_ref[...], x_ref[three, :], NN)

    def put(place):
        copy = pltpu.make_async_copy(tile_ref.at[place], schur_ref.at[place], outs.at[place])
        copy.start()
        return copy

    def fill(place, left, right_ref):
        keep_halves(left_refs, left.T)

        def put(lanes, value):
            tile_ref[place, :, lanes] = value

        tall_product(
            left_refs, width, left.shape[0], lambda lanes: right_ref[:, lanes], put, width
        )

    def from_coupling(place, member):
        copy = pltpu.make_async_copy(
            partial_ref.at[member, pl.ds(0, cut), :],
            tile_ref.at[place, pl.ds(0, cut), :],
            outs.at[place],
        )
        copy.start()
        tile_ref[place, cut:, :] = buffer_ref[member]
        copy.wait()

    @pl.when(own)
    def _():
        tile_ref[2] = low_ref[...]

    @pl.when(jnp.logical_not(own))
    def _():
        fill(2, x_ref[...], rest_ref)
        for i in range(width // TILE):
            rows = slice(i * TILE, (i + 1) * TILE)
            row = lax.broadcasted_iota(jnp.int32, (TILE, TILE), 0)
            col = lax.broadcasted_iota(jnp.int32, (TILE, TILE), 1)
            tile_ref[2, rows, rows] = tile_ref[2, rows, rows] + jnp.where(
                row == col, jnp.broadcast_to(shift_ref[:, rows], (TILE, TILE)), 0.0
            )

    copies.append(put(2))

    @pl.when(under)
    def _():
        from_coupling(1, 2)

    @pl.when(jnp.logical_not(under))
    def _():
        below = direct_ref[...] + onward_ref[...]
        fill(1, jnp.concatenate([below, extra_ref[...]], axis=0), near_ref)

    copies.append(put(1))

    @pl.when(second_under)
    def _():
        from_coupling(0, 3)

    @pl.when(jnp.logical_not(second_under))
    def _():
        fill(0, second_ref[...], far_ref)

    copies.append(put(0))
    for copy in copies:
        copy.wait()


def late(flags, x, shift, received, low, grams, mine, parts, partial, starts, side):
    depth, width = x.shape
    rest = parts[-1][0].shape[1]
    inputs = [x, shift, *received, low, *grams, *mine] + [piece for part in parts for piece in part]
    return pl.pallas_call(
        functools.partial(late_kernel, side, starts),
        out_shape=(
            jax.ShapeDtypeStruct((3, width, width), jnp.float32),
            jax.ShapeDtypeStruct((4, width, width), jnp.float32),
        ),
        in_specs=[SMEM_SPEC] + [VMEM_SPEC] * len(inputs) + [ANY_SPEC],
        out_specs=(ANY_SPEC, ANY_SPEC),
        input_output_aliases={1 + len(inputs): 1},
        scratch_shapes=[
            pltpu.VMEM((4, rest, width), jnp.float32),
            pltpu.VMEM((3, width, width), jnp.float32),
            pltpu.VMEM((depth, width), jnp.float32),
            pltpu.VMEM((depth, width), jnp.float32),
            pltpu.VMEM((2 * side, width), jnp.float32),
            pltpu.VMEM((width, depth), jnp.bfloat16),
            pltpu.VMEM((width, depth), jnp.bfloat16),
            pltpu.SemaphoreType.DMA((4,)),
            pltpu.SemaphoreType.DMA((3,)),
        ],
        compiler_params=pltpu.CompilerParams(vmem_limit_bytes=40 << 20),
        cost_estimate=pl.CostEstimate(
            flops=12_000_000_000, bytes_accessed=7 * width * width * 4, transcendentals=0
        ),
        name="late",
    )(flags, *inputs, partial)


def local(weighted_jacobian_strips, leading_pose_index, levenberg_shift, removal_flags):
    count = lax.axis_size(AXES)
    own = lax.axis_index(AXES)
    surfels, _, width = weighted_jacobian_strips.shape
    capacity = max(2, (3 * surfels + 2 * count - 1) // (2 * count))
    side = count * capacity
    tiles = width // TILE
    bounds = tuple(tiles * k // PARTS for k in range(PARTS + 1))
    starts = tuple(bound * TILE for bound in bounds[:-1])
    flags = removal_flags[(own + jnp.array((0, 1, 2, -1, -2), jnp.int32)) % count]

    chunks = bucketed(
        leading_pose_index.reshape(1, surfels),
        weighted_jacobian_strips.transpose(1, 0, 2),
        count,
        capacity,
    )
    chunks = lax.all_to_all(chunks, AXES, split_axis=0, concat_axis=0, tiled=True)
    x, two, last = regrouped(chunks, capacity, width)

    def sent_parts(parts):
        return [passed_along(part, steps) for part, steps in zip(parts, (1, -1, 2, -2))]

    direct = lax.ppermute(two, AXES, [(k, k + 1) for k in range(0, count, 2)])
    second = passed_along(two, 2)

    def solved(number, start, known):
        before = [part[k] for part in known for k in (0, 3)]
        return factored_part(x, start, before, side, bounds, number)

    low, *part = solved(0, levenberg_shift, ())
    known = [part]
    parts = [sent_parts(part)]
    for number in range(1, PARTS - 1):
        low, *part = solved(number, low, known)
        known.append(part)
        parts.append(sent_parts(part))
    onward = lax.ppermute(second, AXES, [(k + 1, k) for k in range(0, count, 2)])
    extra = passed_along(last, 1)
    low, *part, gram_one, gram_two = solved(PARTS - 1, low, known)
    known.append(part)
    parts.append(sent_parts(part))
    grams = (passed_along(gram_one, 1), passed_along(gram_two, 2))
    partial = early(x, parts[:-1], starts[:-1], side)
    schur, coupling = late(
        flags,
        x,
        levenberg_shift,
        (direct, onward, second, extra),
        low,
        grams,
        [part[1] for part in known],
        parts,
        partial,
        starts,
        side,
    )
    return schur[None], coupling[None]


def solution(mesh):
    in_specs = (P(AXES, None, None), P(AXES, None), P(AXES, None), P())
    out_specs = (P(AXES, None, None, None), P(AXES, None, None, None))

    return jax.shard_map(local, mesh=mesh, in_specs=in_specs, out_specs=out_specs, check_vma=False)
```

```python
import functools
import math

import jax
import jax.numpy as jnp
from jax import lax
from jax.experimental import pallas as pl
from jax.experimental.pallas import tpu as pltpu
from jax.sharding import PartitionSpec as P


AXES = ("gx", "gy")
TILE = 128
GROUP = 8
WIDE = 256
PARTS = 4
NT = (((1,), (1,)), ((), ()))
TN = (((0,), (0,)), ((), ()))
NN = (((1,), (0,)), ((), ()))
VMEM_SPEC = pl.BlockSpec(memory_space=pltpu.VMEM)
SMEM_SPEC = pl.BlockSpec(memory_space=pltpu.SMEM)
ANY_SPEC = pl.BlockSpec(memory_space=pl.ANY)
PIECES = ((0, 2), (1, 3), (0, 1), (2, 3))


def passed_along(value, steps):
    count = lax.axis_size(AXES)
    pairs = [(source, (source + steps) % count) for source in range(count)]
    return lax.ppermute(value, AXES, pairs)


def product(left, right, dims, precision=lax.Precision.HIGHEST):
    return lax.dot_general(
        left, right, dims, precision=precision, preferred_element_type=jnp.float32
    )


def bucket_kernel(count, capacity, index_ref, strips_ref, out_ref, rows_ref):
    surfels = strips_ref.shape[1]
    width = strips_ref.shape[2]
    lane_tiles = width // WIDE
    index = index_ref[...]
    base = lax.broadcasted_iota(jnp.int32, (count, surfels), 0)
    hot = (base == index).astype(jnp.float32)
    first = lax.broadcasted_iota(jnp.int32, (surfels, surfels), 0)
    second = lax.broadcasted_iota(jnp.int32, (surfels, surfels), 1)
    ahead = (first < second).astype(jnp.float32)
    earlier = product(hot, ahead, NN)
    within = jnp.sum(earlier * hot, axis=0, keepdims=True).astype(jnp.int32)
    period = GROUP // math.gcd(capacity, GROUP)
    for piece in range(3):
        moved = index + piece
        moved = jnp.where(moved >= count, moved - count, moved)
        slot = moved * capacity + within
        row = lax.broadcasted_iota(jnp.int32, (count * capacity, surfels), 0)
        pick = (row == slot).astype(jnp.bfloat16)
        values = strips_ref[piece]
        high = values.astype(jnp.bfloat16)
        rest = values - high.astype(jnp.float32)
        middle = rest.astype(jnp.bfloat16)
        low = (rest - middle.astype(jnp.float32)).astype(jnp.bfloat16)
        rows_ref[...] = product(
            jnp.concatenate([pick, pick, pick], axis=1),
            jnp.concatenate([high, middle, low], axis=0),
            NN,
            lax.Precision.DEFAULT,
        )

        def spread(turn, carry, piece=piece):
            start = pl.multiple_of(turn * (period * capacity), GROUP)
            for tile in range(lane_tiles):
                block = rows_ref[pl.ds(start, period * capacity), WIDE * tile : WIDE * (tile + 1)]
                for member in range(period):
                    begin = (piece * lane_tiles + tile) * capacity
                    out_ref[turn * period + member, begin : begin + capacity, :] = block[
                        member * capacity : (member + 1) * capacity
                    ]
            return carry

        lax.fori_loop(0, count // period, spread, 0)


def bucketed(index_row, strips, count, capacity):
    width = strips.shape[2]
    return pl.pallas_call(
        functools.partial(bucket_kernel, count, capacity),
        out_shape=jax.ShapeDtypeStruct(
            (count, 3 * (width // WIDE) * capacity, WIDE), jnp.float32
        ),
        in_specs=[VMEM_SPEC, VMEM_SPEC],
        out_specs=VMEM_SPEC,
        scratch_shapes=[pltpu.VMEM((count * capacity, width), jnp.float32)],
        name="bucket",
    )(index_row, strips)


def regroup_kernel(capacity, in_ref, out_ref, two_ref, one_ref):
    count = in_ref.shape[0]
    width = out_ref.shape[1]
    lane_tiles = width // WIDE
    period = GROUP // math.gcd(capacity, GROUP)

    def gather(turn, carry):
        for piece in range(3):
            for tile in range(lane_tiles):
                begin = (piece * lane_tiles + tile) * capacity
                block = jnp.concatenate(
                    [
                        in_ref[turn * period + member, begin : begin + capacity, :]
                        for member in range(period)
                    ],
                    axis=0,
                )
                start = pl.multiple_of(
                    piece * count * capacity + turn * (period * capacity), GROUP
                )
                out_ref[
                    pl.ds(start, period * capacity), WIDE * tile : WIDE * (tile + 1)
                ] = block
        return carry

    lax.fori_loop(0, count // period, gather, 0)
    side = count * capacity
    two_ref[...] = out_ref[: 2 * side, :]
    one_ref[...] = out_ref[2 * side :, :]


def regrouped(chunks, capacity, width):
    side = chunks.shape[0] * capacity
    return pl.pallas_call(
        functools.partial(regroup_kernel, capacity),
        out_shape=tuple(
            jax.ShapeDtypeStruct((parts * side, width), jnp.float32) for parts in (3, 2, 1)
        ),
        in_specs=[VMEM_SPEC],
        out_specs=(VMEM_SPEC,) * 3,
        compiler_params=pltpu.CompilerParams(vmem_limit_bytes=16 << 20),
        name="regroup",
    )(chunks)


def full(value):
    return jnp.broadcast_to(value, (GROUP, TILE))


def half_factor(pair_ref, done_ref, start):
    groups = pair_ref.shape[0] // GROUP
    sub = lax.broadcasted_iota(jnp.int32, (GROUP, TILE), 0)
    rows = [pair_ref[GROUP * g : GROUP * (g + 1), :] for g in range(groups)]
    eight = range(GROUP)
    for p in range(groups):
        strip = rows[p]
        cols = [full(strip[:, GROUP * p + k : GROUP * p + k + 1]) for k in eight]
        m = [[full(cols[k][i : i + 1, :]) if k <= i else None for k in eight] for i in eight]
        r = [None] * GROUP
        u = [full(strip[j : j + 1, :]) for j in eight]
        for j in eight:
            r[j] = lax.rsqrt(m[j][j])
            for i in range(j + 1, GROUP):
                m[i][j] = m[i][j] * r[j]
            for k in range(j + 1, GROUP):
                for i in range(k, GROUP):
                    m[i][k] = m[i][k] - m[i][j] * m[k][j]
            u[j] = u[j] * r[j]
            for i in range(j + 1, GROUP):
                u[i] = u[i] - m[i][j] * u[j]
        joined = u[0]
        for j in range(1, GROUP):
            joined = jnp.where(sub == j, u[j], joined)
        done_ref[pl.ds(start + GROUP * p, GROUP), :] = joined
        for g in range(p + 1, groups):
            side = [full(rows[g][:, GROUP * p + k : GROUP * p + k + 1]) for k in eight]
            x = rows[g]
            for j in eight:
                side[j] = side[j] * r[j]
                for i in range(j + 1, GROUP):
                    side[i] = side[i] - m[i][j] * side[j]
                x = x - side[j] * u[j]
            rows[g] = x


def tile_factor(tile, pair_ref, done_ref, cross_ref, corner_ref):
    half = TILE // 2
    row = lax.broadcasted_iota(jnp.int32, (half, half), 0)
    col = lax.broadcasted_iota(jnp.int32, (half, half), 1)
    unit = jnp.where(row == col, 1.0, 0.0).astype(jnp.float32)
    zero = jnp.zeros((half, half), jnp.float32)
    pair_ref[...] = jnp.concatenate([tile[:half, :half], unit], axis=1)
    cross_ref[...] = tile[:half, half:]
    corner_ref[...] = tile[half:, half:]

    def turn(number, carry):
        half_factor(pair_ref, done_ref, pl.multiple_of(number * half, half))

        @pl.when(number == 0)
        def _():
            cross = near_product(done_ref[:half, half:], cross_ref[...], NN)
            cross_ref[...] = cross
            both = halves(cross)
            rest = corner_ref[...] - product_of_halves(both, both, TN)
            pair_ref[...] = jnp.concatenate([rest, unit], axis=1)

        return carry

    lax.fori_loop(0, 2, turn, 0)
    first, second = done_ref[:half, half:], done_ref[half:, half:]
    middle = near_product(cross_ref[...], first, TN)
    upper = jnp.concatenate(
        [
            jnp.concatenate([done_ref[:half, :half], cross_ref[...]], axis=1),
            jnp.concatenate([zero, done_ref[half:, :half]], axis=1),
        ],
        axis=0,
    )
    inverse = jnp.concatenate(
        [
            jnp.concatenate([first, zero], axis=1),
            jnp.concatenate([-near_product(second, middle, NN), second], axis=1),
        ],
        axis=0,
    )
    return upper, inverse


def halves(value):
    high = value.astype(jnp.bfloat16)
    return high, (value - high.astype(jnp.float32)).astype(jnp.bfloat16)


def product_of_halves(left, right, dims):
    total = product(left[0], right[0], dims, lax.Precision.DEFAULT)
    total = total + product(left[0], right[1], dims, lax.Precision.DEFAULT)
    return total + product(left[1], right[0], dims, lax.Precision.DEFAULT)


def lanes_at(number):
    return pl.ds(pl.multiple_of(number * WIDE, WIDE), WIDE)


def tall_product(left_refs, rows, depth, right_at, put, width):
    left = tuple(ref[:rows, :depth] for ref in left_refs)

    def block(number, carry):
        put(lanes_at(number), product_of_halves(left, halves(right_at(lanes_at(number))), NN))
        return carry

    lax.fori_loop(0, width // WIDE, block, 0)


def keep_halves(left_refs, value):
    rows, depth = value.shape
    high, low = halves(value)
    left_refs[0][:rows, :depth] = high
    left_refs[1][:rows, :depth] = low


def piece_shapes(side, lanes):
    return tuple(
        jax.ShapeDtypeStruct(((stop - start) * side, lanes), jnp.float32) for start, stop in PIECES
    )


def part_kernel(side, bounds, number, *refs):
    first, last = bounds[number], bounds[number + 1]
    final = number == len(bounds) - 2
    x_ref, start_ref = refs[:2]
    before = refs[2 : 2 + 2 * number]
    refs = refs[2 + 2 * number :]
    low_ref, outs = refs[0], refs[1:5]
    gram_refs, refs = (refs[5:7], refs[7:]) if final else ((), refs[5:])
    small_refs, refs = refs[:4], refs[4:]
    low_high_ref, low_less_ref, y_high_ref, y_less_ref = refs[:4]
    depth, width = x_ref.shape
    begin, end = first * TILE, last * TILE
    reach = end - TILE
    row = lax.broadcasted_iota(jnp.int32, (TILE, TILE), 0)
    col = lax.broadcasted_iota(jnp.int32, (TILE, TILE), 1)

    if number == 0:
        turned = refs[4:6]
        keep_halves(turned, x_ref[...].T)

        def gram(lanes, value):
            low_ref[:, lanes] = value

        tall_product(turned, width, depth, lambda lanes: x_ref[:, lanes], gram, width)
        for i in range(width // TILE):
            rows = slice(i * TILE, (i + 1) * TILE)
            low_ref[rows, rows] = low_ref[rows, rows] + jnp.where(
                row == col, jnp.broadcast_to(start_ref[:, rows], (TILE, TILE)), 0.0
            )
    else:
        low_ref[...] = start_ref[...]
        high, less = halves(start_ref[:, :begin])
        low_high_ref[:, :begin] = high
        low_less_ref[:, :begin] = less
        for k in range(number):
            lanes = slice(bounds[k] * TILE, bounds[k + 1] * TILE)
            for ref, rows in ((before[2 * k], slice(0, 2 * side)), (before[2 * k + 1], slice(2 * side, 3 * side))):
                high, less = halves(ref[...])
                y_high_ref[rows, lanes] = high
                y_less_ref[rows, lanes] = less
    for ref in (low_high_ref, low_less_ref):
        ref[:, begin:] = jnp.zeros((width, end - begin), jnp.bfloat16)
    for ref in (y_high_ref, y_less_ref):
        ref[:, begin:] = jnp.zeros((depth, end - begin), jnp.bfloat16)

    def step(j, carry):
        start = pl.multiple_of(j * TILE, TILE)
        cols = pl.ds(start, TILE)
        local = pl.ds(pl.multiple_of((j - first) * TILE, TILE), TILE)

        def reduced(value, high_ref, less_ref, rows):
            if reach == 0:
                return value
            return value - product_of_halves(
                (high_ref[rows, :reach], less_ref[rows, :reach]),
                (low_high_ref[cols, :reach], low_less_ref[cols, :reach]),
                NT,
            )

        tile = reduced(low_ref[cols, cols], low_high_ref, low_less_ref, cols)
        upper, inverse = tile_factor(tile, *small_refs)
        inverse = halves(inverse)
        for i in range(depth // side):
            rows = slice(i * side, (i + 1) * side)
            value = reduced(x_ref[rows, cols], y_high_ref, y_less_ref, rows)
            value = product_of_halves(halves(value), inverse, NT)
            for out_ref, (head, tail) in zip(outs, PIECES):
                if head <= i < tail:
                    out_ref[(i - head) * side : (i - head + 1) * side, local] = value
            high, less = halves(value)
            y_high_ref[rows, cols] = high
            y_less_ref[rows, cols] = less
        for i in range(first * TILE // WIDE, width // WIDE):
            rows = slice(i * WIDE, (i + 1) * WIDE)
            value = reduced(low_ref[rows, cols], low_high_ref, low_less_ref, rows)
            value = product_of_halves(halves(value), inverse, NT)
            place = lax.broadcasted_iota(jnp.int32, (WIDE, TILE), 0) + i * WIDE
            value = jnp.where(place >= start + TILE, value, 0.0)
            low_ref[rows, cols] = value
            high, less = halves(value)
            low_high_ref[rows, cols] = high
            low_less_ref[rows, cols] = less
        low_ref[cols, cols] = jnp.where(col <= row, upper.T, 0.0)
        return carry

    lax.fori_loop(first, last, step, 0)
    if number > 0:
        for i in range(first * TILE // WIDE):
            rows = slice(i * WIDE, (i + 1) * WIDE)
            low_ref[rows, begin:end] = jnp.zeros((WIDE, end - begin), jnp.float32)
    if final:
        for gram_ref, left, right in (
            (gram_refs[0], slice(2 * side, 3 * side), slice(0, 2 * side)),
            (gram_refs[1], slice(side, 2 * side), slice(0, side)),
        ):
            gram_ref[...] = product_of_halves(
                (y_high_ref[left, :], y_less_ref[left, :]),
                (y_high_ref[right, :], y_less_ref[right, :]),
                NT,
            )


def factored_part(x, start, before, side, bounds, number):
    depth, width = x.shape
    first, last = bounds[number], bounds[number + 1]
    final = number == len(bounds) - 2
    end = last * TILE
    shapes = [jax.ShapeDtypeStruct((width, width), jnp.float32)]
    shapes += piece_shapes(side, (last - first) * TILE)
    if final:
        shapes += [
            jax.ShapeDtypeStruct((side, 2 * side), jnp.float32),
            jax.ShapeDtypeStruct((side, side), jnp.float32),
        ]
    half = TILE // 2
    scratch = [pltpu.VMEM((half, TILE), jnp.float32), pltpu.VMEM((TILE, TILE), jnp.float32)]
    scratch += [pltpu.VMEM((half, half), jnp.float32)] * 2
    scratch += [pltpu.VMEM((width, end), jnp.bfloat16)] * 2
    scratch += [pltpu.VMEM((depth, end), jnp.bfloat16)] * 2
    if number == 0:
        scratch += [pltpu.VMEM((width, depth), jnp.bfloat16)] * 2
    return pl.pallas_call(
        functools.partial(part_kernel, side, bounds, number),
        out_shape=tuple(shapes),
        in_specs=[VMEM_SPEC] * (2 + len(before)),
        out_specs=(VMEM_SPEC,) * len(shapes),
        scratch_shapes=scratch,
        compiler_params=pltpu.CompilerParams(vmem_limit_bytes=24 << 20),
        cost_estimate=pl.CostEstimate(
            flops=20_000_000_000, bytes_accessed=3 * depth * width * 4, transcendentals=0
        ),
        name="factor_part",
    )(x, start, *before)


def near_product(left, right, dims):
    return product_of_halves(halves(left), halves(right), dims)


def put_coupling(side, start, y_refs, x_ref, buffer_ref, left_refs, out_ref, sems):
    rows = buffer_ref.shape[1]
    width = x_ref.shape[1]
    copies = []
    for place, (number, begin, end) in enumerate(((3, 0, 1), (1, 0, 2), (0, 1, 3), (2, 2, 3))):
        keep_halves(left_refs, y_refs[number][...].T)

        def put(lanes, value, place=place):
            buffer_ref[place, :, lanes] = value

        tall_product(
            left_refs,
            rows,
            (end - begin) * side,
            lambda lanes, begin=begin, end=end: x_ref[begin * side : end * side, lanes],
            put,
            width,
        )
        copy = pltpu.make_async_copy(
            buffer_ref.at[place], out_ref.at[place, pl.ds(start, rows), :], sems.at[place]
        )
        copy.start()
        copies.append(copy)
    return copies


def early_kernel(side, starts, x_ref, *refs):
    parts = len(starts)
    y_refs, refs = refs[: 4 * parts], refs[4 * parts :]
    out_ref, refs = refs[0], refs[1:]
    buffers, (high_ref, less_ref, sems) = refs[:parts], refs[parts:]
    copies = []
    for number, start in enumerate(starts):
        copies += put_coupling(
            side,
            start,
            y_refs[4 * number : 4 * number + 4],
            x_ref,
            buffers[number],
            (high_ref, less_ref),
            out_ref,
            sems.at[number],
        )
    for copy in copies:
        copy.wait()


def early(x, parts, starts, side):
    width = x.shape[1]
    heights = [part[0].shape[1] for part in parts]
    most = max(heights)
    return pl.pallas_call(
        functools.partial(early_kernel, side, starts),
        out_shape=jax.ShapeDtypeStruct((4, width, width), jnp.float32),
        in_specs=[VMEM_SPEC] * (1 + 4 * len(parts)),
        out_specs=ANY_SPEC,
        scratch_shapes=[pltpu.VMEM((4, height, width), jnp.float32) for height in heights]
        + [
            pltpu.VMEM((most, 2 * side), jnp.bfloat16),
            pltpu.VMEM((most, 2 * side), jnp.bfloat16),
            pltpu.SemaphoreType.DMA((len(parts), 4)),
        ],
        compiler_params=pltpu.CompilerParams(vmem_limit_bytes=24 << 20),
        cost_estimate=pl.CostEstimate(
            flops=8_000_000_000, bytes_accessed=4 * width * width * 4, transcendentals=0
        ),
        name="early",
    )(x, *[piece for part in parts for piece in part])


def late_kernel(side, starts, flags_ref, *refs):
    (
        x_ref,
        shift_ref,
        direct_ref,
        onward_ref,
        second_ref,
        extra_ref,
        low_ref,
        gram_one_ref,
        gram_two_ref,
    ) = refs[:9]
    parts = len(starts)
    refs = refs[9:]
    mine, refs = refs[:parts], refs[parts:]
    pieces, refs = [refs[4 * k : 4 * k + 4] for k in range(parts)], refs[4 * parts :]
    lasts = pieces[-1]
    partial_ref, schur_ref, coupling_ref = refs[:3]
    buffer_ref, tile_ref, rest_ref, near_ref, far_ref, high_ref, less_ref, sems, outs = refs[3:]
    left_refs = (high_ref, less_ref)
    width = x_ref.shape[1]
    cut = starts[-1]
    copies = put_coupling(side, cut, lasts, x_ref, buffer_ref, left_refs, coupling_ref, sems)
    own, above, second_above, under, second_under = [flags_ref[k] > 0 for k in range(5)]
    one, two, three = slice(0, side), slice(side, 2 * side), slice(2 * side, 3 * side)
    pair, tail = slice(0, 2 * side), slice(side, 3 * side)
    rest_ref[...] = x_ref[...]
    near_ref[three, :] = jnp.zeros((side, width), jnp.float32)
    far_ref[two, :] = jnp.zeros((side, width), jnp.float32)

    @pl.when(own)
    def _():
        for start, ref in zip(starts, mine):
            lanes = slice(start, start + ref.shape[1])
            near_ref[pair, lanes] = ref[...]
            far_ref[one, lanes] = ref[side:, :]

    @pl.when(jnp.logical_not(own))
    def _():
        near_ref[pair, :] = x_ref[tail, :]
        far_ref[one, :] = x_ref[three, :]

    def weighed(number, rows):
        gram = 0.0
        for part in pieces:
            both = halves(part[number][...])
            gram = gram + product_of_halves(both, both, NT)
        return near_product(gram, x_ref[rows, :], NN)

    @pl.when(second_above)
    def _():
        rest_ref[one, :] = rest_ref[one, :] - weighed(3, one)

    @pl.when(above)
    def _():
        term = weighed(1, pair)
        rest_ref[pair, :] = rest_ref[pair, :] - term
        near_ref[one, :] = near_ref[one, :] - term[side:]

    @pl.when(under)
    def _():
        term = weighed(0, tail)
        rest_ref[tail, :] = rest_ref[tail, :] - term
        far_ref[one, :] = far_ref[one, :] - term[side:]
        far_ref[two, :] = -near_product(gram_one_ref[...], x_ref[tail, :], NN)

    @pl.when(second_under)
    def _():
        term = weighed(2, three)
        rest_ref[three, :] = rest_ref[three, :] - term
        near_ref[two, :] = near_ref[two, :] - term
        near_ref[three, :] = -near_product(gram_two_ref[...], x_ref[three, :], NN)

    def put(place):
        copy = pltpu.make_async_copy(tile_ref.at[place], schur_ref.at[place], outs.at[place])
        copy.start()
        return copy

    def fill(place, left, right_ref):
        keep_halves(left_refs, left.T)

        def put(lanes, value):
            tile_ref[place, :, lanes] = value

        tall_product(
            left_refs, width, left.shape[0], lambda lanes: right_ref[:, lanes], put, width
        )

    def from_coupling(place, member):
        copy = pltpu.make_async_copy(
            partial_ref.at[member, pl.ds(0, cut), :],
            tile_ref.at[place, pl.ds(0, cut), :],
            outs.at[place],
        )
        copy.start()
        tile_ref[place, cut:, :] = buffer_ref[member]
        copy.wait()

    @pl.when(own)
    def _():
        tile_ref[2] = low_ref[...]

    @pl.when(jnp.logical_not(own))
    def _():
        fill(2, x_ref[...], rest_ref)
        for i in range(width // TILE):
            rows = slice(i * TILE, (i + 1) * TILE)
            row = lax.broadcasted_iota(jnp.int32, (TILE, TILE), 0)
            col = lax.broadcasted_iota(jnp.int32, (TILE, TILE), 1)
            tile_ref[2, rows, rows] = tile_ref[2, rows, rows] + jnp.where(
                row == col, jnp.broadcast_to(shift_ref[:, rows], (TILE, TILE)), 0.0
            )

    copies.append(put(2))

    @pl.when(under)
    def _():
        from_coupling(1, 2)

    @pl.when(jnp.logical_not(under))
    def _():
        below = direct_ref[...] + onward_ref[...]
        fill(1, jnp.concatenate([below, extra_ref[...]], axis=0), near_ref)

    copies.append(put(1))

    @pl.when(second_under)
    def _():
        from_coupling(0, 3)

    @pl.when(jnp.logical_not(second_under))
    def _():
        fill(0, second_ref[...], far_ref)

    copies.append(put(0))
    for copy in copies:
        copy.wait()


def late(flags, x, shift, received, low, grams, mine, parts, partial, starts, side):
    depth, width = x.shape
    rest = parts[-1][0].shape[1]
    inputs = [x, shift, *received, low, *grams, *mine] + [piece for part in parts for piece in part]
    return pl.pallas_call(
        functools.partial(late_kernel, side, starts),
        out_shape=(
            jax.ShapeDtypeStruct((3, width, width), jnp.float32),
            jax.ShapeDtypeStruct((4, width, width), jnp.float32),
        ),
        in_specs=[SMEM_SPEC] + [VMEM_SPEC] * len(inputs) + [ANY_SPEC],
        out_specs=(ANY_SPEC, ANY_SPEC),
        input_output_aliases={1 + len(inputs): 1},
        scratch_shapes=[
            pltpu.VMEM((4, rest, width), jnp.float32),
            pltpu.VMEM((3, width, width), jnp.float32),
            pltpu.VMEM((depth, width), jnp.float32),
            pltpu.VMEM((depth, width), jnp.float32),
            pltpu.VMEM((2 * side, width), jnp.float32),
            pltpu.VMEM((width, depth), jnp.bfloat16),
            pltpu.VMEM((width, depth), jnp.bfloat16),
            pltpu.SemaphoreType.DMA((4,)),
            pltpu.SemaphoreType.DMA((3,)),
        ],
        compiler_params=pltpu.CompilerParams(vmem_limit_bytes=40 << 20),
        cost_estimate=pl.CostEstimate(
            flops=12_000_000_000, bytes_accessed=7 * width * width * 4, transcendentals=0
        ),
        name="late",
    )(flags, *inputs, partial)


def local(weighted_jacobian_strips, leading_pose_index, levenberg_shift, removal_flags):
    count = lax.axis_size(AXES)
    own = lax.axis_index(AXES)
    surfels, _, width = weighted_jacobian_strips.shape
    capacity = max(2, (3 * surfels + 2 * count - 1) // (2 * count))
    side = count * capacity
    tiles = width // TILE
    bounds = (0, 1, tiles // 2, tiles - 1, tiles)
    starts = tuple(bound * TILE for bound in bounds[:-1])
    flags = removal_flags[(own + jnp.array((0, 1, 2, -1, -2), jnp.int32)) % count]

    chunks = bucketed(
        leading_pose_index.reshape(1, surfels),
        weighted_jacobian_strips.transpose(1, 0, 2),
        count,
        capacity,
    )
    chunks = lax.all_to_all(chunks, AXES, split_axis=0, concat_axis=0, tiled=True)
    x, two, last = regrouped(chunks, capacity, width)

    def sent_parts(parts):
        return [passed_along(part, steps) for part, steps in zip(parts, (1, -1, 2, -2))]

    direct = lax.ppermute(two, AXES, [(k, k + 1) for k in range(0, count, 2)])
    second = passed_along(two, 2)

    def solved(number, start, known):
        before = [part[k] for part in known for k in (0, 3)]
        return factored_part(x, start, before, side, bounds, number)

    low, *part = solved(0, levenberg_shift, ())
    known = [part]
    parts = [sent_parts(part)]
    for number in range(1, PARTS - 1):
        if number == 2:
            onward = lax.ppermute(second, AXES, [(k + 1, k) for k in range(0, count, 2)])
        low, *part = solved(number, low, known)
        known.append(part)
        parts.append(sent_parts(part))
    extra = passed_along(last, 1)
    low, *part, gram_one, gram_two = solved(PARTS - 1, low, known)
    known.append(part)
    parts.append(sent_parts(part))
    grams = (passed_along(gram_one, 1), passed_along(gram_two, 2))
    partial = early(x, parts[:-1], starts[:-1], side)
    schur, coupling = late(
        flags,
        x,
        levenberg_shift,
        (direct, onward, second, extra),
        low,
        grams,
        [part[1] for part in known],
        parts,
        partial,
        starts,
        side,
    )
    return schur[None], coupling[None]


def solution(mesh):
    in_specs = (P(AXES, None, None), P(AXES, None), P(AXES, None), P())
    out_specs = (P(AXES, None, None, None), P(AXES, None, None, None))

    return jax.shard_map(local, mesh=mesh, in_specs=in_specs, out_specs=out_specs, check_vma=False)
```

```python
import functools
import math

import jax
import jax.numpy as jnp
from jax import lax
from jax.experimental import pallas as pl
from jax.experimental.pallas import tpu as pltpu
from jax.sharding import PartitionSpec as P


AXES = ("gx", "gy")
TILE = 128
GROUP = 8
WIDE = 256
PARTS = 3
NT = (((1,), (1,)), ((), ()))
TN = (((0,), (0,)), ((), ()))
NN = (((1,), (0,)), ((), ()))
VMEM_SPEC = pl.BlockSpec(memory_space=pltpu.VMEM)
SMEM_SPEC = pl.BlockSpec(memory_space=pltpu.SMEM)
ANY_SPEC = pl.BlockSpec(memory_space=pl.ANY)
PIECES = ((0, 2), (1, 3), (0, 1), (2, 3))


def passed_along(value, steps):
    count = lax.axis_size(AXES)
    pairs = [(source, (source + steps) % count) for source in range(count)]
    return lax.ppermute(value, AXES, pairs)


def product(left, right, dims, precision=lax.Precision.HIGHEST):
    return lax.dot_general(
        left, right, dims, precision=precision, preferred_element_type=jnp.float32
    )


def bucket_kernel(count, capacity, index_ref, strips_ref, out_ref, rows_ref):
    surfels = strips_ref.shape[1]
    width = strips_ref.shape[2]
    lane_tiles = width // WIDE
    index = index_ref[...]
    base = lax.broadcasted_iota(jnp.int32, (count, surfels), 0)
    hot = (base == index).astype(jnp.float32)
    first = lax.broadcasted_iota(jnp.int32, (surfels, surfels), 0)
    second = lax.broadcasted_iota(jnp.int32, (surfels, surfels), 1)
    ahead = (first < second).astype(jnp.float32)
    earlier = product(hot, ahead, NN)
    within = jnp.sum(earlier * hot, axis=0, keepdims=True).astype(jnp.int32)
    period = GROUP // math.gcd(capacity, GROUP)
    for piece in range(3):
        moved = index + piece
        moved = jnp.where(moved >= count, moved - count, moved)
        slot = moved * capacity + within
        row = lax.broadcasted_iota(jnp.int32, (count * capacity, surfels), 0)
        pick = (row == slot).astype(jnp.bfloat16)
        values = strips_ref[piece]
        high = values.astype(jnp.bfloat16)
        rest = values - high.astype(jnp.float32)
        middle = rest.astype(jnp.bfloat16)
        low = (rest - middle.astype(jnp.float32)).astype(jnp.bfloat16)
        rows_ref[...] = product(
            jnp.concatenate([pick, pick, pick], axis=1),
            jnp.concatenate([high, middle, low], axis=0),
            NN,
            lax.Precision.DEFAULT,
        )

        def spread(turn, carry, piece=piece):
            start = pl.multiple_of(turn * (period * capacity), GROUP)
            for tile in range(lane_tiles):
                block = rows_ref[pl.ds(start, period * capacity), WIDE * tile : WIDE * (tile + 1)]
                for member in range(period):
                    begin = (piece * lane_tiles + tile) * capacity
                    out_ref[turn * period + member, begin : begin + capacity, :] = block[
                        member * capacity : (member + 1) * capacity
                    ]
            return carry

        lax.fori_loop(0, count // period, spread, 0)


def bucketed(index_row, strips, count, capacity):
    width = strips.shape[2]
    return pl.pallas_call(
        functools.partial(bucket_kernel, count, capacity),
        out_shape=jax.ShapeDtypeStruct(
            (count, 3 * (width // WIDE) * capacity, WIDE), jnp.float32
        ),
        in_specs=[VMEM_SPEC, VMEM_SPEC],
        out_specs=VMEM_SPEC,
        scratch_shapes=[pltpu.VMEM((count * capacity, width), jnp.float32)],
        name="bucket",
    )(index_row, strips)


def regroup_kernel(capacity, in_ref, out_ref, two_ref, one_ref):
    count = in_ref.shape[0]
    width = out_ref.shape[1]
    lane_tiles = width // WIDE
    period = GROUP // math.gcd(capacity, GROUP)

    def gather(turn, carry):
        for piece in range(3):
            for tile in range(lane_tiles):
                begin = (piece * lane_tiles + tile) * capacity
                block = jnp.concatenate(
                    [
                        in_ref[turn * period + member, begin : begin + capacity, :]
                        for member in range(period)
                    ],
                    axis=0,
                )
                start = pl.multiple_of(
                    piece * count * capacity + turn * (period * capacity), GROUP
                )
                out_ref[
                    pl.ds(start, period * capacity), WIDE * tile : WIDE * (tile + 1)
                ] = block
        return carry

    lax.fori_loop(0, count // period, gather, 0)
    side = count * capacity
    two_ref[...] = out_ref[: 2 * side, :]
    one_ref[...] = out_ref[2 * side :, :]


def regrouped(chunks, capacity, width):
    side = chunks.shape[0] * capacity
    return pl.pallas_call(
        functools.partial(regroup_kernel, capacity),
        out_shape=tuple(
            jax.ShapeDtypeStruct((parts * side, width), jnp.float32) for parts in (3, 2, 1)
        ),
        in_specs=[VMEM_SPEC],
        out_specs=(VMEM_SPEC,) * 3,
        compiler_params=pltpu.CompilerParams(vmem_limit_bytes=16 << 20),
        name="regroup",
    )(chunks)


def full(value):
    return jnp.broadcast_to(value, (GROUP, TILE))


def half_factor(pair_ref, done_ref, start):
    groups = pair_ref.shape[0] // GROUP
    sub = lax.broadcasted_iota(jnp.int32, (GROUP, TILE), 0)
    rows = [pair_ref[GROUP * g : GROUP * (g + 1), :] for g in range(groups)]
    eight = range(GROUP)
    for p in range(groups):
        strip = rows[p]
        cols = [full(strip[:, GROUP * p + k : GROUP * p + k + 1]) for k in eight]
        m = [[full(cols[k][i : i + 1, :]) if k <= i else None for k in eight] for i in eight]
        r = [None] * GROUP
        u = [full(strip[j : j + 1, :]) for j in eight]
        for j in eight:
            r[j] = lax.rsqrt(m[j][j])
            for i in range(j + 1, GROUP):
                m[i][j] = m[i][j] * r[j]
            for k in range(j + 1, GROUP):
                for i in range(k, GROUP):
                    m[i][k] = m[i][k] - m[i][j] * m[k][j]
            u[j] = u[j] * r[j]
            for i in range(j + 1, GROUP):
                u[i] = u[i] - m[i][j] * u[j]
        joined = u[0]
        for j in range(1, GROUP):
            joined = jnp.where(sub == j, u[j], joined)
        done_ref[pl.ds(start + GROUP * p, GROUP), :] = joined
        for g in range(p + 1, groups):
            side = [full(rows[g][:, GROUP * p + k : GROUP * p + k + 1]) for k in eight]
            x = rows[g]
            for j in eight:
                side[j] = side[j] * r[j]
                for i in range(j + 1, GROUP):
                    side[i] = side[i] - m[i][j] * side[j]
                x = x - side[j] * u[j]
            rows[g] = x


def tile_factor(tile, pair_ref, done_ref, cross_ref, corner_ref):
    half = TILE // 2
    row = lax.broadcasted_iota(jnp.int32, (half, half), 0)
    col = lax.broadcasted_iota(jnp.int32, (half, half), 1)
    unit = jnp.where(row == col, 1.0, 0.0).astype(jnp.float32)
    zero = jnp.zeros((half, half), jnp.float32)
    pair_ref[...] = jnp.concatenate([tile[:half, :half], unit], axis=1)
    cross_ref[...] = tile[:half, half:]
    corner_ref[...] = tile[half:, half:]

    def turn(number, carry):
        half_factor(pair_ref, done_ref, pl.multiple_of(number * half, half))

        @pl.when(number == 0)
        def _():
            cross = near_product(done_ref[:half, half:], cross_ref[...], NN)
            cross_ref[...] = cross
            both = halves(cross)
            rest = corner_ref[...] - product_of_halves(both, both, TN)
            pair_ref[...] = jnp.concatenate([rest, unit], axis=1)

        return carry

    lax.fori_loop(0, 2, turn, 0)
    first, second = done_ref[:half, half:], done_ref[half:, half:]
    middle = near_product(cross_ref[...], first, TN)
    upper = jnp.concatenate(
        [
            jnp.concatenate([done_ref[:half, :half], cross_ref[...]], axis=1),
            jnp.concatenate([zero, done_ref[half:, :half]], axis=1),
        ],
        axis=0,
    )
    inverse = jnp.concatenate(
        [
            jnp.concatenate([first, zero], axis=1),
            jnp.concatenate([-near_product(second, middle, NN), second], axis=1),
        ],
        axis=0,
    )
    return upper, inverse


def halves(value):
    high = value.astype(jnp.bfloat16)
    return high, (value - high.astype(jnp.float32)).astype(jnp.bfloat16)


def product_of_halves(left, right, dims):
    total = product(left[0], right[0], dims, lax.Precision.DEFAULT)
    total = total + product(left[0], right[1], dims, lax.Precision.DEFAULT)
    return total + product(left[1], right[0], dims, lax.Precision.DEFAULT)


def lanes_at(number):
    return pl.ds(pl.multiple_of(number * WIDE, WIDE), WIDE)


def tall_product(left_refs, rows, depth, right_at, put, width):
    left = tuple(ref[:rows, :depth] for ref in left_refs)

    def block(number, carry):
        put(lanes_at(number), product_of_halves(left, halves(right_at(lanes_at(number))), NN))
        return carry

    lax.fori_loop(0, width // WIDE, block, 0)


def keep_halves(left_refs, value):
    rows, depth = value.shape
    high, low = halves(value)
    left_refs[0][:rows, :depth] = high
    left_refs[1][:rows, :depth] = low


def piece_shapes(side, lanes):
    return tuple(
        jax.ShapeDtypeStruct(((stop - start) * side, lanes), jnp.float32) for start, stop in PIECES
    )


def part_kernel(side, bounds, number, *refs):
    first, last = bounds[number], bounds[number + 1]
    final = number == len(bounds) - 2
    x_ref, start_ref = refs[:2]
    before = refs[2 : 2 + 2 * number]
    refs = refs[2 + 2 * number :]
    low_ref, outs = refs[0], refs[1:5]
    gram_refs, refs = (refs[5:7], refs[7:]) if final else ((), refs[5:])
    small_refs, refs = refs[:4], refs[4:]
    low_high_ref, low_less_ref, y_high_ref, y_less_ref = refs[:4]
    depth, width = x_ref.shape
    begin, end = first * TILE, last * TILE
    reach = end - TILE
    row = lax.broadcasted_iota(jnp.int32, (TILE, TILE), 0)
    col = lax.broadcasted_iota(jnp.int32, (TILE, TILE), 1)

    if number == 0:
        turned = refs[4:6]
        keep_halves(turned, x_ref[...].T)

        def gram(lanes, value):
            low_ref[:, lanes] = value

        tall_product(turned, width, depth, lambda lanes: x_ref[:, lanes], gram, width)
        for i in range(width // TILE):
            rows = slice(i * TILE, (i + 1) * TILE)
            low_ref[rows, rows] = low_ref[rows, rows] + jnp.where(
                row == col, jnp.broadcast_to(start_ref[:, rows], (TILE, TILE)), 0.0
            )
    else:
        low_ref[...] = start_ref[...]
        high, less = halves(start_ref[:, :begin])
        low_high_ref[:, :begin] = high
        low_less_ref[:, :begin] = less
        for k in range(number):
            lanes = slice(bounds[k] * TILE, bounds[k + 1] * TILE)
            for ref, rows in ((before[2 * k], slice(0, 2 * side)), (before[2 * k + 1], slice(2 * side, 3 * side))):
                high, less = halves(ref[...])
                y_high_ref[rows, lanes] = high
                y_less_ref[rows, lanes] = less
    for ref in (low_high_ref, low_less_ref):
        ref[:, begin:] = jnp.zeros((width, end - begin), jnp.bfloat16)
    for ref in (y_high_ref, y_less_ref):
        ref[:, begin:] = jnp.zeros((depth, end - begin), jnp.bfloat16)

    def step(j, carry):
        start = pl.multiple_of(j * TILE, TILE)
        cols = pl.ds(start, TILE)
        local = pl.ds(pl.multiple_of((j - first) * TILE, TILE), TILE)

        def reduced(value, high_ref, less_ref, rows):
            if reach == 0:
                return value
            return value - product_of_halves(
                (high_ref[rows, :reach], less_ref[rows, :reach]),
                (low_high_ref[cols, :reach], low_less_ref[cols, :reach]),
                NT,
            )

        tile = reduced(low_ref[cols, cols], low_high_ref, low_less_ref, cols)
        upper, inverse = tile_factor(tile, *small_refs)
        inverse = halves(inverse)
        for i in range(depth // side):
            rows = slice(i * side, (i + 1) * side)
            value = reduced(x_ref[rows, cols], y_high_ref, y_less_ref, rows)
            value = product_of_halves(halves(value), inverse, NT)
            for out_ref, (head, tail) in zip(outs, PIECES):
                if head <= i < tail:
                    out_ref[(i - head) * side : (i - head + 1) * side, local] = value
            high, less = halves(value)
            y_high_ref[rows, cols] = high
            y_less_ref[rows, cols] = less
        for i in range(first * TILE // WIDE, width // WIDE):
            rows = slice(i * WIDE, (i + 1) * WIDE)
            value = reduced(low_ref[rows, cols], low_high_ref, low_less_ref, rows)
            value = product_of_halves(halves(value), inverse, NT)
            place = lax.broadcasted_iota(jnp.int32, (WIDE, TILE), 0) + i * WIDE
            value = jnp.where(place >= start + TILE, value, 0.0)
            low_ref[rows, cols] = value
            high, less = halves(value)
            low_high_ref[rows, cols] = high
            low_less_ref[rows, cols] = less
        low_ref[cols, cols] = jnp.where(col <= row, upper.T, 0.0)
        return carry

    lax.fori_loop(first, last, step, 0)
    if number > 0:
        for i in range(first * TILE // WIDE):
            rows = slice(i * WIDE, (i + 1) * WIDE)
            low_ref[rows, begin:end] = jnp.zeros((WIDE, end - begin), jnp.float32)
    if final:
        for gram_ref, left, right in (
            (gram_refs[0], slice(2 * side, 3 * side), slice(0, 2 * side)),
            (gram_refs[1], slice(side, 2 * side), slice(0, side)),
        ):
            gram_ref[...] = product_of_halves(
                (y_high_ref[left, :], y_less_ref[left, :]),
                (y_high_ref[right, :], y_less_ref[right, :]),
                NT,
            )


def factored_part(x, start, before, side, bounds, number):
    depth, width = x.shape
    first, last = bounds[number], bounds[number + 1]
    final = number == len(bounds) - 2
    end = last * TILE
    shapes = [jax.ShapeDtypeStruct((width, width), jnp.float32)]
    shapes += piece_shapes(side, (last - first) * TILE)
    if final:
        shapes += [
            jax.ShapeDtypeStruct((side, 2 * side), jnp.float32),
            jax.ShapeDtypeStruct((side, side), jnp.float32),
        ]
    half = TILE // 2
    scratch = [pltpu.VMEM((half, TILE), jnp.float32), pltpu.VMEM((TILE, TILE), jnp.float32)]
    scratch += [pltpu.VMEM((half, half), jnp.float32)] * 2
    scratch += [pltpu.VMEM((width, end), jnp.bfloat16)] * 2
    scratch += [pltpu.VMEM((depth, end), jnp.bfloat16)] * 2
    if number == 0:
        scratch += [pltpu.VMEM((width, depth), jnp.bfloat16)] * 2
    return pl.pallas_call(
        functools.partial(part_kernel, side, bounds, number),
        out_shape=tuple(shapes),
        in_specs=[VMEM_SPEC] * (2 + len(before)),
        out_specs=(VMEM_SPEC,) * len(shapes),
        scratch_shapes=scratch,
        compiler_params=pltpu.CompilerParams(vmem_limit_bytes=24 << 20),
        cost_estimate=pl.CostEstimate(
            flops=20_000_000_000, bytes_accessed=3 * depth * width * 4, transcendentals=0
        ),
        name="factor_part",
    )(x, start, *before)


def near_product(left, right, dims):
    return product_of_halves(halves(left), halves(right), dims)


COUPLINGS = ((3, 0, 1), (1, 0, 2), (0, 1, 3), (2, 2, 3))


def put_coupling(side, start, y_refs, x_ref, buffer_ref, left_refs, out_ref, sems, places=range(4)):
    rows = buffer_ref.shape[1]
    width = x_ref.shape[1]
    copies = []
    for place in places:
        number, begin, end = COUPLINGS[place]
        keep_halves(left_refs, y_refs[number][...].T)

        def put(lanes, value, place=place):
            buffer_ref[place, :, lanes] = value

        tall_product(
            left_refs,
            rows,
            (end - begin) * side,
            lambda lanes, begin=begin, end=end: x_ref[begin * side : end * side, lanes],
            put,
            width,
        )
        copy = pltpu.make_async_copy(
            buffer_ref.at[place], out_ref.at[place, pl.ds(start, rows), :], sems.at[place]
        )
        copy.start()
        copies.append(copy)
    return copies


def early_kernel(side, starts, x_ref, *refs):
    parts = len(starts)
    y_refs, refs = refs[: 4 * parts], refs[4 * parts :]
    out_ref, refs = refs[0], refs[1:]
    buffers, (high_ref, less_ref, sems) = refs[:parts], refs[parts:]
    copies = []
    for number, start in enumerate(starts):
        copies += put_coupling(
            side,
            start,
            y_refs[4 * number : 4 * number + 4],
            x_ref,
            buffers[number],
            (high_ref, less_ref),
            out_ref,
            sems.at[number],
        )
    for copy in copies:
        copy.wait()


def early(x, parts, starts, side):
    width = x.shape[1]
    heights = [part[0].shape[1] for part in parts]
    most = max(heights)
    return pl.pallas_call(
        functools.partial(early_kernel, side, starts),
        out_shape=jax.ShapeDtypeStruct((4, width, width), jnp.float32),
        in_specs=[VMEM_SPEC] * (1 + 4 * len(parts)),
        out_specs=ANY_SPEC,
        scratch_shapes=[pltpu.VMEM((4, height, width), jnp.float32) for height in heights]
        + [
            pltpu.VMEM((most, 2 * side), jnp.bfloat16),
            pltpu.VMEM((most, 2 * side), jnp.bfloat16),
            pltpu.SemaphoreType.DMA((len(parts), 4)),
        ],
        compiler_params=pltpu.CompilerParams(vmem_limit_bytes=24 << 20),
        cost_estimate=pl.CostEstimate(
            flops=8_000_000_000, bytes_accessed=4 * width * width * 4, transcendentals=0
        ),
        name="early",
    )(x, *[piece for part in parts for piece in part])


def middle_kernel(side, starts, flags_ref, *refs):
    (
        x_ref,
        shift_ref,
        direct_ref,
        onward_ref,
        second_ref,
        extra_ref,
        low_ref,
        gram_one_ref,
        gram_two_ref,
    ) = refs[:9]
    parts = len(starts)
    refs = refs[9:]
    mine, refs = refs[:parts], refs[parts:]
    pieces, refs = [refs[4 * k : 4 * k + 4] for k in range(parts - 1)], refs[4 * parts - 4 :]
    lasts, refs = (refs[0], None, *refs[1:3]), refs[3:]
    pieces.append(lasts)
    partial_ref, schur_ref, coupling_ref = refs[:3]
    buffer_ref, tile_ref, rest_ref, near_ref, far_ref, high_ref, less_ref, sems, outs = refs[3:]
    left_refs = (high_ref, less_ref)
    width = x_ref.shape[1]
    cut = starts[-1]
    copies = put_coupling(
        side, cut, lasts, x_ref, buffer_ref, left_refs, coupling_ref, sems, (0, 3, 2)
    )
    own, above, second_above, under, second_under = [flags_ref[k] > 0 for k in range(5)]
    one, two, three = slice(0, side), slice(side, 2 * side), slice(2 * side, 3 * side)
    pair, tail = slice(0, 2 * side), slice(side, 3 * side)
    rest_ref[...] = x_ref[...]
    near_ref[three, :] = jnp.zeros((side, width), jnp.float32)
    far_ref[two, :] = jnp.zeros((side, width), jnp.float32)

    @pl.when(own)
    def _():
        for start, ref in zip(starts, mine):
            lanes = slice(start, start + ref.shape[1])
            near_ref[pair, lanes] = ref[...]
            far_ref[one, lanes] = ref[side:, :]

    @pl.when(jnp.logical_not(own))
    def _():
        near_ref[pair, :] = x_ref[tail, :]
        far_ref[one, :] = x_ref[three, :]

    def weighed(number, rows):
        gram = 0.0
        for part in pieces:
            if part[number] is None:
                continue
            both = halves(part[number][...])
            gram = gram + product_of_halves(both, both, NT)
        return near_product(gram, x_ref[rows, :], NN)

    @pl.when(second_above)
    def _():
        rest_ref[one, :] = rest_ref[one, :] - weighed(3, one)

    @pl.when(above)
    def _():
        term = weighed(1, pair)
        rest_ref[pair, :] = rest_ref[pair, :] - term
        near_ref[one, :] = near_ref[one, :] - term[side:]

    @pl.when(under)
    def _():
        term = weighed(0, tail)
        rest_ref[tail, :] = rest_ref[tail, :] - term
        far_ref[one, :] = far_ref[one, :] - term[side:]
        far_ref[two, :] = -near_product(gram_one_ref[...], x_ref[tail, :], NN)

    @pl.when(second_under)
    def _():
        term = weighed(2, three)
        rest_ref[three, :] = rest_ref[three, :] - term
        near_ref[two, :] = near_ref[two, :] - term
        near_ref[three, :] = -near_product(gram_two_ref[...], x_ref[three, :], NN)

    def put(place):
        copy = pltpu.make_async_copy(tile_ref.at[place], schur_ref.at[place], outs.at[place])
        copy.start()
        return copy

    def fill(place, left, right_ref):
        keep_halves(left_refs, left.T)

        def put(lanes, value):
            tile_ref[place, :, lanes] = value

        tall_product(
            left_refs, width, left.shape[0], lambda lanes: right_ref[:, lanes], put, width
        )

    def from_coupling(place, member):
        copy = pltpu.make_async_copy(
            partial_ref.at[member, pl.ds(0, cut), :],
            tile_ref.at[place, pl.ds(0, cut), :],
            outs.at[place],
        )
        copy.start()
        tile_ref[place, cut:, :] = buffer_ref[member]
        copy.wait()

    @pl.when(own)
    def _():
        tile_ref[2] = low_ref[...]

    @pl.when(jnp.logical_not(own))
    def _():
        fill(2, x_ref[...], rest_ref)
        for i in range(width // TILE):
            rows = slice(i * TILE, (i + 1) * TILE)
            row = lax.broadcasted_iota(jnp.int32, (TILE, TILE), 0)
            col = lax.broadcasted_iota(jnp.int32, (TILE, TILE), 1)
            tile_ref[2, rows, rows] = tile_ref[2, rows, rows] + jnp.where(
                row == col, jnp.broadcast_to(shift_ref[:, rows], (TILE, TILE)), 0.0
            )

    copies.append(put(2))

    @pl.when(under)
    def _():
        from_coupling(1, 2)

    @pl.when(jnp.logical_not(under))
    def _():
        below = direct_ref[...] + onward_ref[...]
        fill(1, jnp.concatenate([below, extra_ref[...]], axis=0), near_ref)

    copies.append(put(1))

    @pl.when(second_under)
    def _():
        from_coupling(0, 3)

    @pl.when(jnp.logical_not(second_under))
    def _():
        fill(0, second_ref[...], far_ref)

    copies.append(put(0))
    for copy in copies:
        copy.wait()


def middle(flags, x, shift, received, low, grams, mine, parts, partial, starts, side):
    depth, width = x.shape
    rest = parts[-1][0].shape[1]
    inputs = [x, shift, *received, low, *grams, *mine] + [piece for part in parts[:-1] for piece in part]
    inputs += [parts[-1][0], *parts[-1][2:]]
    return pl.pallas_call(
        functools.partial(middle_kernel, side, starts),
        out_shape=(
            jax.ShapeDtypeStruct((3, width, width), jnp.float32),
            jax.ShapeDtypeStruct((4, width, width), jnp.float32),
        ),
        in_specs=[SMEM_SPEC] + [VMEM_SPEC] * len(inputs) + [ANY_SPEC],
        out_specs=(ANY_SPEC, ANY_SPEC),
        input_output_aliases={1 + len(inputs): 1},
        scratch_shapes=[
            pltpu.VMEM((4, rest, width), jnp.float32),
            pltpu.VMEM((3, width, width), jnp.float32),
            pltpu.VMEM((depth, width), jnp.float32),
            pltpu.VMEM((depth, width), jnp.float32),
            pltpu.VMEM((2 * side, width), jnp.float32),
            pltpu.VMEM((width, depth), jnp.bfloat16),
            pltpu.VMEM((width, depth), jnp.bfloat16),
            pltpu.SemaphoreType.DMA((4,)),
            pltpu.SemaphoreType.DMA((3,)),
        ],
        compiler_params=pltpu.CompilerParams(vmem_limit_bytes=40 << 20),
        cost_estimate=pl.CostEstimate(
            flops=12_000_000_000, bytes_accessed=7 * width * width * 4, transcendentals=0
        ),
        name="middle",
    )(flags, *inputs, partial)


def late_kernel(side, flags_ref, x_ref, direct_ref, onward_ref, y_ref, *refs):
    tiles_ref, _, schur_ref, coupling_ref = refs[:4]
    buffer_ref, tile_ref, high_ref, less_ref, small_ref, sem, ins, outs = refs[4:]
    left_refs = (high_ref, less_ref)
    rows, width = buffer_ref.shape[1:]
    above = flags_ref[1] > 0

    def moved(place, back):
        held = tile_ref.at[place - 1]
        if back:
            return pltpu.make_async_copy(held, schur_ref.at[place], outs.at[place - 1])
        return pltpu.make_async_copy(tiles_ref.at[place], held, ins.at[place - 1])

    @pl.when(above)
    def _():
        moved(2, False).start()
        moved(1, False).start()

    keep_halves(left_refs, y_ref[...].T)

    def put(lanes, value):
        buffer_ref[0, :, lanes] = value

    tall_product(left_refs, rows, 2 * side, lambda lanes: x_ref[: 2 * side, lanes], put, width)
    copy = pltpu.make_async_copy(
        buffer_ref.at[0], coupling_ref.at[1, pl.ds(width - rows, rows), :], sem
    )
    copy.start()

    @pl.when(above)
    def _():
        keep_halves(left_refs, buffer_ref[0].T)
        moved(2, False).wait()

        def less_diag(lanes, value):
            tile_ref[1, :, lanes] = tile_ref[1, :, lanes] - value

        tall_product(left_refs, width, rows, lambda lanes: buffer_ref[0, :, lanes], less_diag, width)
        moved(2, True).start()
        keep_halves(left_refs, y_ref[side:, :])

        def put_small(lanes, value):
            small_ref[:, lanes] = value

        tall_product(left_refs, side, rows, lambda lanes: buffer_ref[0, :, lanes], put_small, width)
        keep_halves(left_refs, (direct_ref[:side, :] + onward_ref[:side, :]).T)
        moved(1, False).wait()

        def less_near(lanes, value):
            tile_ref[0, :, lanes] = tile_ref[0, :, lanes] - value

        tall_product(left_refs, width, side, lambda lanes: small_ref[:, lanes], less_near, width)
        moved(1, True).start()
        moved(2, True).wait()
        moved(1, True).wait()

    copy.wait()


def late(flags, x, direct, onward, y, tiles, coupling, side):
    _, width = x.shape
    rows = y.shape[1]
    return pl.pallas_call(
        functools.partial(late_kernel, side),
        out_shape=(
            jax.ShapeDtypeStruct((3, width, width), jnp.float32),
            jax.ShapeDtypeStruct((4, width, width), jnp.float32),
        ),
        in_specs=[SMEM_SPEC] + [VMEM_SPEC] * 4 + [ANY_SPEC] * 2,
        out_specs=(ANY_SPEC, ANY_SPEC),
        input_output_aliases={5: 0, 6: 1},
        scratch_shapes=[
            pltpu.VMEM((1, rows, width), jnp.float32),
            pltpu.VMEM((2, width, width), jnp.float32),
            pltpu.VMEM((width, max(2 * side, rows)), jnp.bfloat16),
            pltpu.VMEM((width, max(2 * side, rows)), jnp.bfloat16),
            pltpu.VMEM((side, width), jnp.float32),
            pltpu.SemaphoreType.DMA,
            pltpu.SemaphoreType.DMA((2,)),
            pltpu.SemaphoreType.DMA((2,)),
        ],
        compiler_params=pltpu.CompilerParams(vmem_limit_bytes=24 << 20),
        cost_estimate=pl.CostEstimate(
            flops=4_000_000_000, bytes_accessed=4 * width * width * 4, transcendentals=0
        ),
        name="late",
    )(flags, x, direct, onward, y, tiles, coupling)


def local(weighted_jacobian_strips, leading_pose_index, levenberg_shift, removal_flags):
    count = lax.axis_size(AXES)
    own = lax.axis_index(AXES)
    surfels, _, width = weighted_jacobian_strips.shape
    capacity = max(2, (3 * surfels + 2 * count - 1) // (2 * count))
    side = count * capacity
    tiles = width // TILE
    bounds = tuple(tiles * k // PARTS for k in range(PARTS + 1))
    starts = tuple(bound * TILE for bound in bounds[:-1])
    flags = removal_flags[(own + jnp.array((0, 1, 2, -1, -2), jnp.int32)) % count]

    chunks = bucketed(
        leading_pose_index.reshape(1, surfels),
        weighted_jacobian_strips.transpose(1, 0, 2),
        count,
        capacity,
    )
    chunks = lax.all_to_all(chunks, AXES, split_axis=0, concat_axis=0, tiled=True)
    x, two, last = regrouped(chunks, capacity, width)

    def sent_parts(parts):
        return [passed_along(part, steps) for part, steps in zip(parts, (1, -1, 2, -2))]

    direct = lax.ppermute(two, AXES, [(k, k + 1) for k in range(0, count, 2)])
    second = passed_along(two, 2)

    def solved(number, start, known):
        before = [part[k] for part in known for k in (0, 3)]
        return factored_part(x, start, before, side, bounds, number)

    low, *part = solved(0, levenberg_shift, ())
    known = [part]
    parts = [sent_parts(part)]
    for number in range(1, PARTS - 1):
        low, *part = solved(number, low, known)
        known.append(part)
        parts.append(sent_parts(part))
    onward = lax.ppermute(second, AXES, [(k + 1, k) for k in range(0, count, 2)])
    extra = passed_along(last, 1)
    low, *part, gram_one, gram_two = solved(PARTS - 1, low, known)
    known.append(part)
    parts.append(sent_parts(part))
    grams = (passed_along(gram_one, 1), passed_along(gram_two, 2))
    partial = early(x, parts[:-1], starts[:-1], side)
    schur, coupling = middle(
        flags,
        x,
        levenberg_shift,
        (direct, onward, second, extra),
        low,
        grams,
        [part[1] for part in known],
        parts,
        partial,
        starts,
        side,
    )
    schur, coupling = late(
        flags, x, direct, onward, parts[-1][1], schur, coupling, side
    )
    return schur[None], coupling[None]


def solution(mesh):
    in_specs = (P(AXES, None, None), P(AXES, None), P(AXES, None), P())
    out_specs = (P(AXES, None, None, None), P(AXES, None, None, None))

    return jax.shard_map(local, mesh=mesh, in_specs=in_specs, out_specs=out_specs, check_vma=False)
```

```python
import functools
import math

import jax
import jax.numpy as jnp
from jax import lax
from jax.experimental import pallas as pl
from jax.experimental.pallas import tpu as pltpu
from jax.sharding import PartitionSpec as P


AXES = ("gx", "gy")
TILE = 128
GROUP = 8
WIDE = 256
PARTS = 3
NT = (((1,), (1,)), ((), ()))
TN = (((0,), (0,)), ((), ()))
NN = (((1,), (0,)), ((), ()))
VMEM_SPEC = pl.BlockSpec(memory_space=pltpu.VMEM)
SMEM_SPEC = pl.BlockSpec(memory_space=pltpu.SMEM)
ANY_SPEC = pl.BlockSpec(memory_space=pl.ANY)
PIECES = ((0, 2), (1, 3), (0, 1), (2, 3))


def passed_along(value, steps):
    count = lax.axis_size(AXES)
    pairs = [(source, (source + steps) % count) for source in range(count)]
    return lax.ppermute(value, AXES, pairs)


def product(left, right, dims, precision=lax.Precision.HIGHEST):
    return lax.dot_general(
        left, right, dims, precision=precision, preferred_element_type=jnp.float32
    )


def bucket_kernel(count, capacity, index_ref, strips_ref, out_ref, rows_ref):
    surfels = strips_ref.shape[1]
    width = strips_ref.shape[2]
    lane_tiles = width // WIDE
    index = index_ref[...]
    base = lax.broadcasted_iota(jnp.int32, (count, surfels), 0)
    hot = (base == index).astype(jnp.float32)
    first = lax.broadcasted_iota(jnp.int32, (surfels, surfels), 0)
    second = lax.broadcasted_iota(jnp.int32, (surfels, surfels), 1)
    ahead = (first < second).astype(jnp.float32)
    earlier = product(hot, ahead, NN)
    within = jnp.sum(earlier * hot, axis=0, keepdims=True).astype(jnp.int32)
    period = GROUP // math.gcd(capacity, GROUP)
    for piece in range(3):
        moved = index + piece
        moved = jnp.where(moved >= count, moved - count, moved)
        slot = moved * capacity + within
        row = lax.broadcasted_iota(jnp.int32, (count * capacity, surfels), 0)
        pick = (row == slot).astype(jnp.bfloat16)
        values = strips_ref[piece]
        high = values.astype(jnp.bfloat16)
        rest = values - high.astype(jnp.float32)
        middle = rest.astype(jnp.bfloat16)
        low = (rest - middle.astype(jnp.float32)).astype(jnp.bfloat16)
        rows_ref[...] = product(
            jnp.concatenate([pick, pick, pick], axis=1),
            jnp.concatenate([high, middle, low], axis=0),
            NN,
            lax.Precision.DEFAULT,
        )

        def spread(turn, carry, piece=piece):
            start = pl.multiple_of(turn * (period * capacity), GROUP)
            for tile in range(lane_tiles):
                block = rows_ref[pl.ds(start, period * capacity), WIDE * tile : WIDE * (tile + 1)]
                for member in range(period):
                    begin = (piece * lane_tiles + tile) * capacity
                    out_ref[turn * period + member, begin : begin + capacity, :] = block[
                        member * capacity : (member + 1) * capacity
                    ]
            return carry

        lax.fori_loop(0, count // period, spread, 0)


def bucketed(index_row, strips, count, capacity):
    width = strips.shape[2]
    return pl.pallas_call(
        functools.partial(bucket_kernel, count, capacity),
        out_shape=jax.ShapeDtypeStruct(
            (count, 3 * (width // WIDE) * capacity, WIDE), jnp.float32
        ),
        in_specs=[VMEM_SPEC, VMEM_SPEC],
        out_specs=VMEM_SPEC,
        scratch_shapes=[pltpu.VMEM((count * capacity, width), jnp.float32)],
        name="bucket",
    )(index_row, strips)


def regroup_kernel(capacity, in_ref, out_ref, two_ref, one_ref):
    count = in_ref.shape[0]
    width = out_ref.shape[1]
    lane_tiles = width // WIDE
    period = GROUP // math.gcd(capacity, GROUP)

    def gather(turn, carry):
        for piece in range(3):
            for tile in range(lane_tiles):
                begin = (piece * lane_tiles + tile) * capacity
                block = jnp.concatenate(
                    [
                        in_ref[turn * period + member, begin : begin + capacity, :]
                        for member in range(period)
                    ],
                    axis=0,
                )
                start = pl.multiple_of(
                    piece * count * capacity + turn * (period * capacity), GROUP
                )
                out_ref[
                    pl.ds(start, period * capacity), WIDE * tile : WIDE * (tile + 1)
                ] = block
        return carry

    lax.fori_loop(0, count // period, gather, 0)
    side = count * capacity
    two_ref[...] = out_ref[: 2 * side, :]
    one_ref[...] = out_ref[2 * side :, :]


def regrouped(chunks, capacity, width):
    side = chunks.shape[0] * capacity
    return pl.pallas_call(
        functools.partial(regroup_kernel, capacity),
        out_shape=tuple(
            jax.ShapeDtypeStruct((parts * side, width), jnp.float32) for parts in (3, 2, 1)
        ),
        in_specs=[VMEM_SPEC],
        out_specs=(VMEM_SPEC,) * 3,
        compiler_params=pltpu.CompilerParams(vmem_limit_bytes=16 << 20),
        name="regroup",
    )(chunks)


def full(value):
    return jnp.broadcast_to(value, (GROUP, TILE))


def half_factor(pair_ref, done_ref, start):
    groups = pair_ref.shape[0] // GROUP
    sub = lax.broadcasted_iota(jnp.int32, (GROUP, TILE), 0)
    rows = [pair_ref[GROUP * g : GROUP * (g + 1), :] for g in range(groups)]
    eight = range(GROUP)
    for p in range(groups):
        strip = rows[p]
        cols = [full(strip[:, GROUP * p + k : GROUP * p + k + 1]) for k in eight]
        m = [[full(cols[k][i : i + 1, :]) if k <= i else None for k in eight] for i in eight]
        r = [None] * GROUP
        u = [full(strip[j : j + 1, :]) for j in eight]
        for j in eight:
            r[j] = lax.rsqrt(m[j][j])
            for i in range(j + 1, GROUP):
                m[i][j] = m[i][j] * r[j]
            for k in range(j + 1, GROUP):
                for i in range(k, GROUP):
                    m[i][k] = m[i][k] - m[i][j] * m[k][j]
            u[j] = u[j] * r[j]
            for i in range(j + 1, GROUP):
                u[i] = u[i] - m[i][j] * u[j]
        joined = u[0]
        for j in range(1, GROUP):
            joined = jnp.where(sub == j, u[j], joined)
        done_ref[pl.ds(start + GROUP * p, GROUP), :] = joined
        for g in range(p + 1, groups):
            side = [full(rows[g][:, GROUP * p + k : GROUP * p + k + 1]) for k in eight]
            x = rows[g]
            for j in eight:
                side[j] = side[j] * r[j]
                for i in range(j + 1, GROUP):
                    side[i] = side[i] - m[i][j] * side[j]
                x = x - side[j] * u[j]
            rows[g] = x


def tile_factor(tile, pair_ref, done_ref, cross_ref, corner_ref):
    half = TILE // 2
    row = lax.broadcasted_iota(jnp.int32, (half, half), 0)
    col = lax.broadcasted_iota(jnp.int32, (half, half), 1)
    unit = jnp.where(row == col, 1.0, 0.0).astype(jnp.float32)
    zero = jnp.zeros((half, half), jnp.float32)
    pair_ref[...] = jnp.concatenate([tile[:half, :half], unit], axis=1)
    cross_ref[...] = tile[:half, half:]
    corner_ref[...] = tile[half:, half:]

    def turn(number, carry):
        half_factor(pair_ref, done_ref, pl.multiple_of(number * half, half))

        @pl.when(number == 0)
        def _():
            cross = near_product(done_ref[:half, half:], cross_ref[...], NN)
            cross_ref[...] = cross
            both = halves(cross)
            rest = corner_ref[...] - product_of_halves(both, both, TN)
            pair_ref[...] = jnp.concatenate([rest, unit], axis=1)

        return carry

    lax.fori_loop(0, 2, turn, 0)
    first, second = done_ref[:half, half:], done_ref[half:, half:]
    middle = near_product(cross_ref[...], first, TN)
    upper = jnp.concatenate(
        [
            jnp.concatenate([done_ref[:half, :half], cross_ref[...]], axis=1),
            jnp.concatenate([zero, done_ref[half:, :half]], axis=1),
        ],
        axis=0,
    )
    inverse = jnp.concatenate(
        [
            jnp.concatenate([first, zero], axis=1),
            jnp.concatenate([-near_product(second, middle, NN), second], axis=1),
        ],
        axis=0,
    )
    return upper, inverse


def halves(value):
    high = value.astype(jnp.bfloat16)
    return high, (value - high.astype(jnp.float32)).astype(jnp.bfloat16)


def product_of_halves(left, right, dims):
    total = product(left[0], right[0], dims, lax.Precision.DEFAULT)
    total = total + product(left[0], right[1], dims, lax.Precision.DEFAULT)
    return total + product(left[1], right[0], dims, lax.Precision.DEFAULT)


def lanes_at(number):
    return pl.ds(pl.multiple_of(number * WIDE, WIDE), WIDE)


def tall_product(left_refs, rows, depth, right_at, put, width):
    left = tuple(ref[:rows, :depth] for ref in left_refs)

    def block(number, carry):
        put(lanes_at(number), product_of_halves(left, halves(right_at(lanes_at(number))), NN))
        return carry

    lax.fori_loop(0, width // WIDE, block, 0)


def keep_halves(left_refs, value):
    rows, depth = value.shape
    high, low = halves(value)
    left_refs[0][:rows, :depth] = high
    left_refs[1][:rows, :depth] = low


def piece_shapes(side, lanes):
    return tuple(
        jax.ShapeDtypeStruct(((stop - start) * side, lanes), jnp.float32) for start, stop in PIECES
    )


def part_kernel(side, bounds, number, *refs):
    first, last = bounds[number], bounds[number + 1]
    final = number == len(bounds) - 2
    x_ref, start_ref = refs[:2]
    before = refs[2 : 2 + 2 * number]
    refs = refs[2 + 2 * number :]
    low_ref, outs = refs[0], refs[1:5]
    gram_refs, refs = (refs[5:7], refs[7:]) if final else ((), refs[5:])
    small_refs, refs = refs[:4], refs[4:]
    low_high_ref, low_less_ref, y_high_ref, y_less_ref = refs[:4]
    depth, width = x_ref.shape
    begin, end = first * TILE, last * TILE
    reach = end - TILE
    row = lax.broadcasted_iota(jnp.int32, (TILE, TILE), 0)
    col = lax.broadcasted_iota(jnp.int32, (TILE, TILE), 1)

    if number == 0:
        turned = refs[4:6]
        keep_halves(turned, x_ref[...].T)

        def gram(lanes, value):
            low_ref[:, lanes] = value

        tall_product(turned, width, depth, lambda lanes: x_ref[:, lanes], gram, width)
        for i in range(width // TILE):
            rows = slice(i * TILE, (i + 1) * TILE)
            low_ref[rows, rows] = low_ref[rows, rows] + jnp.where(
                row == col, jnp.broadcast_to(start_ref[:, rows], (TILE, TILE)), 0.0
            )
    else:
        low_ref[...] = start_ref[...]
        high, less = halves(start_ref[:, :begin])
        low_high_ref[:, :begin] = high
        low_less_ref[:, :begin] = less
        for k in range(number):
            lanes = slice(bounds[k] * TILE, bounds[k + 1] * TILE)
            for ref, rows in ((before[2 * k], slice(0, 2 * side)), (before[2 * k + 1], slice(2 * side, 3 * side))):
                high, less = halves(ref[...])
                y_high_ref[rows, lanes] = high
                y_less_ref[rows, lanes] = less
    for ref in (low_high_ref, low_less_ref):
        ref[:, begin:] = jnp.zeros((width, end - begin), jnp.bfloat16)
    for ref in (y_high_ref, y_less_ref):
        ref[:, begin:] = jnp.zeros((depth, end - begin), jnp.bfloat16)

    def step(j, carry):
        start = pl.multiple_of(j * TILE, TILE)
        cols = pl.ds(start, TILE)
        local = pl.ds(pl.multiple_of((j - first) * TILE, TILE), TILE)

        def reduced(value, high_ref, less_ref, rows):
            if reach == 0:
                return value
            return value - product_of_halves(
                (high_ref[rows, :reach], less_ref[rows, :reach]),
                (low_high_ref[cols, :reach], low_less_ref[cols, :reach]),
                NT,
            )

        tile = reduced(low_ref[cols, cols], low_high_ref, low_less_ref, cols)
        upper, inverse = tile_factor(tile, *small_refs)
        inverse = halves(inverse)
        for i in range(depth // side):
            rows = slice(i * side, (i + 1) * side)
            value = reduced(x_ref[rows, cols], y_high_ref, y_less_ref, rows)
            value = product_of_halves(halves(value), inverse, NT)
            for out_ref, (head, tail) in zip(outs, PIECES):
                if head <= i < tail:
                    out_ref[(i - head) * side : (i - head + 1) * side, local] = value
            high, less = halves(value)
            y_high_ref[rows, cols] = high
            y_less_ref[rows, cols] = less
        for i in range(first * TILE // WIDE, width // WIDE):
            rows = slice(i * WIDE, (i + 1) * WIDE)
            value = reduced(low_ref[rows, cols], low_high_ref, low_less_ref, rows)
            value = product_of_halves(halves(value), inverse, NT)
            place = lax.broadcasted_iota(jnp.int32, (WIDE, TILE), 0) + i * WIDE
            value = jnp.where(place >= start + TILE, value, 0.0)
            low_ref[rows, cols] = value
            high, less = halves(value)
            low_high_ref[rows, cols] = high
            low_less_ref[rows, cols] = less
        low_ref[cols, cols] = jnp.where(col <= row, upper.T, 0.0)
        return carry

    lax.fori_loop(first, last, step, 0)
    if number > 0:
        for i in range(first * TILE // WIDE):
            rows = slice(i * WIDE, (i + 1) * WIDE)
            low_ref[rows, begin:end] = jnp.zeros((WIDE, end - begin), jnp.float32)
    if final:
        for gram_ref, left, right in (
            (gram_refs[0], slice(2 * side, 3 * side), slice(0, 2 * side)),
            (gram_refs[1], slice(side, 2 * side), slice(0, side)),
        ):
            gram_ref[...] = product_of_halves(
                (y_high_ref[left, :], y_less_ref[left, :]),
                (y_high_ref[right, :], y_less_ref[right, :]),
                NT,
            )


def factored_part(x, start, before, side, bounds, number):
    depth, width = x.shape
    first, last = bounds[number], bounds[number + 1]
    final = number == len(bounds) - 2
    end = last * TILE
    shapes = [jax.ShapeDtypeStruct((width, width), jnp.float32)]
    shapes += piece_shapes(side, (last - first) * TILE)
    if final:
        shapes += [
            jax.ShapeDtypeStruct((side, 2 * side), jnp.float32),
            jax.ShapeDtypeStruct((side, side), jnp.float32),
        ]
    half = TILE // 2
    scratch = [pltpu.VMEM((half, TILE), jnp.float32), pltpu.VMEM((TILE, TILE), jnp.float32)]
    scratch += [pltpu.VMEM((half, half), jnp.float32)] * 2
    scratch += [pltpu.VMEM((width, end), jnp.bfloat16)] * 2
    scratch += [pltpu.VMEM((depth, end), jnp.bfloat16)] * 2
    if number == 0:
        scratch += [pltpu.VMEM((width, depth), jnp.bfloat16)] * 2
    return pl.pallas_call(
        functools.partial(part_kernel, side, bounds, number),
        out_shape=tuple(shapes),
        in_specs=[VMEM_SPEC] * (2 + len(before)),
        out_specs=(VMEM_SPEC,) * len(shapes),
        scratch_shapes=scratch,
        compiler_params=pltpu.CompilerParams(vmem_limit_bytes=24 << 20),
        cost_estimate=pl.CostEstimate(
            flops=20_000_000_000, bytes_accessed=3 * depth * width * 4, transcendentals=0
        ),
        name="factor_part",
    )(x, start, *before)


def near_product(left, right, dims):
    return product_of_halves(halves(left), halves(right), dims)


COUPLINGS = ((3, 0, 1), (1, 0, 2), (0, 1, 3), (2, 2, 3))


def put_coupling(side, start, y_refs, x_ref, buffer_ref, left_refs, out_ref, sems, places=range(4)):
    rows = buffer_ref.shape[1]
    width = x_ref.shape[1]
    copies = []
    for place in places:
        number, begin, end = COUPLINGS[place]
        keep_halves(left_refs, y_refs[number][...].T)

        def put(lanes, value, place=place):
            buffer_ref[place, :, lanes] = value

        tall_product(
            left_refs,
            rows,
            (end - begin) * side,
            lambda lanes, begin=begin, end=end: x_ref[begin * side : end * side, lanes],
            put,
            width,
        )
        copy = pltpu.make_async_copy(
            buffer_ref.at[place], out_ref.at[place, pl.ds(start, rows), :], sems.at[place]
        )
        copy.start()
        copies.append(copy)
    return copies


def early_kernel(side, starts, x_ref, *refs):
    parts = len(starts)
    y_refs, refs = refs[: 4 * parts], refs[4 * parts :]
    out_ref, refs = refs[0], refs[1:]
    buffers, (high_ref, less_ref, sems) = refs[:parts], refs[parts:]
    copies = []
    for number, start in enumerate(starts):
        copies += put_coupling(
            side,
            start,
            y_refs[4 * number : 4 * number + 4],
            x_ref,
            buffers[number],
            (high_ref, less_ref),
            out_ref,
            sems.at[number],
        )
    for copy in copies:
        copy.wait()


def early(x, parts, starts, side):
    width = x.shape[1]
    heights = [part[0].shape[1] for part in parts]
    most = max(heights)
    return pl.pallas_call(
        functools.partial(early_kernel, side, starts),
        out_shape=jax.ShapeDtypeStruct((4, width, width), jnp.float32),
        in_specs=[VMEM_SPEC] * (1 + 4 * len(parts)),
        out_specs=ANY_SPEC,
        scratch_shapes=[pltpu.VMEM((4, height, width), jnp.float32) for height in heights]
        + [
            pltpu.VMEM((most, 2 * side), jnp.bfloat16),
            pltpu.VMEM((most, 2 * side), jnp.bfloat16),
            pltpu.SemaphoreType.DMA((len(parts), 4)),
        ],
        compiler_params=pltpu.CompilerParams(vmem_limit_bytes=24 << 20),
        cost_estimate=pl.CostEstimate(
            flops=8_000_000_000, bytes_accessed=4 * width * width * 4, transcendentals=0
        ),
        name="early",
    )(x, *[piece for part in parts for piece in part])


def base_kernel(side, cut, flags_ref, *refs):
    (
        x_ref,
        shift_ref,
        direct_ref,
        onward_ref,
        second_ref,
        extra_ref,
        low_ref,
        gram_one_ref,
        gram_two_ref,
    ) = refs[:9]
    refs = refs[9:]
    mine, refs = refs[:PARTS], refs[PARTS:]
    pieces, refs = [refs[4 * k : 4 * k + 4] for k in range(PARTS - 1)], refs[4 * PARTS - 4 :]
    partial_ref, schur_ref = refs[:2]
    tile_ref, rest_ref, near_ref, far_ref, high_ref, less_ref, outs = refs[2:]
    left_refs = (high_ref, less_ref)
    width = x_ref.shape[1]
    copies = []
    own, above, second_above, under, second_under = [flags_ref[k] > 0 for k in range(5)]
    one, two, three = slice(0, side), slice(side, 2 * side), slice(2 * side, 3 * side)
    pair, tail = slice(0, 2 * side), slice(side, 3 * side)
    rest_ref[...] = x_ref[...]
    near_ref[three, :] = jnp.zeros((side, width), jnp.float32)
    far_ref[two, :] = jnp.zeros((side, width), jnp.float32)

    @pl.when(own)
    def _():
        start = 0
        for ref in mine:
            lanes = slice(start, start + ref.shape[1])
            near_ref[pair, lanes] = ref[...]
            far_ref[one, lanes] = ref[side:, :]
            start += ref.shape[1]

    @pl.when(jnp.logical_not(own))
    def _():
        near_ref[pair, :] = x_ref[tail, :]
        far_ref[one, :] = x_ref[three, :]

    def weighed(number, rows):
        gram = 0.0
        for part in pieces:
            both = halves(part[number][...])
            gram = gram + product_of_halves(both, both, NT)
        return near_product(gram, x_ref[rows, :], NN)

    @pl.when(second_above)
    def _():
        rest_ref[one, :] = rest_ref[one, :] - weighed(3, one)

    @pl.when(above)
    def _():
        term = weighed(1, pair)
        rest_ref[pair, :] = rest_ref[pair, :] - term
        near_ref[one, :] = near_ref[one, :] - term[side:]

    @pl.when(under)
    def _():
        term = weighed(0, tail)
        rest_ref[tail, :] = rest_ref[tail, :] - term
        far_ref[one, :] = far_ref[one, :] - term[side:]
        far_ref[two, :] = -near_product(gram_one_ref[...], x_ref[tail, :], NN)

    @pl.when(second_under)
    def _():
        term = weighed(2, three)
        rest_ref[three, :] = rest_ref[three, :] - term
        near_ref[two, :] = near_ref[two, :] - term
        near_ref[three, :] = -near_product(gram_two_ref[...], x_ref[three, :], NN)

    def put(place):
        copy = pltpu.make_async_copy(tile_ref.at[place], schur_ref.at[place], outs.at[place])
        copy.start()
        return copy

    def fill(place, left, right_ref):
        keep_halves(left_refs, left.T)

        def put(lanes, value):
            tile_ref[place, :, lanes] = value

        tall_product(
            left_refs, width, left.shape[0], lambda lanes: right_ref[:, lanes], put, width
        )

    def from_coupling(place, member):
        copy = pltpu.make_async_copy(
            partial_ref.at[member, pl.ds(0, cut), :],
            tile_ref.at[place, pl.ds(0, cut), :],
            outs.at[place],
        )
        copy.start()
        tile_ref[place, cut:, :] = jnp.zeros((width - cut, width), jnp.float32)
        copy.wait()

    @pl.when(own)
    def _():
        tile_ref[2] = low_ref[...]

    @pl.when(jnp.logical_not(own))
    def _():
        fill(2, x_ref[...], rest_ref)
        for i in range(width // TILE):
            rows = slice(i * TILE, (i + 1) * TILE)
            row = lax.broadcasted_iota(jnp.int32, (TILE, TILE), 0)
            col = lax.broadcasted_iota(jnp.int32, (TILE, TILE), 1)
            tile_ref[2, rows, rows] = tile_ref[2, rows, rows] + jnp.where(
                row == col, jnp.broadcast_to(shift_ref[:, rows], (TILE, TILE)), 0.0
            )

    copies.append(put(2))

    @pl.when(under)
    def _():
        from_coupling(1, 2)

    @pl.when(jnp.logical_not(under))
    def _():
        below = direct_ref[...] + onward_ref[...]
        fill(1, jnp.concatenate([below, extra_ref[...]], axis=0), near_ref)

    copies.append(put(1))

    @pl.when(second_under)
    def _():
        from_coupling(0, 3)

    @pl.when(jnp.logical_not(second_under))
    def _():
        fill(0, second_ref[...], far_ref)

    copies.append(put(0))
    for copy in copies:
        copy.wait()


def base(flags, x, shift, received, low, grams, mine, parts, partial, cut, side):
    depth, width = x.shape
    inputs = [x, shift, *received, low, *grams, *mine] + [piece for part in parts for piece in part]
    return pl.pallas_call(
        functools.partial(base_kernel, side, cut),
        out_shape=jax.ShapeDtypeStruct((3, width, width), jnp.float32),
        in_specs=[SMEM_SPEC] + [VMEM_SPEC] * len(inputs) + [ANY_SPEC],
        out_specs=ANY_SPEC,
        scratch_shapes=[
            pltpu.VMEM((3, width, width), jnp.float32),
            pltpu.VMEM((depth, width), jnp.float32),
            pltpu.VMEM((depth, width), jnp.float32),
            pltpu.VMEM((2 * side, width), jnp.float32),
            pltpu.VMEM((width, depth), jnp.bfloat16),
            pltpu.VMEM((width, depth), jnp.bfloat16),
            pltpu.SemaphoreType.DMA((3,)),
        ],
        compiler_params=pltpu.CompilerParams(vmem_limit_bytes=36 << 20),
        cost_estimate=pl.CostEstimate(
            flops=12_000_000_000, bytes_accessed=7 * width * width * 4, transcendentals=0
        ),
        name="base",
    )(flags, *inputs, partial)


def late_kernel(side, flags_ref, x_ref, direct_ref, onward_ref, second_ref, *refs):
    y_refs, refs = refs[:4], refs[4:]
    tiles_ref, _, schur_ref, coupling_ref = refs[:4]
    buffer_ref, tile_ref, high_ref, less_ref, small_ref, sems, ins, outs, edges = refs[4:]
    left_refs = (high_ref, less_ref)
    rows, width = buffer_ref.shape[1:]
    above, second_above, under, second_under = [flags_ref[k] > 0 for k in range(1, 5)]
    beside = jnp.logical_or(above, second_under)
    touched = jnp.logical_or(jnp.logical_or(beside, under), second_above)

    def taken(place, slot):
        return pltpu.make_async_copy(tiles_ref.at[place], tile_ref.at[slot], ins.at[slot])

    def given(place, slot):
        return pltpu.make_async_copy(tile_ref.at[slot], schur_ref.at[place], outs.at[slot])

    moves = ((touched, 2, 0), (beside, 1, 1), (under, 0, 1))
    for wanted, place, slot in moves:

        @pl.when(wanted)
        def _(place=place, slot=slot):
            taken(place, slot).start()

    copies = put_coupling(
        side, width - rows, y_refs, x_ref, buffer_ref, left_refs, coupling_ref, sems, (0, 3, 2, 1)
    )

    def edge(place, member):
        return pltpu.make_async_copy(
            buffer_ref.at[member], schur_ref.at[place, pl.ds(width - rows, rows), :], edges.at[place]
        )

    replaced = ((under, 1, 2), (second_under, 0, 3))
    for wanted, place, member in replaced:

        @pl.when(wanted)
        def _(place=place, member=member):
            edge(place, member).start()

    for wanted, place, slot in moves:

        @pl.when(wanted)
        def _(place=place, slot=slot):
            taken(place, slot).wait()

    def take_off(slot, depth, right_at):
        def put(lanes, value):
            tile_ref[slot, :, lanes] = tile_ref[slot, :, lanes] - value

        tall_product(left_refs, width, depth, right_at, put, width)

    for wanted, place in ((second_above, 0), (above, 1), (under, 2), (second_under, 3)):

        @pl.when(wanted)
        def _(place=place):
            keep_halves(left_refs, buffer_ref[place].T)
            take_off(0, rows, lambda lanes: buffer_ref[place, :, lanes])

    def put_small(lanes, value):
        small_ref[:, lanes] = value

    pair_sum = ((above, 1, y_refs[1], 1, 0), (second_under, 3, y_refs[2], 0, 1))
    for wanted, place, y_ref, row, piece in pair_sum + ((under, 2, y_refs[0], 1, None),):

        @pl.when(wanted)
        def _(place=place, y_ref=y_ref, row=row, piece=piece):
            keep_halves(left_refs, y_ref[row * side : (row + 1) * side, :])
            tall_product(
                left_refs, side, rows, lambda lanes: buffer_ref[place, :, lanes], put_small, width
            )
            if piece is None:
                left = second_ref[:side, :]
            else:
                picked = slice(piece * side, (piece + 1) * side)
                left = direct_ref[picked, :] + onward_ref[picked, :]
            keep_halves(left_refs, left.T)
            take_off(1, side, lambda lanes: small_ref[:, lanes])

    for wanted, place, slot in moves:

        @pl.when(wanted)
        def _(place=place, slot=slot):
            given(place, slot).start()

    for wanted, place, slot in moves:

        @pl.when(wanted)
        def _(place=place, slot=slot):
            given(place, slot).wait()

    for wanted, place, member in replaced:

        @pl.when(wanted)
        def _(place=place, member=member):
            edge(place, member).wait()

    for copy in copies:
        copy.wait()


def late(flags, x, direct, onward, second, pieces, tiles, coupling, side):
    _, width = x.shape
    rows = pieces[0].shape[1]
    most = max(2 * side, rows)
    return pl.pallas_call(
        functools.partial(late_kernel, side),
        out_shape=(
            jax.ShapeDtypeStruct((3, width, width), jnp.float32),
            jax.ShapeDtypeStruct((4, width, width), jnp.float32),
        ),
        in_specs=[SMEM_SPEC] + [VMEM_SPEC] * 8 + [ANY_SPEC] * 2,
        out_specs=(ANY_SPEC, ANY_SPEC),
        input_output_aliases={9: 0, 10: 1},
        scratch_shapes=[
            pltpu.VMEM((4, rows, width), jnp.float32),
            pltpu.VMEM((2, width, width), jnp.float32),
            pltpu.VMEM((width, most), jnp.bfloat16),
            pltpu.VMEM((width, most), jnp.bfloat16),
            pltpu.VMEM((side, width), jnp.float32),
            pltpu.SemaphoreType.DMA((4,)),
            pltpu.SemaphoreType.DMA((2,)),
            pltpu.SemaphoreType.DMA((2,)),
            pltpu.SemaphoreType.DMA((2,)),
        ],
        compiler_params=pltpu.CompilerParams(vmem_limit_bytes=24 << 20),
        cost_estimate=pl.CostEstimate(
            flops=4_000_000_000, bytes_accessed=4 * width * width * 4, transcendentals=0
        ),
        name="late",
    )(flags, x, direct, onward, second, *pieces, tiles, coupling)


def local(weighted_jacobian_strips, leading_pose_index, levenberg_shift, removal_flags):
    count = lax.axis_size(AXES)
    own = lax.axis_index(AXES)
    surfels, _, width = weighted_jacobian_strips.shape
    capacity = max(2, (3 * surfels + 2 * count - 1) // (2 * count))
    side = count * capacity
    count_tiles = width // TILE
    bounds = tuple(count_tiles * k // PARTS for k in range(PARTS + 1))
    starts = tuple(bound * TILE for bound in bounds[:-1])
    flags = removal_flags[(own + jnp.array((0, 1, 2, -1, -2), jnp.int32)) % count]

    chunks = bucketed(
        leading_pose_index.reshape(1, surfels),
        weighted_jacobian_strips.transpose(1, 0, 2),
        count,
        capacity,
    )
    chunks = lax.all_to_all(chunks, AXES, split_axis=0, concat_axis=0, tiled=True)
    x, two, last = regrouped(chunks, capacity, width)

    def sent_parts(parts):
        return [passed_along(part, steps) for part, steps in zip(parts, (1, -1, 2, -2))]

    direct = lax.ppermute(two, AXES, [(k, k + 1) for k in range(0, count, 2)])
    second = passed_along(two, 2)

    def solved(number, start, known):
        before = [part[k] for part in known for k in (0, 3)]
        return factored_part(x, start, before, side, bounds, number)

    low, *part = solved(0, levenberg_shift, ())
    known = [part]
    parts = [sent_parts(part)]
    onward = lax.ppermute(second, AXES, [(k + 1, k) for k in range(0, count, 2)])
    extra = passed_along(last, 1)
    for number in range(1, PARTS - 1):
        low, *part = solved(number, low, known)
        known.append(part)
        parts.append(sent_parts(part))
    low, *part, gram_one, gram_two = solved(PARTS - 1, low, known)
    known.append(part)
    parts.append(sent_parts(part))
    grams = (passed_along(gram_one, 1), passed_along(gram_two, 2))
    partial = early(x, parts[:-1], starts[:-1], side)
    tiles = base(
        flags,
        x,
        levenberg_shift,
        (direct, onward, second, extra),
        low,
        grams,
        [part[1] for part in known],
        parts[:-1],
        partial,
        starts[-1],
        side,
    )
    schur, coupling = late(flags, x, direct, onward, second, parts[-1], tiles, partial, side)
    return schur[None], coupling[None]


def solution(mesh):
    in_specs = (P(AXES, None, None), P(AXES, None), P(AXES, None), P())
    out_specs = (P(AXES, None, None, None), P(AXES, None, None, None))

    return jax.shard_map(local, mesh=mesh, in_specs=in_specs, out_specs=out_specs, check_vma=False)
```

```python
import functools
import math

import jax
import jax.numpy as jnp
from jax import lax
from jax.experimental import pallas as pl
from jax.experimental.pallas import tpu as pltpu
from jax.sharding import PartitionSpec as P


AXES = ("gx", "gy")
TILE = 128
GROUP = 8
WIDE = 256
PARTS = 3
NT = (((1,), (1,)), ((), ()))
TN = (((0,), (0,)), ((), ()))
NN = (((1,), (0,)), ((), ()))
VMEM_SPEC = pl.BlockSpec(memory_space=pltpu.VMEM)
SMEM_SPEC = pl.BlockSpec(memory_space=pltpu.SMEM)
ANY_SPEC = pl.BlockSpec(memory_space=pl.ANY)
PIECES = ((0, 2), (1, 3), (0, 1), (2, 3))


def passed_along(value, steps):
    count = lax.axis_size(AXES)
    pairs = [(source, (source + steps) % count) for source in range(count)]
    return lax.ppermute(value, AXES, pairs)


def product(left, right, dims, precision=lax.Precision.HIGHEST):
    return lax.dot_general(
        left, right, dims, precision=precision, preferred_element_type=jnp.float32
    )


def bucket_kernel(count, capacity, index_ref, strips_ref, out_ref, rows_ref):
    surfels = strips_ref.shape[1]
    width = strips_ref.shape[2]
    lane_tiles = width // WIDE
    index = index_ref[...]
    base = lax.broadcasted_iota(jnp.int32, (count, surfels), 0)
    hot = (base == index).astype(jnp.float32)
    first = lax.broadcasted_iota(jnp.int32, (surfels, surfels), 0)
    second = lax.broadcasted_iota(jnp.int32, (surfels, surfels), 1)
    ahead = (first < second).astype(jnp.float32)
    earlier = product(hot, ahead, NN)
    within = jnp.sum(earlier * hot, axis=0, keepdims=True).astype(jnp.int32)
    period = GROUP // math.gcd(capacity, GROUP)
    for piece in range(3):
        moved = index + piece
        moved = jnp.where(moved >= count, moved - count, moved)
        slot = moved * capacity + within
        row = lax.broadcasted_iota(jnp.int32, (count * capacity, surfels), 0)
        pick = (row == slot).astype(jnp.bfloat16)
        values = strips_ref[piece]
        high = values.astype(jnp.bfloat16)
        rest = values - high.astype(jnp.float32)
        middle = rest.astype(jnp.bfloat16)
        low = (rest - middle.astype(jnp.float32)).astype(jnp.bfloat16)
        rows_ref[...] = product(
            jnp.concatenate([pick, pick, pick], axis=1),
            jnp.concatenate([high, middle, low], axis=0),
            NN,
            lax.Precision.DEFAULT,
        )

        def spread(turn, carry, piece=piece):
            start = pl.multiple_of(turn * (period * capacity), GROUP)
            for tile in range(lane_tiles):
                block = rows_ref[pl.ds(start, period * capacity), WIDE * tile : WIDE * (tile + 1)]
                for member in range(period):
                    begin = (piece * lane_tiles + tile) * capacity
                    out_ref[turn * period + member, begin : begin + capacity, :] = block[
                        member * capacity : (member + 1) * capacity
                    ]
            return carry

        lax.fori_loop(0, count // period, spread, 0)


def bucketed(index_row, strips, count, capacity):
    width = strips.shape[2]
    return pl.pallas_call(
        functools.partial(bucket_kernel, count, capacity),
        out_shape=jax.ShapeDtypeStruct(
            (count, 3 * (width // WIDE) * capacity, WIDE), jnp.float32
        ),
        in_specs=[VMEM_SPEC, VMEM_SPEC],
        out_specs=VMEM_SPEC,
        scratch_shapes=[pltpu.VMEM((count * capacity, width), jnp.float32)],
        name="bucket",
    )(index_row, strips)


def regroup_kernel(capacity, in_ref, out_ref, two_ref, one_ref):
    count = in_ref.shape[0]
    width = out_ref.shape[1]
    lane_tiles = width // WIDE
    period = GROUP // math.gcd(capacity, GROUP)

    def gather(turn, carry):
        for piece in range(3):
            for tile in range(lane_tiles):
                begin = (piece * lane_tiles + tile) * capacity
                block = jnp.concatenate(
                    [
                        in_ref[turn * period + member, begin : begin + capacity, :]
                        for member in range(period)
                    ],
                    axis=0,
                )
                start = pl.multiple_of(
                    piece * count * capacity + turn * (period * capacity), GROUP
                )
                out_ref[
                    pl.ds(start, period * capacity), WIDE * tile : WIDE * (tile + 1)
                ] = block
        return carry

    lax.fori_loop(0, count // period, gather, 0)
    side = count * capacity
    two_ref[...] = out_ref[: 2 * side, :]
    one_ref[...] = out_ref[2 * side :, :]


def regrouped(chunks, capacity, width):
    side = chunks.shape[0] * capacity
    return pl.pallas_call(
        functools.partial(regroup_kernel, capacity),
        out_shape=tuple(
            jax.ShapeDtypeStruct((parts * side, width), jnp.float32) for parts in (3, 2, 1)
        ),
        in_specs=[VMEM_SPEC],
        out_specs=(VMEM_SPEC,) * 3,
        compiler_params=pltpu.CompilerParams(vmem_limit_bytes=16 << 20),
        name="regroup",
    )(chunks)


def full(value):
    return jnp.broadcast_to(value, (GROUP, TILE))


def half_factor(pair_ref, done_ref, start):
    groups = pair_ref.shape[0] // GROUP
    sub = lax.broadcasted_iota(jnp.int32, (GROUP, TILE), 0)
    rows = [pair_ref[GROUP * g : GROUP * (g + 1), :] for g in range(groups)]
    eight = range(GROUP)
    for p in range(groups):
        strip = rows[p]
        cols = [full(strip[:, GROUP * p + k : GROUP * p + k + 1]) for k in eight]
        m = [[full(cols[k][i : i + 1, :]) if k <= i else None for k in eight] for i in eight]
        r = [None] * GROUP
        u = [full(strip[j : j + 1, :]) for j in eight]
        for j in eight:
            r[j] = lax.rsqrt(m[j][j])
            for i in range(j + 1, GROUP):
                m[i][j] = m[i][j] * r[j]
            for k in range(j + 1, GROUP):
                for i in range(k, GROUP):
                    m[i][k] = m[i][k] - m[i][j] * m[k][j]
            u[j] = u[j] * r[j]
            for i in range(j + 1, GROUP):
                u[i] = u[i] - m[i][j] * u[j]
        joined = u[0]
        for j in range(1, GROUP):
            joined = jnp.where(sub == j, u[j], joined)
        done_ref[pl.ds(start + GROUP * p, GROUP), :] = joined
        for g in range(p + 1, groups):
            side = [full(rows[g][:, GROUP * p + k : GROUP * p + k + 1]) for k in eight]
            x = rows[g]
            for j in eight:
                side[j] = side[j] * r[j]
                for i in range(j + 1, GROUP):
                    side[i] = side[i] - m[i][j] * side[j]
                x = x - side[j] * u[j]
            rows[g] = x


def tile_factor(tile, pair_ref, done_ref, cross_ref, corner_ref):
    half = TILE // 2
    row = lax.broadcasted_iota(jnp.int32, (half, half), 0)
    col = lax.broadcasted_iota(jnp.int32, (half, half), 1)
    unit = jnp.where(row == col, 1.0, 0.0).astype(jnp.float32)
    zero = jnp.zeros((half, half), jnp.float32)
    pair_ref[...] = jnp.concatenate([tile[:half, :half], unit], axis=1)
    cross_ref[...] = tile[:half, half:]
    corner_ref[...] = tile[half:, half:]

    def turn(number, carry):
        half_factor(pair_ref, done_ref, pl.multiple_of(number * half, half))

        @pl.when(number == 0)
        def _():
            cross = near_product(done_ref[:half, half:], cross_ref[...], NN)
            cross_ref[...] = cross
            both = halves(cross)
            rest = corner_ref[...] - product_of_halves(both, both, TN)
            pair_ref[...] = jnp.concatenate([rest, unit], axis=1)

        return carry

    lax.fori_loop(0, 2, turn, 0)
    first, second = done_ref[:half, half:], done_ref[half:, half:]
    middle = near_product(cross_ref[...], first, TN)
    upper = jnp.concatenate(
        [
            jnp.concatenate([done_ref[:half, :half], cross_ref[...]], axis=1),
            jnp.concatenate([zero, done_ref[half:, :half]], axis=1),
        ],
        axis=0,
    )
    inverse = jnp.concatenate(
        [
            jnp.concatenate([first, zero], axis=1),
            jnp.concatenate([-near_product(second, middle, NN), second], axis=1),
        ],
        axis=0,
    )
    return upper, inverse


def halves(value):
    high = value.astype(jnp.bfloat16)
    return high, (value - high.astype(jnp.float32)).astype(jnp.bfloat16)


def product_of_halves(left, right, dims):
    total = product(left[0], right[0], dims, lax.Precision.DEFAULT)
    total = total + product(left[0], right[1], dims, lax.Precision.DEFAULT)
    return total + product(left[1], right[0], dims, lax.Precision.DEFAULT)


def lanes_at(number):
    return pl.ds(pl.multiple_of(number * WIDE, WIDE), WIDE)


def tall_product(left_refs, rows, depth, right_at, put, width):
    left = tuple(ref[:rows, :depth] for ref in left_refs)

    def block(number, carry):
        put(lanes_at(number), product_of_halves(left, halves(right_at(lanes_at(number))), NN))
        return carry

    lax.fori_loop(0, width // WIDE, block, 0)


def keep_halves(left_refs, value):
    rows, depth = value.shape
    high, low = halves(value)
    left_refs[0][:rows, :depth] = high
    left_refs[1][:rows, :depth] = low


def piece_shapes(side, lanes):
    return tuple(
        jax.ShapeDtypeStruct(((stop - start) * side, lanes), jnp.float32) for start, stop in PIECES
    )


def part_kernel(side, bounds, number, *refs):
    first, last = bounds[number], bounds[number + 1]
    final = number == len(bounds) - 2
    x_ref, start_ref = refs[:2]
    before = refs[2 : 2 + 2 * number]
    refs = refs[2 + 2 * number :]
    low_ref, outs = refs[0], refs[1:5]
    gram_refs, refs = (refs[5:7], refs[7:]) if final else ((), refs[5:])
    small_refs, refs = refs[:4], refs[4:]
    low_high_ref, low_less_ref, y_high_ref, y_less_ref = refs[:4]
    depth, width = x_ref.shape
    begin, end = first * TILE, last * TILE
    reach = end - TILE
    row = lax.broadcasted_iota(jnp.int32, (TILE, TILE), 0)
    col = lax.broadcasted_iota(jnp.int32, (TILE, TILE), 1)

    if number == 0:
        turned = refs[4:6]
        keep_halves(turned, x_ref[...].T)

        def gram(lanes, value):
            low_ref[:, lanes] = value

        tall_product(turned, width, depth, lambda lanes: x_ref[:, lanes], gram, width)
        for i in range(width // TILE):
            rows = slice(i * TILE, (i + 1) * TILE)
            low_ref[rows, rows] = low_ref[rows, rows] + jnp.where(
                row == col, jnp.broadcast_to(start_ref[:, rows], (TILE, TILE)), 0.0
            )
    else:
        low_ref[...] = start_ref[...]
        high, less = halves(start_ref[:, :begin])
        low_high_ref[:, :begin] = high
        low_less_ref[:, :begin] = less
        for k in range(number):
            lanes = slice(bounds[k] * TILE, bounds[k + 1] * TILE)
            for ref, rows in ((before[2 * k], slice(0, 2 * side)), (before[2 * k + 1], slice(2 * side, 3 * side))):
                high, less = halves(ref[...])
                y_high_ref[rows, lanes] = high
                y_less_ref[rows, lanes] = less
    for ref in (low_high_ref, low_less_ref):
        ref[:, begin:] = jnp.zeros((width, end - begin), jnp.bfloat16)
    for ref in (y_high_ref, y_less_ref):
        ref[:, begin:] = jnp.zeros((depth, end - begin), jnp.bfloat16)

    def step(j, carry):
        start = pl.multiple_of(j * TILE, TILE)
        cols = pl.ds(start, TILE)
        local = pl.ds(pl.multiple_of((j - first) * TILE, TILE), TILE)

        def reduced(value, high_ref, less_ref, rows):
            if reach == 0:
                return value
            return value - product_of_halves(
                (high_ref[rows, :reach], less_ref[rows, :reach]),
                (low_high_ref[cols, :reach], low_less_ref[cols, :reach]),
                NT,
            )

        tile = reduced(low_ref[cols, cols], low_high_ref, low_less_ref, cols)
        upper, inverse = tile_factor(tile, *small_refs)
        inverse = halves(inverse)
        for i in range(depth // side):
            rows = slice(i * side, (i + 1) * side)
            value = reduced(x_ref[rows, cols], y_high_ref, y_less_ref, rows)
            value = product_of_halves(halves(value), inverse, NT)
            for out_ref, (head, tail) in zip(outs, PIECES):
                if head <= i < tail:
                    out_ref[(i - head) * side : (i - head + 1) * side, local] = value
            high, less = halves(value)
            y_high_ref[rows, cols] = high
            y_less_ref[rows, cols] = less
        for i in range(first * TILE // WIDE, width // WIDE):
            rows = slice(i * WIDE, (i + 1) * WIDE)
            value = reduced(low_ref[rows, cols], low_high_ref, low_less_ref, rows)
            value = product_of_halves(halves(value), inverse, NT)
            place = lax.broadcasted_iota(jnp.int32, (WIDE, TILE), 0) + i * WIDE
            value = jnp.where(place >= start + TILE, value, 0.0)
            low_ref[rows, cols] = value
            high, less = halves(value)
            low_high_ref[rows, cols] = high
            low_less_ref[rows, cols] = less
        low_ref[cols, cols] = jnp.where(col <= row, upper.T, 0.0)
        return carry

    lax.fori_loop(first, last, step, 0)
    if number > 0:
        for i in range(first * TILE // WIDE):
            rows = slice(i * WIDE, (i + 1) * WIDE)
            low_ref[rows, begin:end] = jnp.zeros((WIDE, end - begin), jnp.float32)
    if final:
        for gram_ref, left, right in (
            (gram_refs[0], slice(2 * side, 3 * side), slice(0, 2 * side)),
            (gram_refs[1], slice(side, 2 * side), slice(0, side)),
        ):
            gram_ref[...] = product_of_halves(
                (y_high_ref[left, :], y_less_ref[left, :]),
                (y_high_ref[right, :], y_less_ref[right, :]),
                NT,
            )


def factored_part(x, start, before, side, bounds, number):
    depth, width = x.shape
    first, last = bounds[number], bounds[number + 1]
    final = number == len(bounds) - 2
    end = last * TILE
    shapes = [jax.ShapeDtypeStruct((width, width), jnp.float32)]
    shapes += piece_shapes(side, (last - first) * TILE)
    if final:
        shapes += [
            jax.ShapeDtypeStruct((side, 2 * side), jnp.float32),
            jax.ShapeDtypeStruct((side, side), jnp.float32),
        ]
    half = TILE // 2
    scratch = [pltpu.VMEM((half, TILE), jnp.float32), pltpu.VMEM((TILE, TILE), jnp.float32)]
    scratch += [pltpu.VMEM((half, half), jnp.float32)] * 2
    scratch += [pltpu.VMEM((width, end), jnp.bfloat16)] * 2
    scratch += [pltpu.VMEM((depth, end), jnp.bfloat16)] * 2
    if number == 0:
        scratch += [pltpu.VMEM((width, depth), jnp.bfloat16)] * 2
    return pl.pallas_call(
        functools.partial(part_kernel, side, bounds, number),
        out_shape=tuple(shapes),
        in_specs=[VMEM_SPEC] * (2 + len(before)),
        out_specs=(VMEM_SPEC,) * len(shapes),
        scratch_shapes=scratch,
        compiler_params=pltpu.CompilerParams(vmem_limit_bytes=24 << 20),
        cost_estimate=pl.CostEstimate(
            flops=20_000_000_000, bytes_accessed=3 * depth * width * 4, transcendentals=0
        ),
        name="factor_part",
    )(x, start, *before)


def near_product(left, right, dims):
    return product_of_halves(halves(left), halves(right), dims)


def put_coupling(side, start, y_refs, x_ref, buffer_ref, left_refs, out_ref, sems):
    rows = buffer_ref.shape[1]
    width = x_ref.shape[1]
    copies = []
    for place, (number, begin, end) in enumerate(((3, 0, 1), (1, 0, 2), (0, 1, 3), (2, 2, 3))):
        keep_halves(left_refs, y_refs[number][...].T)

        def put(lanes, value, place=place):
            buffer_ref[place, :, lanes] = value

        tall_product(
            left_refs,
            rows,
            (end - begin) * side,
            lambda lanes, begin=begin, end=end: x_ref[begin * side : end * side, lanes],
            put,
            width,
        )
        copy = pltpu.make_async_copy(
            buffer_ref.at[place], out_ref.at[place, pl.ds(start, rows), :], sems.at[place]
        )
        copy.start()
        copies.append(copy)
    return copies


def early_kernel(side, starts, x_ref, *refs):
    parts = len(starts)
    y_refs, refs = refs[: 4 * parts], refs[4 * parts :]
    out_ref, refs = refs[0], refs[1:]
    buffers, (high_ref, less_ref, sems) = refs[:parts], refs[parts:]
    copies = []
    for number, start in enumerate(starts):
        copies += put_coupling(
            side,
            start,
            y_refs[4 * number : 4 * number + 4],
            x_ref,
            buffers[number],
            (high_ref, less_ref),
            out_ref,
            sems.at[number],
        )
    for copy in copies:
        copy.wait()


def early(x, parts, starts, side):
    width = x.shape[1]
    heights = [part[0].shape[1] for part in parts]
    most = max(heights)
    return pl.pallas_call(
        functools.partial(early_kernel, side, starts),
        out_shape=jax.ShapeDtypeStruct((4, width, width), jnp.float32),
        in_specs=[VMEM_SPEC] * (1 + 4 * len(parts)),
        out_specs=ANY_SPEC,
        scratch_shapes=[pltpu.VMEM((4, height, width), jnp.float32) for height in heights]
        + [
            pltpu.VMEM((most, 2 * side), jnp.bfloat16),
            pltpu.VMEM((most, 2 * side), jnp.bfloat16),
            pltpu.SemaphoreType.DMA((len(parts), 4)),
        ],
        compiler_params=pltpu.CompilerParams(vmem_limit_bytes=24 << 20),
        cost_estimate=pl.CostEstimate(
            flops=8_000_000_000, bytes_accessed=4 * width * width * 4, transcendentals=0
        ),
        name="early",
    )(x, *[piece for part in parts for piece in part])


def late_kernel(side, starts, flags_ref, *refs):
    (
        x_ref,
        shift_ref,
        direct_ref,
        onward_ref,
        second_ref,
        extra_ref,
        low_ref,
        gram_one_ref,
        gram_two_ref,
    ) = refs[:9]
    parts = len(starts)
    refs = refs[9:]
    mine, refs = refs[:parts], refs[parts:]
    pieces, refs = [refs[4 * k : 4 * k + 4] for k in range(parts)], refs[4 * parts :]
    lasts = pieces[-1]
    partial_ref, schur_ref, coupling_ref = refs[:3]
    buffer_ref, tile_ref, rest_ref, near_ref, far_ref, high_ref, less_ref, sems, outs = refs[3:]
    left_refs = (high_ref, less_ref)
    width = x_ref.shape[1]
    cut = starts[-1]
    copies = put_coupling(side, cut, lasts, x_ref, buffer_ref, left_refs, coupling_ref, sems)
    own, above, second_above, under, second_under = [flags_ref[k] > 0 for k in range(5)]
    one, two, three = slice(0, side), slice(side, 2 * side), slice(2 * side, 3 * side)
    pair, tail = slice(0, 2 * side), slice(side, 3 * side)
    rest_ref[...] = x_ref[...]
    near_ref[three, :] = jnp.zeros((side, width), jnp.float32)
    far_ref[two, :] = jnp.zeros((side, width), jnp.float32)

    @pl.when(own)
    def _():
        for start, ref in zip(starts, mine):
            lanes = slice(start, start + ref.shape[1])
            near_ref[pair, lanes] = ref[...]
            far_ref[one, lanes] = ref[side:, :]

    @pl.when(jnp.logical_not(own))
    def _():
        near_ref[pair, :] = x_ref[tail, :]
        far_ref[one, :] = x_ref[three, :]

    def weighed(number, rows):
        gram = 0.0
        for part in pieces:
            both = halves(part[number][...])
            gram = gram + product_of_halves(both, both, NT)
        return near_product(gram, x_ref[rows, :], NN)

    @pl.when(second_above)
    def _():
        rest_ref[one, :] = rest_ref[one, :] - weighed(3, one)

    @pl.when(above)
    def _():
        term = weighed(1, pair)
        rest_ref[pair, :] = rest_ref[pair, :] - term
        near_ref[one, :] = near_ref[one, :] - term[side:]

    @pl.when(under)
    def _():
        term = weighed(0, tail)
        rest_ref[tail, :] = rest_ref[tail, :] - term
        far_ref[one, :] = far_ref[one, :] - term[side:]
        far_ref[two, :] = -near_product(gram_one_ref[...], x_ref[tail, :], NN)

    @pl.when(second_under)
    def _():
        term = weighed(2, three)
        rest_ref[three, :] = rest_ref[three, :] - term
        near_ref[two, :] = near_ref[two, :] - term
        near_ref[three, :] = -near_product(gram_two_ref[...], x_ref[three, :], NN)

    def put(place):
        copy = pltpu.make_async_copy(tile_ref.at[place], schur_ref.at[place], outs.at[place])
        copy.start()
        return copy

    def fill(place, left, right_ref):
        keep_halves(left_refs, left.T)

        def put(lanes, value):
            tile_ref[place, :, lanes] = value

        tall_product(
            left_refs, width, left.shape[0], lambda lanes: right_ref[:, lanes], put, width
        )

    def from_coupling(place, member):
        copy = pltpu.make_async_copy(
            partial_ref.at[member, pl.ds(0, cut), :],
            tile_ref.at[place, pl.ds(0, cut), :],
            outs.at[place],
        )
        copy.start()
        tile_ref[place, cut:, :] = buffer_ref[member]
        copy.wait()

    @pl.when(own)
    def _():
        tile_ref[2] = low_ref[...]

    @pl.when(jnp.logical_not(own))
    def _():
        fill(2, x_ref[...], rest_ref)
        for i in range(width // TILE):
            rows = slice(i * TILE, (i + 1) * TILE)
            row = lax.broadcasted_iota(jnp.int32, (TILE, TILE), 0)
            col = lax.broadcasted_iota(jnp.int32, (TILE, TILE), 1)
            tile_ref[2, rows, rows] = tile_ref[2, rows, rows] + jnp.where(
                row == col, jnp.broadcast_to(shift_ref[:, rows], (TILE, TILE)), 0.0
            )

    copies.append(put(2))

    @pl.when(under)
    def _():
        from_coupling(1, 2)

    @pl.when(jnp.logical_not(under))
    def _():
        below = direct_ref[...] + onward_ref[...]
        fill(1, jnp.concatenate([below, extra_ref[...]], axis=0), near_ref)

    copies.append(put(1))

    @pl.when(second_under)
    def _():
        from_coupling(0, 3)

    @pl.when(jnp.logical_not(second_under))
    def _():
        fill(0, second_ref[...], far_ref)

    copies.append(put(0))
    for copy in copies:
        copy.wait()


def late(flags, x, shift, received, low, grams, mine, parts, partial, starts, side):
    depth, width = x.shape
    rest = parts[-1][0].shape[1]
    inputs = [x, shift, *received, low, *grams, *mine] + [piece for part in parts for piece in part]
    return pl.pallas_call(
        functools.partial(late_kernel, side, starts),
        out_shape=(
            jax.ShapeDtypeStruct((3, width, width), jnp.float32),
            jax.ShapeDtypeStruct((4, width, width), jnp.float32),
        ),
        in_specs=[SMEM_SPEC] + [VMEM_SPEC] * len(inputs) + [ANY_SPEC],
        out_specs=(ANY_SPEC, ANY_SPEC),
        input_output_aliases={1 + len(inputs): 1},
        scratch_shapes=[
            pltpu.VMEM((4, rest, width), jnp.float32),
            pltpu.VMEM((3, width, width), jnp.float32),
            pltpu.VMEM((depth, width), jnp.float32),
            pltpu.VMEM((depth, width), jnp.float32),
            pltpu.VMEM((2 * side, width), jnp.float32),
            pltpu.VMEM((width, depth), jnp.bfloat16),
            pltpu.VMEM((width, depth), jnp.bfloat16),
            pltpu.SemaphoreType.DMA((4,)),
            pltpu.SemaphoreType.DMA((3,)),
        ],
        compiler_params=pltpu.CompilerParams(vmem_limit_bytes=40 << 20),
        cost_estimate=pl.CostEstimate(
            flops=12_000_000_000, bytes_accessed=7 * width * width * 4, transcendentals=0
        ),
        name="late",
    )(flags, *inputs, partial)


def relay_kernel(odd_ref, low_ref, high_ref, second_low_ref, second_high_ref, near_ref, far_ref):
    side = near_ref.shape[0]
    odd = odd_ref[0] > 0

    @pl.when(odd)
    def _():
        near_ref[...] = low_ref[side:, :]
        far_ref[...] = second_low_ref[...]

    @pl.when(jnp.logical_not(odd))
    def _():
        near_ref[...] = high_ref[:side, :]
        far_ref[...] = second_high_ref[...]


def join_kernel(odd_ref, low_ref, high_ref, near_ref, far_ref, low_out_ref, high_out_ref):
    side = near_ref.shape[0]
    odd = odd_ref[0] > 0

    @pl.when(odd)
    def _():
        low_out_ref[...] = low_ref[...]
        high_out_ref[:side, :] = near_ref[...]
        high_out_ref[side:, :] = far_ref[...]

    @pl.when(jnp.logical_not(odd))
    def _():
        low_out_ref[:side, :] = far_ref[...]
        low_out_ref[side:, :] = near_ref[...]
        high_out_ref[...] = high_ref[...]


def moved_about(kernel, odd, given, shapes):
    return pl.pallas_call(
        kernel,
        out_shape=tuple(jax.ShapeDtypeStruct(shape, jnp.float32) for shape in shapes),
        in_specs=[SMEM_SPEC] + [VMEM_SPEC] * len(given),
        out_specs=(VMEM_SPEC,) * len(shapes),
        compiler_params=pltpu.CompilerParams(vmem_limit_bytes=12 << 20),
    )(odd, *given)


def local(weighted_jacobian_strips, leading_pose_index, levenberg_shift, removal_flags):
    count = lax.axis_size(AXES)
    own = lax.axis_index(AXES)
    surfels, _, width = weighted_jacobian_strips.shape
    capacity = max(2, (3 * surfels + 2 * count - 1) // (2 * count))
    side = count * capacity
    tiles = width // TILE
    bounds = tuple(tiles * k // PARTS for k in range(PARTS + 1))
    starts = tuple(bound * TILE for bound in bounds[:-1])
    flags = removal_flags[(own + jnp.array((0, 1, 2, -1, -2), jnp.int32)) % count]

    chunks = bucketed(
        leading_pose_index.reshape(1, surfels),
        weighted_jacobian_strips.transpose(1, 0, 2),
        count,
        capacity,
    )
    chunks = lax.all_to_all(chunks, AXES, split_axis=0, concat_axis=0, tiled=True)
    x, two, last = regrouped(chunks, capacity, width)

    def sent_parts(parts):
        return [passed_along(part, steps) for part, steps in zip(parts, (1, -1, 2, -2))]

    direct = lax.ppermute(two, AXES, [(k, k + 1) for k in range(0, count, 2)])
    second = passed_along(two, 2)
    odd = (own % 2).astype(jnp.int32).reshape(1)
    evens = range(0, count, 2)
    swap = [(k, k ^ 1) for k in range(count)]
    onwards = [(k, (k + 2 - 4 * (k % 2)) % count) for k in range(count)]

    def paired(value, pairs):
        return lax.ppermute(value, AXES, pairs)

    def sent_short(part):
        return [
            paired(part[0], [(k, k + 1) for k in evens]),
            paired(part[1], [(k + 1, k) for k in evens]),
            passed_along(part[2], 2),
            passed_along(part[3], -2),
        ]

    def relayed(part):
        shape = part[2].shape
        near, far = moved_about(relay_kernel, odd, part, (shape, shape))
        return paired(near, onwards), paired(far, swap)

    def joined(part, more):
        low, high = moved_about(
            join_kernel, odd, (*part[:2], *more), (part[0].shape, part[1].shape)
        )
        return [low, high, *part[2:]]

    def solved(number, start, known):
        before = [part[k] for part in known for k in (0, 3)]
        return factored_part(x, start, before, side, bounds, number)

    extra = passed_along(last, 1)
    low, *part = solved(0, levenberg_shift, ())
    known = [part]
    parts = [sent_short(part)]
    more = []
    for number in range(1, PARTS):
        low, *part = solved(number, low, known)
        known.append(part[:4])
        if number < PARTS - 1:
            parts.append(sent_short(part))
        else:
            parts.append(sent_parts(part[:4]))
        more.append(relayed(parts[number - 1]))
    onward = paired(second, [(k + 1, k) for k in evens])
    gram_one, gram_two = part[4:]
    parts = [joined(parts[k], more[k]) for k in range(PARTS - 1)] + parts[-1:]
    grams = (passed_along(gram_one, 1), passed_along(gram_two, 2))
    partial = early(x, parts[:-1], starts[:-1], side)
    schur, coupling = late(
        flags,
        x,
        levenberg_shift,
        (direct, onward, second, extra),
        low,
        grams,
        [part[1] for part in known],
        parts,
        partial,
        starts,
        side,
    )
    return schur[None], coupling[None]


def solution(mesh):
    in_specs = (P(AXES, None, None), P(AXES, None), P(AXES, None), P())
    out_specs = (P(AXES, None, None, None), P(AXES, None, None, None))

    return jax.shard_map(local, mesh=mesh, in_specs=in_specs, out_specs=out_specs, check_vma=False)
```

```python
import functools
import math

import jax
import jax.numpy as jnp
from jax import lax
from jax.experimental import pallas as pl
from jax.experimental.pallas import tpu as pltpu
from jax.sharding import PartitionSpec as P


AXES = ("gx", "gy")
TILE = 128
GROUP = 8
WIDE = 256
PARTS = 3
NT = (((1,), (1,)), ((), ()))
TN = (((0,), (0,)), ((), ()))
NN = (((1,), (0,)), ((), ()))
VMEM_SPEC = pl.BlockSpec(memory_space=pltpu.VMEM)
SMEM_SPEC = pl.BlockSpec(memory_space=pltpu.SMEM)
ANY_SPEC = pl.BlockSpec(memory_space=pl.ANY)
PIECES = ((0, 2), (1, 3), (0, 1), (2, 3))


def passed_along(value, steps):
    count = lax.axis_size(AXES)
    pairs = [(source, (source + steps) % count) for source in range(count)]
    return lax.ppermute(value, AXES, pairs)


def product(left, right, dims, precision=lax.Precision.HIGHEST):
    return lax.dot_general(
        left, right, dims, precision=precision, preferred_element_type=jnp.float32
    )


def bucket_kernel(count, capacity, index_ref, strips_ref, out_ref, rows_ref):
    surfels = strips_ref.shape[1]
    width = strips_ref.shape[2]
    lane_tiles = width // WIDE
    index = index_ref[...]
    base = lax.broadcasted_iota(jnp.int32, (count, surfels), 0)
    hot = (base == index).astype(jnp.float32)
    first = lax.broadcasted_iota(jnp.int32, (surfels, surfels), 0)
    second = lax.broadcasted_iota(jnp.int32, (surfels, surfels), 1)
    ahead = (first < second).astype(jnp.float32)
    earlier = product(hot, ahead, NN)
    within = jnp.sum(earlier * hot, axis=0, keepdims=True).astype(jnp.int32)
    period = GROUP // math.gcd(capacity, GROUP)
    for piece in range(3):
        moved = index + piece
        moved = jnp.where(moved >= count, moved - count, moved)
        slot = moved * capacity + within
        row = lax.broadcasted_iota(jnp.int32, (count * capacity, surfels), 0)
        pick = (row == slot).astype(jnp.bfloat16)
        values = strips_ref[piece]
        high = values.astype(jnp.bfloat16)
        rest = values - high.astype(jnp.float32)
        middle = rest.astype(jnp.bfloat16)
        low = (rest - middle.astype(jnp.float32)).astype(jnp.bfloat16)
        rows_ref[...] = product(
            jnp.concatenate([pick, pick, pick], axis=1),
            jnp.concatenate([high, middle, low], axis=0),
            NN,
            lax.Precision.DEFAULT,
        )

        def spread(turn, carry, piece=piece):
            start = pl.multiple_of(turn * (period * capacity), GROUP)
            for tile in range(lane_tiles):
                block = rows_ref[pl.ds(start, period * capacity), WIDE * tile : WIDE * (tile + 1)]
                for member in range(period):
                    begin = (piece * lane_tiles + tile) * capacity
                    out_ref[turn * period + member, begin : begin + capacity, :] = block[
                        member * capacity : (member + 1) * capacity
                    ]
            return carry

        lax.fori_loop(0, count // period, spread, 0)


def bucketed(index_row, strips, count, capacity):
    width = strips.shape[2]
    return pl.pallas_call(
        functools.partial(bucket_kernel, count, capacity),
        out_shape=jax.ShapeDtypeStruct(
            (count, 3 * (width // WIDE) * capacity, WIDE), jnp.float32
        ),
        in_specs=[VMEM_SPEC, VMEM_SPEC],
        out_specs=VMEM_SPEC,
        scratch_shapes=[pltpu.VMEM((count * capacity, width), jnp.float32)],
        name="bucket",
    )(index_row, strips)


def regroup_kernel(capacity, in_ref, out_ref, two_ref, one_ref):
    count = in_ref.shape[0]
    width = out_ref.shape[1]
    lane_tiles = width // WIDE
    period = GROUP // math.gcd(capacity, GROUP)

    def gather(turn, carry):
        for piece in range(3):
            for tile in range(lane_tiles):
                begin = (piece * lane_tiles + tile) * capacity
                block = jnp.concatenate(
                    [
                        in_ref[turn * period + member, begin : begin + capacity, :]
                        for member in range(period)
                    ],
                    axis=0,
                )
                start = pl.multiple_of(
                    piece * count * capacity + turn * (period * capacity), GROUP
                )
                out_ref[
                    pl.ds(start, period * capacity), WIDE * tile : WIDE * (tile + 1)
                ] = block
        return carry

    lax.fori_loop(0, count // period, gather, 0)
    side = count * capacity
    two_ref[...] = out_ref[: 2 * side, :]
    one_ref[...] = out_ref[2 * side :, :]


def regrouped(chunks, capacity, width):
    side = chunks.shape[0] * capacity
    return pl.pallas_call(
        functools.partial(regroup_kernel, capacity),
        out_shape=tuple(
            jax.ShapeDtypeStruct((parts * side, width), jnp.float32) for parts in (3, 2, 1)
        ),
        in_specs=[VMEM_SPEC],
        out_specs=(VMEM_SPEC,) * 3,
        compiler_params=pltpu.CompilerParams(vmem_limit_bytes=16 << 20),
        name="regroup",
    )(chunks)


def full(value):
    return jnp.broadcast_to(value, (GROUP, TILE))


def half_factor(pair_ref, done_ref, start):
    groups = pair_ref.shape[0] // GROUP
    sub = lax.broadcasted_iota(jnp.int32, (GROUP, TILE), 0)
    rows = [pair_ref[GROUP * g : GROUP * (g + 1), :] for g in range(groups)]
    eight = range(GROUP)
    for p in range(groups):
        strip = rows[p]
        cols = [full(strip[:, GROUP * p + k : GROUP * p + k + 1]) for k in eight]
        m = [[full(cols[k][i : i + 1, :]) if k <= i else None for k in eight] for i in eight]
        r = [None] * GROUP
        u = [full(strip[j : j + 1, :]) for j in eight]
        for j in eight:
            r[j] = lax.rsqrt(m[j][j])
            for i in range(j + 1, GROUP):
                m[i][j] = m[i][j] * r[j]
            for k in range(j + 1, GROUP):
                for i in range(k, GROUP):
                    m[i][k] = m[i][k] - m[i][j] * m[k][j]
            u[j] = u[j] * r[j]
            for i in range(j + 1, GROUP):
                u[i] = u[i] - m[i][j] * u[j]
        joined = u[0]
        for j in range(1, GROUP):
            joined = jnp.where(sub == j, u[j], joined)
        done_ref[pl.ds(start + GROUP * p, GROUP), :] = joined
        for g in range(p + 1, groups):
            side = [full(rows[g][:, GROUP * p + k : GROUP * p + k + 1]) for k in eight]
            x = rows[g]
            for j in eight:
                side[j] = side[j] * r[j]
                for i in range(j + 1, GROUP):
                    side[i] = side[i] - m[i][j] * side[j]
                x = x - side[j] * u[j]
            rows[g] = x


def tile_factor(tile, pair_ref, done_ref, cross_ref, corner_ref):
    half = TILE // 2
    row = lax.broadcasted_iota(jnp.int32, (half, half), 0)
    col = lax.broadcasted_iota(jnp.int32, (half, half), 1)
    unit = jnp.where(row == col, 1.0, 0.0).astype(jnp.float32)
    zero = jnp.zeros((half, half), jnp.float32)
    pair_ref[...] = jnp.concatenate([tile[:half, :half], unit], axis=1)
    cross_ref[...] = tile[:half, half:]
    corner_ref[...] = tile[half:, half:]

    def turn(number, carry):
        half_factor(pair_ref, done_ref, pl.multiple_of(number * half, half))

        @pl.when(number == 0)
        def _():
            cross = near_product(done_ref[:half, half:], cross_ref[...], NN)
            cross_ref[...] = cross
            both = halves(cross)
            rest = corner_ref[...] - product_of_halves(both, both, TN)
            pair_ref[...] = jnp.concatenate([rest, unit], axis=1)

        return carry

    lax.fori_loop(0, 2, turn, 0)
    first, second = done_ref[:half, half:], done_ref[half:, half:]
    middle = near_product(cross_ref[...], first, TN)
    upper = jnp.concatenate(
        [
            jnp.concatenate([done_ref[:half, :half], cross_ref[...]], axis=1),
            jnp.concatenate([zero, done_ref[half:, :half]], axis=1),
        ],
        axis=0,
    )
    inverse = jnp.concatenate(
        [
            jnp.concatenate([first, zero], axis=1),
            jnp.concatenate([-near_product(second, middle, NN), second], axis=1),
        ],
        axis=0,
    )
    return upper, inverse


def halves(value):
    high = value.astype(jnp.bfloat16)
    return high, (value - high.astype(jnp.float32)).astype(jnp.bfloat16)


def product_of_halves(left, right, dims):
    total = product(left[0], right[0], dims, lax.Precision.DEFAULT)
    total = total + product(left[0], right[1], dims, lax.Precision.DEFAULT)
    return total + product(left[1], right[0], dims, lax.Precision.DEFAULT)


def lanes_at(number):
    return pl.ds(pl.multiple_of(number * WIDE, WIDE), WIDE)


def tall_product(left_refs, rows, depth, right_at, put, width):
    left = tuple(ref[:rows, :depth] for ref in left_refs)

    def block(number, carry):
        put(lanes_at(number), product_of_halves(left, halves(right_at(lanes_at(number))), NN))
        return carry

    lax.fori_loop(0, width // WIDE, block, 0)


def keep_halves(left_refs, value):
    rows, depth = value.shape
    high, low = halves(value)
    left_refs[0][:rows, :depth] = high
    left_refs[1][:rows, :depth] = low


def piece_shapes(side, lanes):
    return tuple(
        jax.ShapeDtypeStruct(((stop - start) * side, lanes), jnp.float32) for start, stop in PIECES
    )


def part_kernel(side, bounds, number, *refs):
    first, last = bounds[number], bounds[number + 1]
    final = number == len(bounds) - 2
    x_ref, start_ref = refs[:2]
    before = refs[2 : 2 + 2 * number]
    refs = refs[2 + 2 * number :]
    low_ref, outs = refs[0], refs[1:5]
    gram_refs, refs = (refs[5:7], refs[7:]) if final else ((), refs[5:])
    small_refs, refs = refs[:4], refs[4:]
    low_high_ref, low_less_ref, y_high_ref, y_less_ref = refs[:4]
    depth, width = x_ref.shape
    begin, end = first * TILE, last * TILE
    reach = end - TILE
    row = lax.broadcasted_iota(jnp.int32, (TILE, TILE), 0)
    col = lax.broadcasted_iota(jnp.int32, (TILE, TILE), 1)

    if number == 0:
        turned = refs[4:6]
        keep_halves(turned, x_ref[...].T)

        def gram(lanes, value):
            low_ref[:, lanes] = value

        tall_product(turned, width, depth, lambda lanes: x_ref[:, lanes], gram, width)
        for i in range(width // TILE):
            rows = slice(i * TILE, (i + 1) * TILE)
            low_ref[rows, rows] = low_ref[rows, rows] + jnp.where(
                row == col, jnp.broadcast_to(start_ref[:, rows], (TILE, TILE)), 0.0
            )
    else:
        low_ref[...] = start_ref[...]
        high, less = halves(start_ref[:, :begin])
        low_high_ref[:, :begin] = high
        low_less_ref[:, :begin] = less
        for k in range(number):
            lanes = slice(bounds[k] * TILE, bounds[k + 1] * TILE)
            for ref, rows in ((before[2 * k], slice(0, 2 * side)), (before[2 * k + 1], slice(2 * side, 3 * side))):
                high, less = halves(ref[...])
                y_high_ref[rows, lanes] = high
                y_less_ref[rows, lanes] = less
    for ref in (low_high_ref, low_less_ref):
        ref[:, begin:] = jnp.zeros((width, end - begin), jnp.bfloat16)
    for ref in (y_high_ref, y_less_ref):
        ref[:, begin:] = jnp.zeros((depth, end - begin), jnp.bfloat16)

    def step(j, carry):
        start = pl.multiple_of(j * TILE, TILE)
        cols = pl.ds(start, TILE)
        local = pl.ds(pl.multiple_of((j - first) * TILE, TILE), TILE)

        def reduced(value, high_ref, less_ref, rows):
            if reach == 0:
                return value
            return value - product_of_halves(
                (high_ref[rows, :reach], less_ref[rows, :reach]),
                (low_high_ref[cols, :reach], low_less_ref[cols, :reach]),
                NT,
            )

        tile = reduced(low_ref[cols, cols], low_high_ref, low_less_ref, cols)
        upper, inverse = tile_factor(tile, *small_refs)
        inverse = halves(inverse)
        for i in range(depth // side):
            rows = slice(i * side, (i + 1) * side)
            value = reduced(x_ref[rows, cols], y_high_ref, y_less_ref, rows)
            value = product_of_halves(halves(value), inverse, NT)
            for out_ref, (head, tail) in zip(outs, PIECES):
                if head <= i < tail:
                    out_ref[(i - head) * side : (i - head + 1) * side, local] = value
            high, less = halves(value)
            y_high_ref[rows, cols] = high
            y_less_ref[rows, cols] = less
        for i in range(first * TILE // WIDE, width // WIDE):
            rows = slice(i * WIDE, (i + 1) * WIDE)
            value = reduced(low_ref[rows, cols], low_high_ref, low_less_ref, rows)
            value = product_of_halves(halves(value), inverse, NT)
            place = lax.broadcasted_iota(jnp.int32, (WIDE, TILE), 0) + i * WIDE
            value = jnp.where(place >= start + TILE, value, 0.0)
            low_ref[rows, cols] = value
            high, less = halves(value)
            low_high_ref[rows, cols] = high
            low_less_ref[rows, cols] = less
        low_ref[cols, cols] = jnp.where(col <= row, upper.T, 0.0)
        return carry

    lax.fori_loop(first, last, step, 0)
    if number > 0:
        for i in range(first * TILE // WIDE):
            rows = slice(i * WIDE, (i + 1) * WIDE)
            low_ref[rows, begin:end] = jnp.zeros((WIDE, end - begin), jnp.float32)
    if final:
        for gram_ref, left, right in (
            (gram_refs[0], slice(2 * side, 3 * side), slice(0, 2 * side)),
            (gram_refs[1], slice(side, 2 * side), slice(0, side)),
        ):
            gram_ref[...] = product_of_halves(
                (y_high_ref[left, :], y_less_ref[left, :]),
                (y_high_ref[right, :], y_less_ref[right, :]),
                NT,
            )


def factored_part(x, start, before, side, bounds, number):
    depth, width = x.shape
    first, last = bounds[number], bounds[number + 1]
    final = number == len(bounds) - 2
    end = last * TILE
    shapes = [jax.ShapeDtypeStruct((width, width), jnp.float32)]
    shapes += piece_shapes(side, (last - first) * TILE)
    if final:
        shapes += [
            jax.ShapeDtypeStruct((side, 2 * side), jnp.float32),
            jax.ShapeDtypeStruct((side, side), jnp.float32),
        ]
    half = TILE // 2
    scratch = [pltpu.VMEM((half, TILE), jnp.float32), pltpu.VMEM((TILE, TILE), jnp.float32)]
    scratch += [pltpu.VMEM((half, half), jnp.float32)] * 2
    scratch += [pltpu.VMEM((width, end), jnp.bfloat16)] * 2
    scratch += [pltpu.VMEM((depth, end), jnp.bfloat16)] * 2
    if number == 0:
        scratch += [pltpu.VMEM((width, depth), jnp.bfloat16)] * 2
    return pl.pallas_call(
        functools.partial(part_kernel, side, bounds, number),
        out_shape=tuple(shapes),
        in_specs=[VMEM_SPEC] * (2 + len(before)),
        out_specs=(VMEM_SPEC,) * len(shapes),
        scratch_shapes=scratch,
        compiler_params=pltpu.CompilerParams(vmem_limit_bytes=24 << 20),
        cost_estimate=pl.CostEstimate(
            flops=20_000_000_000, bytes_accessed=3 * depth * width * 4, transcendentals=0
        ),
        name="factor_part",
    )(x, start, *before)


def near_product(left, right, dims):
    return product_of_halves(halves(left), halves(right), dims)


COUPLINGS = ((3, 0, 1), (1, 0, 2), (0, 1, 3), (2, 2, 3))


def put_coupling(side, start, y_refs, x_ref, buffer_ref, left_refs, out_ref, sems):
    rows = buffer_ref.shape[1]
    width = x_ref.shape[1]
    copies = []
    for place, (number, begin, end) in enumerate(COUPLINGS):
        keep_halves(left_refs, y_refs[number][...].T)

        def put(lanes, value, place=place):
            buffer_ref[place, :, lanes] = value

        tall_product(
            left_refs,
            rows,
            (end - begin) * side,
            lambda lanes, begin=begin, end=end: x_ref[begin * side : end * side, lanes],
            put,
            width,
        )
        copy = pltpu.make_async_copy(
            buffer_ref.at[place], out_ref.at[place, pl.ds(start, rows), :], sems.at[place]
        )
        copy.start()
        copies.append(copy)
    return copies


def early_kernel(side, starts, x_ref, *refs):
    parts = len(starts)
    y_refs, refs = refs[: 4 * parts], refs[4 * parts :]
    out_ref, refs = refs[0], refs[1:]
    buffers, (high_ref, less_ref, sems) = refs[:parts], refs[parts:]
    copies = []
    for number, start in enumerate(starts):
        copies += put_coupling(
            side,
            start,
            y_refs[4 * number : 4 * number + 4],
            x_ref,
            buffers[number],
            (high_ref, less_ref),
            out_ref,
            sems.at[number],
        )
    for copy in copies:
        copy.wait()


def early(x, parts, starts, side):
    width = x.shape[1]
    heights = [part[0].shape[1] for part in parts]
    most = max(heights)
    return pl.pallas_call(
        functools.partial(early_kernel, side, starts),
        out_shape=jax.ShapeDtypeStruct((4, width, width), jnp.float32),
        in_specs=[VMEM_SPEC] * (1 + 4 * len(parts)),
        out_specs=ANY_SPEC,
        scratch_shapes=[pltpu.VMEM((4, height, width), jnp.float32) for height in heights]
        + [
            pltpu.VMEM((most, 2 * side), jnp.bfloat16),
            pltpu.VMEM((most, 2 * side), jnp.bfloat16),
            pltpu.SemaphoreType.DMA((len(parts), 4)),
        ],
        compiler_params=pltpu.CompilerParams(vmem_limit_bytes=24 << 20),
        cost_estimate=pl.CostEstimate(
            flops=8_000_000_000, bytes_accessed=4 * width * width * 4, transcendentals=0
        ),
        name="early",
    )(x, *[piece for part in parts for piece in part])


def before_kernel(side, flags_ref, x_ref, gram_one_ref, gram_two_ref, *refs):
    mine, refs = refs[:PARTS], refs[PARTS:]
    pieces, refs = [refs[4 * k : 4 * k + 4] for k in range(PARTS - 1)], refs[4 * PARTS - 4 :]
    rest_ref, near_ref, far_ref, high_ref, less_ref = refs
    width = x_ref.shape[1]
    own, above, second_above, under, second_under = [flags_ref[k] > 0 for k in range(5)]
    one, two, three = slice(0, side), slice(side, 2 * side), slice(2 * side, 3 * side)
    pair, tail = slice(0, 2 * side), slice(side, 3 * side)
    keep_halves((high_ref, less_ref), x_ref[...].T)
    rest_ref[...] = x_ref[...]
    near_ref[three, :] = jnp.zeros((side, width), jnp.float32)
    far_ref[two, :] = jnp.zeros((side, width), jnp.float32)

    @pl.when(own)
    def _():
        start = 0
        for ref in mine:
            lanes = slice(start, start + ref.shape[1])
            near_ref[pair, lanes] = ref[...]
            far_ref[one, lanes] = ref[side:, :]
            start += ref.shape[1]

    @pl.when(jnp.logical_not(own))
    def _():
        near_ref[pair, :] = x_ref[tail, :]
        far_ref[one, :] = x_ref[three, :]

    def weighed(number, rows):
        gram = 0.0
        for part in pieces:
            both = halves(part[number][...])
            gram = gram + product_of_halves(both, both, NT)
        return near_product(gram, x_ref[rows, :], NN)

    @pl.when(second_above)
    def _():
        rest_ref[one, :] = rest_ref[one, :] - weighed(3, one)

    @pl.when(above)
    def _():
        term = weighed(1, pair)
        rest_ref[pair, :] = rest_ref[pair, :] - term
        near_ref[one, :] = near_ref[one, :] - term[side:]

    @pl.when(under)
    def _():
        term = weighed(0, tail)
        rest_ref[tail, :] = rest_ref[tail, :] - term
        far_ref[one, :] = far_ref[one, :] - term[side:]
        far_ref[two, :] = -near_product(gram_one_ref[...], x_ref[tail, :], NN)

    @pl.when(second_under)
    def _():
        term = weighed(2, three)
        rest_ref[three, :] = rest_ref[three, :] - term
        near_ref[two, :] = near_ref[two, :] - term
        near_ref[three, :] = -near_product(gram_two_ref[...], x_ref[three, :], NN)


def before_last(flags, x, grams, mine, parts, side):
    depth, width = x.shape
    inputs = [x, *grams, *mine] + [piece for part in parts for piece in part]
    return pl.pallas_call(
        functools.partial(before_kernel, side),
        out_shape=(
            jax.ShapeDtypeStruct((depth, width), jnp.float32),
            jax.ShapeDtypeStruct((depth, width), jnp.float32),
            jax.ShapeDtypeStruct((2 * side, width), jnp.float32),
            jax.ShapeDtypeStruct((width, depth), jnp.bfloat16),
            jax.ShapeDtypeStruct((width, depth), jnp.bfloat16),
        ),
        in_specs=[SMEM_SPEC] + [VMEM_SPEC] * len(inputs),
        out_specs=(VMEM_SPEC,) * 5,
        compiler_params=pltpu.CompilerParams(vmem_limit_bytes=24 << 20),
        cost_estimate=pl.CostEstimate(
            flops=4_000_000_000, bytes_accessed=4 * width * width * 4, transcendentals=0
        ),
        name="before_last",
    )(flags, *inputs)


def late_kernel(side, cut, flags_ref, *refs):
    x_ref, shift_ref, direct_ref, onward_ref, second_ref, extra_ref, low_ref = refs[:7]
    lasts, ready, refs = refs[7:11], refs[11:16], refs[16:]
    partial_ref, schur_ref, coupling_ref = refs[:3]
    buffer_ref, tile_ref, rest_ref, near_ref, far_ref, high_ref, less_ref, sems, outs = refs[3:]
    left_refs = (high_ref, less_ref)
    width = x_ref.shape[1]
    rows = width - cut
    copies = put_coupling(side, cut, lasts, x_ref, buffer_ref, left_refs, coupling_ref, sems)
    own, above, second_above, under, second_under = [flags_ref[k] > 0 for k in range(5)]
    for ref, given in zip((rest_ref, near_ref, far_ref), ready):
        ref[...] = given[...]

    def take_off(flag, place, targets):
        number, begin, end = COUPLINGS[place]
        height = (end - begin) * side

        @pl.when(flag)
        def _():
            keep_halves(left_refs, lasts[number][...])

            def put(lanes, value):
                for ref, there, here, amount in targets:
                    ref[there : there + amount, lanes] = (
                        ref[there : there + amount, lanes] - value[here : here + amount]
                    )

            tall_product(
                left_refs, height, rows, lambda lanes: buffer_ref[place, :, lanes], put, width
            )

    take_off(second_above, 0, ((rest_ref, 0, 0, side),))
    take_off(above, 1, ((rest_ref, 0, 0, 2 * side), (near_ref, 0, side, side)))
    take_off(under, 2, ((rest_ref, side, 0, 2 * side), (far_ref, 0, side, side)))
    take_off(second_under, 3, ((rest_ref, 2 * side, 0, side), (near_ref, side, 0, side)))

    def put(place):
        copy = pltpu.make_async_copy(tile_ref.at[place], schur_ref.at[place], outs.at[place])
        copy.start()
        return copy

    def fill(place, halved, depth, right_ref):
        def store(lanes, value):
            tile_ref[place, :, lanes] = value

        tall_product(halved, width, depth, lambda lanes: right_ref[:, lanes], store, width)

    def from_coupling(place, member):
        copy = pltpu.make_async_copy(
            partial_ref.at[member, pl.ds(0, cut), :],
            tile_ref.at[place, pl.ds(0, cut), :],
            outs.at[place],
        )
        copy.start()
        tile_ref[place, cut:, :] = buffer_ref[member]
        copy.wait()

    @pl.when(own)
    def _():
        tile_ref[2] = low_ref[...]

    @pl.when(jnp.logical_not(own))
    def _():
        fill(2, ready[3:], 3 * side, rest_ref)
        for i in range(width // TILE):
            rows = slice(i * TILE, (i + 1) * TILE)
            row = lax.broadcasted_iota(jnp.int32, (TILE, TILE), 0)
            col = lax.broadcasted_iota(jnp.int32, (TILE, TILE), 1)
            tile_ref[2, rows, rows] = tile_ref[2, rows, rows] + jnp.where(
                row == col, jnp.broadcast_to(shift_ref[:, rows], (TILE, TILE)), 0.0
            )

    copies.append(put(2))

    @pl.when(under)
    def _():
        from_coupling(1, 2)

    @pl.when(jnp.logical_not(under))
    def _():
        below = direct_ref[...] + onward_ref[...]
        keep_halves(left_refs, jnp.concatenate([below, extra_ref[...]], axis=0).T)
        fill(1, left_refs, 3 * side, near_ref)

    copies.append(put(1))

    @pl.when(second_under)
    def _():
        from_coupling(0, 3)

    @pl.when(jnp.logical_not(second_under))
    def _():
        keep_halves(left_refs, second_ref[...].T)
        fill(0, left_refs, 2 * side, far_ref)

    copies.append(put(0))
    for copy in copies:
        copy.wait()


def late(flags, x, shift, received, low, lasts, ready, partial, cut, side):
    depth, width = x.shape
    rows = width - cut
    inputs = [x, shift, *received, low, *lasts, *ready]
    return pl.pallas_call(
        functools.partial(late_kernel, side, cut),
        out_shape=(
            jax.ShapeDtypeStruct((3, width, width), jnp.float32),
            jax.ShapeDtypeStruct((4, width, width), jnp.float32),
        ),
        in_specs=[SMEM_SPEC] + [VMEM_SPEC] * len(inputs) + [ANY_SPEC],
        out_specs=(ANY_SPEC, ANY_SPEC),
        input_output_aliases={1 + len(inputs): 1},
        scratch_shapes=[
            pltpu.VMEM((4, rows, width), jnp.float32),
            pltpu.VMEM((3, width, width), jnp.float32),
            pltpu.VMEM((depth, width), jnp.float32),
            pltpu.VMEM((depth, width), jnp.float32),
            pltpu.VMEM((2 * side, width), jnp.float32),
            pltpu.VMEM((width, depth), jnp.bfloat16),
            pltpu.VMEM((width, depth), jnp.bfloat16),
            pltpu.SemaphoreType.DMA((4,)),
            pltpu.SemaphoreType.DMA((3,)),
        ],
        compiler_params=pltpu.CompilerParams(vmem_limit_bytes=34 << 20),
        cost_estimate=pl.CostEstimate(
            flops=12_000_000_000, bytes_accessed=7 * width * width * 4, transcendentals=0
        ),
        name="late",
    )(flags, *inputs, partial)


def local(weighted_jacobian_strips, leading_pose_index, levenberg_shift, removal_flags):
    count = lax.axis_size(AXES)
    own = lax.axis_index(AXES)
    surfels, _, width = weighted_jacobian_strips.shape
    capacity = max(2, (3 * surfels + 2 * count - 1) // (2 * count))
    side = count * capacity
    tiles = width // TILE
    bounds = tuple(tiles * k // PARTS for k in range(PARTS + 1))
    starts = tuple(bound * TILE for bound in bounds[:-1])
    flags = removal_flags[(own + jnp.array((0, 1, 2, -1, -2), jnp.int32)) % count]

    chunks = bucketed(
        leading_pose_index.reshape(1, surfels),
        weighted_jacobian_strips.transpose(1, 0, 2),
        count,
        capacity,
    )
    chunks = lax.all_to_all(chunks, AXES, split_axis=0, concat_axis=0, tiled=True)
    x, two, last = regrouped(chunks, capacity, width)

    def sent_parts(parts):
        return [passed_along(part, steps) for part, steps in zip(parts, (1, -1, 2, -2))]

    direct = lax.ppermute(two, AXES, [(k, k + 1) for k in range(0, count, 2)])
    second = passed_along(two, 2)

    def solved(number, start, known):
        before = [part[k] for part in known for k in (0, 3)]
        return factored_part(x, start, before, side, bounds, number)

    low, *part = solved(0, levenberg_shift, ())
    known = [part]
    parts = [sent_parts(part)]
    for number in range(1, PARTS - 1):
        low, *part = solved(number, low, known)
        known.append(part)
        parts.append(sent_parts(part))
    onward = lax.ppermute(second, AXES, [(k + 1, k) for k in range(0, count, 2)])
    extra = passed_along(last, 1)
    low, *part, gram_one, gram_two = solved(PARTS - 1, low, known)
    known.append(part)
    parts.append(sent_parts(part))
    grams = (passed_along(gram_one, 1), passed_along(gram_two, 2))
    partial = early(x, parts[:-1], starts[:-1], side)
    ready = before_last(flags, x, grams, [part[1] for part in known], parts[:-1], side)
    schur, coupling = late(
        flags,
        x,
        levenberg_shift,
        (direct, onward, second, extra),
        low,
        parts[-1],
        ready,
        partial,
        starts[-1],
        side,
    )
    return schur[None], coupling[None]


def solution(mesh):
    in_specs = (P(AXES, None, None), P(AXES, None), P(AXES, None), P())
    out_specs = (P(AXES, None, None, None), P(AXES, None, None, None))

    return jax.shard_map(local, mesh=mesh, in_specs=in_specs, out_specs=out_specs, check_vma=False)
```

```python
import functools
import math

import jax
import jax.numpy as jnp
from jax import lax
from jax.experimental import pallas as pl
from jax.experimental.pallas import tpu as pltpu
from jax.sharding import PartitionSpec as P


AXES = ("gx", "gy")
TILE = 128
GROUP = 8
WIDE = 256
PARTS = 3
NT = (((1,), (1,)), ((), ()))
TN = (((0,), (0,)), ((), ()))
NN = (((1,), (0,)), ((), ()))
VMEM_SPEC = pl.BlockSpec(memory_space=pltpu.VMEM)
SMEM_SPEC = pl.BlockSpec(memory_space=pltpu.SMEM)
ANY_SPEC = pl.BlockSpec(memory_space=pl.ANY)
PIECES = ((0, 2), (1, 3), (0, 1), (2, 3))


def passed_along(value, steps):
    count = lax.axis_size(AXES)
    pairs = [(source, (source + steps) % count) for source in range(count)]
    return lax.ppermute(value, AXES, pairs)


def product(left, right, dims, precision=lax.Precision.HIGHEST):
    return lax.dot_general(
        left, right, dims, precision=precision, preferred_element_type=jnp.float32
    )


def bucket_kernel(count, capacity, index_ref, strips_ref, out_ref, rows_ref):
    surfels = strips_ref.shape[1]
    width = strips_ref.shape[2]
    lane_tiles = width // WIDE
    index = index_ref[...]
    base = lax.broadcasted_iota(jnp.int32, (count, surfels), 0)
    hot = (base == index).astype(jnp.float32)
    first = lax.broadcasted_iota(jnp.int32, (surfels, surfels), 0)
    second = lax.broadcasted_iota(jnp.int32, (surfels, surfels), 1)
    ahead = (first < second).astype(jnp.float32)
    earlier = product(hot, ahead, NN)
    within = jnp.sum(earlier * hot, axis=0, keepdims=True).astype(jnp.int32)
    period = GROUP // math.gcd(capacity, GROUP)
    for piece in range(3):
        moved = index + piece
        moved = jnp.where(moved >= count, moved - count, moved)
        slot = moved * capacity + within
        row = lax.broadcasted_iota(jnp.int32, (count * capacity, surfels), 0)
        pick = (row == slot).astype(jnp.bfloat16)
        values = strips_ref[piece]
        high = values.astype(jnp.bfloat16)
        rest = values - high.astype(jnp.float32)
        middle = rest.astype(jnp.bfloat16)
        low = (rest - middle.astype(jnp.float32)).astype(jnp.bfloat16)
        rows_ref[...] = product(
            jnp.concatenate([pick, pick, pick], axis=1),
            jnp.concatenate([high, middle, low], axis=0),
            NN,
            lax.Precision.DEFAULT,
        )

        def spread(turn, carry, piece=piece):
            start = pl.multiple_of(turn * (period * capacity), GROUP)
            for tile in range(lane_tiles):
                block = rows_ref[pl.ds(start, period * capacity), WIDE * tile : WIDE * (tile + 1)]
                for member in range(period):
                    begin = (piece * lane_tiles + tile) * capacity
                    out_ref[turn * period + member, begin : begin + capacity, :] = block[
                        member * capacity : (member + 1) * capacity
                    ]
            return carry

        lax.fori_loop(0, count // period, spread, 0)


def bucketed(index_row, strips, count, capacity):
    width = strips.shape[2]
    return pl.pallas_call(
        functools.partial(bucket_kernel, count, capacity),
        out_shape=jax.ShapeDtypeStruct(
            (count, 3 * (width // WIDE) * capacity, WIDE), jnp.float32
        ),
        in_specs=[VMEM_SPEC, VMEM_SPEC],
        out_specs=VMEM_SPEC,
        scratch_shapes=[pltpu.VMEM((count * capacity, width), jnp.float32)],
        name="bucket",
    )(index_row, strips)


def regroup_kernel(capacity, in_ref, out_ref, two_ref, one_ref):
    count = in_ref.shape[0]
    width = out_ref.shape[1]
    lane_tiles = width // WIDE
    period = GROUP // math.gcd(capacity, GROUP)

    def gather(turn, carry):
        for piece in range(3):
            for tile in range(lane_tiles):
                begin = (piece * lane_tiles + tile) * capacity
                block = jnp.concatenate(
                    [
                        in_ref[turn * period + member, begin : begin + capacity, :]
                        for member in range(period)
                    ],
                    axis=0,
                )
                start = pl.multiple_of(
                    piece * count * capacity + turn * (period * capacity), GROUP
                )
                out_ref[
                    pl.ds(start, period * capacity), WIDE * tile : WIDE * (tile + 1)
                ] = block
        return carry

    lax.fori_loop(0, count // period, gather, 0)
    side = count * capacity
    two_ref[...] = out_ref[: 2 * side, :]
    one_ref[...] = out_ref[2 * side :, :]


def regrouped(chunks, capacity, width):
    side = chunks.shape[0] * capacity
    return pl.pallas_call(
        functools.partial(regroup_kernel, capacity),
        out_shape=tuple(
            jax.ShapeDtypeStruct((parts * side, width), jnp.float32) for parts in (3, 2, 1)
        ),
        in_specs=[VMEM_SPEC],
        out_specs=(VMEM_SPEC,) * 3,
        compiler_params=pltpu.CompilerParams(vmem_limit_bytes=16 << 20),
        name="regroup",
    )(chunks)


def full(value):
    return jnp.broadcast_to(value, (GROUP, TILE))


def half_factor(pair_ref, done_ref, start):
    groups = pair_ref.shape[0] // GROUP
    sub = lax.broadcasted_iota(jnp.int32, (GROUP, TILE), 0)
    rows = [pair_ref[GROUP * g : GROUP * (g + 1), :] for g in range(groups)]
    eight = range(GROUP)
    for p in range(groups):
        strip = rows[p]
        cols = [full(strip[:, GROUP * p + k : GROUP * p + k + 1]) for k in eight]
        m = [[full(cols[k][i : i + 1, :]) if k <= i else None for k in eight] for i in eight]
        r = [None] * GROUP
        u = [full(strip[j : j + 1, :]) for j in eight]
        for j in eight:
            r[j] = lax.rsqrt(m[j][j])
            for i in range(j + 1, GROUP):
                m[i][j] = m[i][j] * r[j]
            for k in range(j + 1, GROUP):
                for i in range(k, GROUP):
                    m[i][k] = m[i][k] - m[i][j] * m[k][j]
            u[j] = u[j] * r[j]
            for i in range(j + 1, GROUP):
                u[i] = u[i] - m[i][j] * u[j]
        joined = u[0]
        for j in range(1, GROUP):
            joined = jnp.where(sub == j, u[j], joined)
        done_ref[pl.ds(start + GROUP * p, GROUP), :] = joined
        for g in range(p + 1, groups):
            side = [full(rows[g][:, GROUP * p + k : GROUP * p + k + 1]) for k in eight]
            x = rows[g]
            for j in eight:
                side[j] = side[j] * r[j]
                for i in range(j + 1, GROUP):
                    side[i] = side[i] - m[i][j] * side[j]
                x = x - side[j] * u[j]
            rows[g] = x


def tile_factor(tile, pair_ref, done_ref, cross_ref, corner_ref):
    half = TILE // 2
    row = lax.broadcasted_iota(jnp.int32, (half, half), 0)
    col = lax.broadcasted_iota(jnp.int32, (half, half), 1)
    unit = jnp.where(row == col, 1.0, 0.0).astype(jnp.float32)
    zero = jnp.zeros((half, half), jnp.float32)
    pair_ref[...] = jnp.concatenate([tile[:half, :half], unit], axis=1)
    cross_ref[...] = tile[:half, half:]
    corner_ref[...] = tile[half:, half:]

    def turn(number, carry):
        half_factor(pair_ref, done_ref, pl.multiple_of(number * half, half))

        @pl.when(number == 0)
        def _():
            cross = near_product(done_ref[:half, half:], cross_ref[...], NN)
            cross_ref[...] = cross
            both = halves(cross)
            rest = corner_ref[...] - product_of_halves(both, both, TN)
            pair_ref[...] = jnp.concatenate([rest, unit], axis=1)

        return carry

    lax.fori_loop(0, 2, turn, 0)
    first, second = done_ref[:half, half:], done_ref[half:, half:]
    middle = near_product(cross_ref[...], first, TN)
    upper = jnp.concatenate(
        [
            jnp.concatenate([done_ref[:half, :half], cross_ref[...]], axis=1),
            jnp.concatenate([zero, done_ref[half:, :half]], axis=1),
        ],
        axis=0,
    )
    inverse = jnp.concatenate(
        [
            jnp.concatenate([first, zero], axis=1),
            jnp.concatenate([-near_product(second, middle, NN), second], axis=1),
        ],
        axis=0,
    )
    return upper, inverse


def halves(value):
    high = value.astype(jnp.bfloat16)
    return high, (value - high.astype(jnp.float32)).astype(jnp.bfloat16)


def product_of_halves(left, right, dims):
    total = product(left[0], right[0], dims, lax.Precision.DEFAULT)
    total = total + product(left[0], right[1], dims, lax.Precision.DEFAULT)
    return total + product(left[1], right[0], dims, lax.Precision.DEFAULT)


def lanes_at(number):
    return pl.ds(pl.multiple_of(number * WIDE, WIDE), WIDE)


def tall_product(left_refs, rows, depth, right_at, put, width):
    left = tuple(ref[:rows, :depth] for ref in left_refs)

    def block(number, carry):
        put(lanes_at(number), product_of_halves(left, halves(right_at(lanes_at(number))), NN))
        return carry

    lax.fori_loop(0, width // WIDE, block, 0)


def keep_halves(left_refs, value):
    rows, depth = value.shape
    high, low = halves(value)
    left_refs[0][:rows, :depth] = high
    left_refs[1][:rows, :depth] = low


def piece_shapes(side, lanes):
    return tuple(
        jax.ShapeDtypeStruct(((stop - start) * side, lanes), jnp.float32) for start, stop in PIECES
    )


def part_kernel(side, bounds, number, *refs):
    first, last = bounds[number], bounds[number + 1]
    final = number == len(bounds) - 2
    x_ref, start_ref = refs[:2]
    before = refs[2 : 2 + 2 * number]
    refs = refs[2 + 2 * number :]
    low_ref, outs = refs[0], refs[1:5]
    gram_refs, refs = (refs[5:7], refs[7:]) if final else ((), refs[5:])
    small_refs, refs = refs[:4], refs[4:]
    low_high_ref, low_less_ref, y_high_ref, y_less_ref = refs[:4]
    depth, width = x_ref.shape
    begin, end = first * TILE, last * TILE
    reach = end - TILE
    row = lax.broadcasted_iota(jnp.int32, (TILE, TILE), 0)
    col = lax.broadcasted_iota(jnp.int32, (TILE, TILE), 1)

    if number == 0:
        turned = refs[4:6]
        keep_halves(turned, x_ref[...].T)

        def gram(lanes, value):
            low_ref[:, lanes] = value

        tall_product(turned, width, depth, lambda lanes: x_ref[:, lanes], gram, width)
        for i in range(width // TILE):
            rows = slice(i * TILE, (i + 1) * TILE)
            low_ref[rows, rows] = low_ref[rows, rows] + jnp.where(
                row == col, jnp.broadcast_to(start_ref[:, rows], (TILE, TILE)), 0.0
            )
    else:
        low_ref[...] = start_ref[...]
        high, less = halves(start_ref[:, :begin])
        low_high_ref[:, :begin] = high
        low_less_ref[:, :begin] = less
        for k in range(number):
            lanes = slice(bounds[k] * TILE, bounds[k + 1] * TILE)
            for ref, rows in ((before[2 * k], slice(0, 2 * side)), (before[2 * k + 1], slice(2 * side, 3 * side))):
                high, less = halves(ref[...])
                y_high_ref[rows, lanes] = high
                y_less_ref[rows, lanes] = less
    for ref in (low_high_ref, low_less_ref):
        ref[:, begin:] = jnp.zeros((width, end - begin), jnp.bfloat16)
    for ref in (y_high_ref, y_less_ref):
        ref[:, begin:] = jnp.zeros((depth, end - begin), jnp.bfloat16)

    def step(j, carry):
        start = pl.multiple_of(j * TILE, TILE)
        cols = pl.ds(start, TILE)
        local = pl.ds(pl.multiple_of((j - first) * TILE, TILE), TILE)

        def reduced(value, high_ref, less_ref, rows):
            if reach == 0:
                return value
            return value - product_of_halves(
                (high_ref[rows, :reach], less_ref[rows, :reach]),
                (low_high_ref[cols, :reach], low_less_ref[cols, :reach]),
                NT,
            )

        tile = reduced(low_ref[cols, cols], low_high_ref, low_less_ref, cols)
        upper, inverse = tile_factor(tile, *small_refs)
        inverse = halves(inverse)
        for i in range(depth // side):
            rows = slice(i * side, (i + 1) * side)
            value = reduced(x_ref[rows, cols], y_high_ref, y_less_ref, rows)
            value = product_of_halves(halves(value), inverse, NT)
            for out_ref, (head, tail) in zip(outs, PIECES):
                if head <= i < tail:
                    out_ref[(i - head) * side : (i - head + 1) * side, local] = value
            high, less = halves(value)
            y_high_ref[rows, cols] = high
            y_less_ref[rows, cols] = less
        for i in range(first * TILE // WIDE, width // WIDE):
            rows = slice(i * WIDE, (i + 1) * WIDE)
            value = reduced(low_ref[rows, cols], low_high_ref, low_less_ref, rows)
            value = product_of_halves(halves(value), inverse, NT)
            place = lax.broadcasted_iota(jnp.int32, (WIDE, TILE), 0) + i * WIDE
            value = jnp.where(place >= start + TILE, value, 0.0)
            low_ref[rows, cols] = value
            high, less = halves(value)
            low_high_ref[rows, cols] = high
            low_less_ref[rows, cols] = less
        low_ref[cols, cols] = jnp.where(col <= row, upper.T, 0.0)
        return carry

    lax.fori_loop(first, last, step, 0)
    if number > 0:
        for i in range(first * TILE // WIDE):
            rows = slice(i * WIDE, (i + 1) * WIDE)
            low_ref[rows, begin:end] = jnp.zeros((WIDE, end - begin), jnp.float32)
    if final:
        for gram_ref, left, right in (
            (gram_refs[0], slice(2 * side, 3 * side), slice(0, 2 * side)),
            (gram_refs[1], slice(side, 2 * side), slice(0, side)),
        ):
            gram_ref[...] = product_of_halves(
                (y_high_ref[left, :], y_less_ref[left, :]),
                (y_high_ref[right, :], y_less_ref[right, :]),
                NT,
            )


def factored_part(x, start, before, side, bounds, number):
    depth, width = x.shape
    first, last = bounds[number], bounds[number + 1]
    final = number == len(bounds) - 2
    end = last * TILE
    shapes = [jax.ShapeDtypeStruct((width, width), jnp.float32)]
    shapes += piece_shapes(side, (last - first) * TILE)
    if final:
        shapes += [
            jax.ShapeDtypeStruct((side, 2 * side), jnp.float32),
            jax.ShapeDtypeStruct((side, side), jnp.float32),
        ]
    half = TILE // 2
    scratch = [pltpu.VMEM((half, TILE), jnp.float32), pltpu.VMEM((TILE, TILE), jnp.float32)]
    scratch += [pltpu.VMEM((half, half), jnp.float32)] * 2
    scratch += [pltpu.VMEM((width, end), jnp.bfloat16)] * 2
    scratch += [pltpu.VMEM((depth, end), jnp.bfloat16)] * 2
    if number == 0:
        scratch += [pltpu.VMEM((width, depth), jnp.bfloat16)] * 2
    return pl.pallas_call(
        functools.partial(part_kernel, side, bounds, number),
        out_shape=tuple(shapes),
        in_specs=[VMEM_SPEC] * (2 + len(before)),
        out_specs=(VMEM_SPEC,) * len(shapes),
        scratch_shapes=scratch,
        compiler_params=pltpu.CompilerParams(vmem_limit_bytes=24 << 20),
        cost_estimate=pl.CostEstimate(
            flops=20_000_000_000, bytes_accessed=3 * depth * width * 4, transcendentals=0
        ),
        name="factor_part",
    )(x, start, *before)


def near_product(left, right, dims):
    return product_of_halves(halves(left), halves(right), dims)


COUPLINGS = ((3, 0, 1), (1, 0, 2), (0, 1, 3), (2, 2, 3))


def put_coupling(side, start, y_refs, x_ref, buffer_ref, left_refs, out_ref, sems, places=range(4)):
    rows = buffer_ref.shape[1]
    width = x_ref.shape[1]
    copies = []
    for place in places:
        number, begin, end = COUPLINGS[place]
        slot = place % buffer_ref.shape[0]
        keep_halves(left_refs, y_refs[number][...].T)

        def put(lanes, value, slot=slot):
            buffer_ref[slot, :, lanes] = value

        tall_product(
            left_refs,
            rows,
            (end - begin) * side,
            lambda lanes, begin=begin, end=end: x_ref[begin * side : end * side, lanes],
            put,
            width,
        )
        copy = pltpu.make_async_copy(
            buffer_ref.at[slot], out_ref.at[place, pl.ds(start, rows), :], sems.at[place]
        )
        copy.start()
        copies.append(copy)
    return copies


def early_kernel(side, starts, x_ref, *refs):
    parts = len(starts)
    y_refs, refs = refs[: 4 * parts], refs[4 * parts :]
    out_ref, refs = refs[0], refs[1:]
    buffers, (high_ref, less_ref, sems) = refs[:parts], refs[parts:]
    copies = []
    for number, start in enumerate(starts):
        copies += put_coupling(
            side,
            start,
            y_refs[4 * number : 4 * number + 4],
            x_ref,
            buffers[number],
            (high_ref, less_ref),
            out_ref,
            sems.at[number],
        )
    for copy in copies:
        copy.wait()


def early(x, parts, starts, side):
    width = x.shape[1]
    heights = [part[0].shape[1] for part in parts]
    most = max(heights)
    return pl.pallas_call(
        functools.partial(early_kernel, side, starts),
        out_shape=jax.ShapeDtypeStruct((4, width, width), jnp.float32),
        in_specs=[VMEM_SPEC] * (1 + 4 * len(parts)),
        out_specs=ANY_SPEC,
        scratch_shapes=[pltpu.VMEM((4, height, width), jnp.float32) for height in heights]
        + [
            pltpu.VMEM((most, 2 * side), jnp.bfloat16),
            pltpu.VMEM((most, 2 * side), jnp.bfloat16),
            pltpu.SemaphoreType.DMA((len(parts), 4)),
        ],
        compiler_params=pltpu.CompilerParams(vmem_limit_bytes=24 << 20),
        cost_estimate=pl.CostEstimate(
            flops=8_000_000_000, bytes_accessed=4 * width * width * 4, transcendentals=0
        ),
        name="early",
    )(x, *[piece for part in parts for piece in part])


def before_kernel(side, flags_ref, x_ref, gram_one_ref, gram_two_ref, *refs):
    mine, refs = refs[:PARTS], refs[PARTS:]
    pieces, refs = [refs[4 * k : 4 * k + 4] for k in range(PARTS - 1)], refs[4 * PARTS - 4 :]
    rest_ref, near_ref, far_ref, high_ref, less_ref = refs
    width = x_ref.shape[1]
    own, above, second_above, under, second_under = [flags_ref[k] > 0 for k in range(5)]
    one, two, three = slice(0, side), slice(side, 2 * side), slice(2 * side, 3 * side)
    pair, tail = slice(0, 2 * side), slice(side, 3 * side)
    keep_halves((high_ref, less_ref), x_ref[...].T)
    rest_ref[...] = x_ref[...]
    near_ref[three, :] = jnp.zeros((side, width), jnp.float32)
    far_ref[two, :] = jnp.zeros((side, width), jnp.float32)

    @pl.when(own)
    def _():
        start = 0
        for ref in mine:
            lanes = slice(start, start + ref.shape[1])
            near_ref[pair, lanes] = ref[...]
            far_ref[one, lanes] = ref[side:, :]
            start += ref.shape[1]

    @pl.when(jnp.logical_not(own))
    def _():
        near_ref[pair, :] = x_ref[tail, :]
        far_ref[one, :] = x_ref[three, :]

    def weighed(number, rows):
        gram = 0.0
        for part in pieces:
            both = halves(part[number][...])
            gram = gram + product_of_halves(both, both, NT)
        return near_product(gram, x_ref[rows, :], NN)

    @pl.when(second_above)
    def _():
        rest_ref[one, :] = rest_ref[one, :] - weighed(3, one)

    @pl.when(above)
    def _():
        term = weighed(1, pair)
        rest_ref[pair, :] = rest_ref[pair, :] - term
        near_ref[one, :] = near_ref[one, :] - term[side:]

    @pl.when(under)
    def _():
        term = weighed(0, tail)
        rest_ref[tail, :] = rest_ref[tail, :] - term
        far_ref[one, :] = far_ref[one, :] - term[side:]
        far_ref[two, :] = -near_product(gram_one_ref[...], x_ref[tail, :], NN)

    @pl.when(second_under)
    def _():
        term = weighed(2, three)
        rest_ref[three, :] = rest_ref[three, :] - term
        near_ref[two, :] = near_ref[two, :] - term
        near_ref[three, :] = -near_product(gram_two_ref[...], x_ref[three, :], NN)


def before_last(flags, x, grams, mine, parts, side):
    depth, width = x.shape
    inputs = [x, *grams, *mine] + [piece for part in parts for piece in part]
    return pl.pallas_call(
        functools.partial(before_kernel, side),
        out_shape=(
            jax.ShapeDtypeStruct((depth, width), jnp.float32),
            jax.ShapeDtypeStruct((depth, width), jnp.float32),
            jax.ShapeDtypeStruct((2 * side, width), jnp.float32),
            jax.ShapeDtypeStruct((width, depth), jnp.bfloat16),
            jax.ShapeDtypeStruct((width, depth), jnp.bfloat16),
        ),
        in_specs=[SMEM_SPEC] + [VMEM_SPEC] * len(inputs),
        out_specs=(VMEM_SPEC,) * 5,
        compiler_params=pltpu.CompilerParams(vmem_limit_bytes=24 << 20),
        cost_estimate=pl.CostEstimate(
            flops=4_000_000_000, bytes_accessed=4 * width * width * 4, transcendentals=0
        ),
        name="before_last",
    )(flags, *inputs)


def late_kernel(side, cut, flags_ref, *refs):
    x_ref, shift_ref, second_ref, low_ref = refs[:4]
    lasts, ready, refs = (refs[4], None, *refs[5:7]), refs[7:12], refs[12:]
    partial_ref, schur_ref, coupling_ref, near_ref = refs[:4]
    buffer_ref, tile_ref, rest_ref, far_ref, high_ref, less_ref, sems, outs = refs[4:]
    left_refs = (high_ref, less_ref)
    width = x_ref.shape[1]
    rows = width - cut
    copies = put_coupling(
        side, cut, lasts, x_ref, buffer_ref, left_refs, coupling_ref, sems, (0, 3, 2)
    )
    own, _, second_above, under, second_under = [flags_ref[k] > 0 for k in range(5)]
    for ref, given in zip((rest_ref, near_ref, far_ref), ready):
        ref[...] = given[...]

    def take_off(flag, place, targets):
        number, begin, end = COUPLINGS[place]
        height = (end - begin) * side

        @pl.when(flag)
        def _():
            keep_halves(left_refs, lasts[number][...])

            def put(lanes, value):
                for ref, there, here, amount in targets:
                    ref[there : there + amount, lanes] = (
                        ref[there : there + amount, lanes] - value[here : here + amount]
                    )

            tall_product(
                left_refs, height, rows, lambda lanes: buffer_ref[place, :, lanes], put, width
            )

    take_off(second_above, 0, ((rest_ref, 0, 0, side),))
    take_off(under, 2, ((rest_ref, side, 0, 2 * side), (far_ref, 0, side, side)))
    take_off(second_under, 3, ((rest_ref, 2 * side, 0, side), (near_ref, side, 0, side)))

    def put(place):
        return pltpu.make_async_copy(tile_ref.at[place], schur_ref.at[place], outs.at[place])

    def fill(place, halved, depth, right_ref):
        def store(lanes, value):
            tile_ref[place, :, lanes] = value

        tall_product(halved, width, depth, lambda lanes: right_ref[:, lanes], store, width)

    def from_coupling(place, member):
        copy = pltpu.make_async_copy(
            partial_ref.at[member, pl.ds(0, cut), :],
            tile_ref.at[place, pl.ds(0, cut), :],
            outs.at[place],
        )
        copy.start()
        tile_ref[place, cut:, :] = buffer_ref[member]
        copy.wait()

    @pl.when(own)
    def _():
        tile_ref[2] = low_ref[...]

    @pl.when(jnp.logical_not(own))
    def _():
        fill(2, ready[3:], 3 * side, rest_ref)
        for i in range(width // TILE):
            rows = slice(i * TILE, (i + 1) * TILE)
            row = lax.broadcasted_iota(jnp.int32, (TILE, TILE), 0)
            col = lax.broadcasted_iota(jnp.int32, (TILE, TILE), 1)
            tile_ref[2, rows, rows] = tile_ref[2, rows, rows] + jnp.where(
                row == col, jnp.broadcast_to(shift_ref[:, rows], (TILE, TILE)), 0.0
            )

    put(2).start()

    @pl.when(under)
    def _():
        from_coupling(1, 2)

    @pl.when(under)
    def _():
        put(1).start()

    @pl.when(second_under)
    def _():
        from_coupling(0, 3)

    @pl.when(jnp.logical_not(second_under))
    def _():
        keep_halves(left_refs, second_ref[...].T)
        fill(0, left_refs, 2 * side, far_ref)

    put(0).start()

    @pl.when(under)
    def _():
        put(1).wait()

    put(2).wait()
    put(0).wait()
    for copy in copies:
        copy.wait()


def late(flags, x, shift, second, low, lasts, ready, partial, cut, side):
    depth, width = x.shape
    rows = width - cut
    inputs = [x, shift, second, low, lasts[0], *lasts[2:], *ready]
    return pl.pallas_call(
        functools.partial(late_kernel, side, cut),
        out_shape=(
            jax.ShapeDtypeStruct((3, width, width), jnp.float32),
            jax.ShapeDtypeStruct((4, width, width), jnp.float32),
            jax.ShapeDtypeStruct((depth, width), jnp.float32),
        ),
        in_specs=[SMEM_SPEC] + [VMEM_SPEC] * len(inputs) + [ANY_SPEC],
        out_specs=(ANY_SPEC, ANY_SPEC, VMEM_SPEC),
        input_output_aliases={1 + len(inputs): 1},
        scratch_shapes=[
            pltpu.VMEM((4, rows, width), jnp.float32),
            pltpu.VMEM((3, width, width), jnp.float32),
            pltpu.VMEM((depth, width), jnp.float32),
            pltpu.VMEM((2 * side, width), jnp.float32),
            pltpu.VMEM((width, depth), jnp.bfloat16),
            pltpu.VMEM((width, depth), jnp.bfloat16),
            pltpu.SemaphoreType.DMA((4,)),
            pltpu.SemaphoreType.DMA((3,)),
        ],
        compiler_params=pltpu.CompilerParams(vmem_limit_bytes=34 << 20),
        cost_estimate=pl.CostEstimate(
            flops=12_000_000_000, bytes_accessed=7 * width * width * 4, transcendentals=0
        ),
        name="late",
    )(flags, *inputs, partial)


def final_kernel(side, flags_ref, x_ref, direct_ref, onward_ref, extra_ref, y_ref, given_ref, *refs):
    tiles_ref, _, schur_ref, coupling_ref = refs[:4]
    buffer_ref, tile_ref, near_ref, high_ref, less_ref, sems, ins, outs = refs[4:]
    left_refs = (high_ref, less_ref)
    rows, width = buffer_ref.shape[1:]
    above, under = flags_ref[1] > 0, flags_ref[3] > 0
    taken = pltpu.make_async_copy(tiles_ref.at[2], tile_ref.at[1], ins)
    back = pltpu.make_async_copy(tile_ref.at[1], schur_ref.at[2], outs.at[1])
    beside = pltpu.make_async_copy(tile_ref.at[0], schur_ref.at[1], outs.at[0])

    @pl.when(above)
    def _():
        taken.start()

    copies = put_coupling(
        side,
        width - rows,
        (None, y_ref, None, None),
        x_ref,
        buffer_ref,
        left_refs,
        coupling_ref,
        sems,
        (1,),
    )
    near_ref[...] = given_ref[...]

    @pl.when(above)
    def _():
        keep_halves(left_refs, y_ref[side:, :])

        def put_near(lanes, value):
            near_ref[:side, lanes] = near_ref[:side, lanes] - value

        tall_product(left_refs, side, rows, lambda lanes: buffer_ref[0, :, lanes], put_near, width)
        keep_halves(left_refs, buffer_ref[0].T)
        taken.wait()

        def put_diag(lanes, value):
            tile_ref[1, :, lanes] = tile_ref[1, :, lanes] - value

        tall_product(left_refs, width, rows, lambda lanes: buffer_ref[0, :, lanes], put_diag, width)
        back.start()

    @pl.when(jnp.logical_not(under))
    def _():
        below = direct_ref[...] + onward_ref[...]
        keep_halves(left_refs, jnp.concatenate([below, extra_ref[...]], axis=0).T)

        def put_beside(lanes, value):
            tile_ref[0, :, lanes] = value

        tall_product(left_refs, width, 3 * side, lambda lanes: near_ref[:, lanes], put_beside, width)
        beside.start()
        beside.wait()

    @pl.when(above)
    def _():
        back.wait()

    for copy in copies:
        copy.wait()


def final(flags, x, received, y, near, tiles, coupling, side):
    depth, width = x.shape
    rows = y.shape[1]
    inputs = [x, *received, y, near]
    return pl.pallas_call(
        functools.partial(final_kernel, side),
        out_shape=(
            jax.ShapeDtypeStruct((3, width, width), jnp.float32),
            jax.ShapeDtypeStruct((4, width, width), jnp.float32),
        ),
        in_specs=[SMEM_SPEC] + [VMEM_SPEC] * len(inputs) + [ANY_SPEC] * 2,
        out_specs=(ANY_SPEC, ANY_SPEC),
        input_output_aliases={1 + len(inputs): 0, 2 + len(inputs): 1},
        scratch_shapes=[
            pltpu.VMEM((1, rows, width), jnp.float32),
            pltpu.VMEM((2, width, width), jnp.float32),
            pltpu.VMEM((depth, width), jnp.float32),
            pltpu.VMEM((width, depth), jnp.bfloat16),
            pltpu.VMEM((width, depth), jnp.bfloat16),
            pltpu.SemaphoreType.DMA((4,)),
            pltpu.SemaphoreType.DMA,
            pltpu.SemaphoreType.DMA((2,)),
        ],
        compiler_params=pltpu.CompilerParams(vmem_limit_bytes=24 << 20),
        cost_estimate=pl.CostEstimate(
            flops=4_000_000_000, bytes_accessed=4 * width * width * 4, transcendentals=0
        ),
        name="final",
    )(flags, *inputs, tiles, coupling)


def local(weighted_jacobian_strips, leading_pose_index, levenberg_shift, removal_flags):
    count = lax.axis_size(AXES)
    own = lax.axis_index(AXES)
    surfels, _, width = weighted_jacobian_strips.shape
    capacity = max(2, (3 * surfels + 2 * count - 1) // (2 * count))
    side = count * capacity
    tiles = width // TILE
    bounds = tuple(tiles * k // PARTS for k in range(PARTS + 1))
    starts = tuple(bound * TILE for bound in bounds[:-1])
    flags = removal_flags[(own + jnp.array((0, 1, 2, -1, -2), jnp.int32)) % count]

    chunks = bucketed(
        leading_pose_index.reshape(1, surfels),
        weighted_jacobian_strips.transpose(1, 0, 2),
        count,
        capacity,
    )
    chunks = lax.all_to_all(chunks, AXES, split_axis=0, concat_axis=0, tiled=True)
    x, two, last = regrouped(chunks, capacity, width)

    def sent_parts(parts):
        return [passed_along(part, steps) for part, steps in zip(parts, (1, -1, 2, -2))]

    direct = lax.ppermute(two, AXES, [(k, k + 1) for k in range(0, count, 2)])
    second = passed_along(two, 2)

    def solved(number, start, known):
        before = [part[k] for part in known for k in (0, 3)]
        return factored_part(x, start, before, side, bounds, number)

    low, *part = solved(0, levenberg_shift, ())
    known = [part]
    parts = [sent_parts(part)]
    for number in range(1, PARTS - 1):
        low, *part = solved(number, low, known)
        known.append(part)
        parts.append(sent_parts(part))
    onward = lax.ppermute(second, AXES, [(k + 1, k) for k in range(0, count, 2)])
    extra = passed_along(last, 1)
    low, *part, gram_one, gram_two = solved(PARTS - 1, low, known)
    known.append(part)
    parts.append(sent_parts(part))
    grams = (passed_along(gram_one, 1), passed_along(gram_two, 2))
    partial = early(x, parts[:-1], starts[:-1], side)
    ready = before_last(flags, x, grams, [part[1] for part in known], parts[:-1], side)
    schur, coupling, near = late(
        flags, x, levenberg_shift, second, low, parts[-1], ready, partial, starts[-1], side
    )
    schur, coupling = final(
        flags, x, (direct, onward, extra), parts[-1][1], near, schur, coupling, side
    )
    return schur[None], coupling[None]


def solution(mesh):
    in_specs = (P(AXES, None, None), P(AXES, None), P(AXES, None), P())
    out_specs = (P(AXES, None, None, None), P(AXES, None, None, None))

    return jax.shard_map(local, mesh=mesh, in_specs=in_specs, out_specs=out_specs, check_vma=False)
```

```python
import functools
import math

import jax
import jax.numpy as jnp
from jax import lax
from jax.experimental import pallas as pl
from jax.experimental.pallas import tpu as pltpu
from jax.sharding import PartitionSpec as P


AXES = ("gx", "gy")
TILE = 128
GROUP = 8
WIDE = 256
PARTS = 3
NT = (((1,), (1,)), ((), ()))
TN = (((0,), (0,)), ((), ()))
NN = (((1,), (0,)), ((), ()))
VMEM_SPEC = pl.BlockSpec(memory_space=pltpu.VMEM)
SMEM_SPEC = pl.BlockSpec(memory_space=pltpu.SMEM)
ANY_SPEC = pl.BlockSpec(memory_space=pl.ANY)
PIECES = ((0, 2), (1, 3), (0, 1), (2, 3))


def passed_along(value, steps):
    count = lax.axis_size(AXES)
    pairs = [(source, (source + steps) % count) for source in range(count)]
    return lax.ppermute(value, AXES, pairs)


def product(left, right, dims, precision=lax.Precision.HIGHEST):
    return lax.dot_general(
        left, right, dims, precision=precision, preferred_element_type=jnp.float32
    )


def bucket_kernel(count, capacity, index_ref, strips_ref, out_ref, rows_ref):
    surfels = strips_ref.shape[1]
    width = strips_ref.shape[2]
    lane_tiles = width // WIDE
    index = index_ref[...]
    base = lax.broadcasted_iota(jnp.int32, (count, surfels), 0)
    hot = (base == index).astype(jnp.float32)
    first = lax.broadcasted_iota(jnp.int32, (surfels, surfels), 0)
    second = lax.broadcasted_iota(jnp.int32, (surfels, surfels), 1)
    ahead = (first < second).astype(jnp.float32)
    earlier = product(hot, ahead, NN)
    within = jnp.sum(earlier * hot, axis=0, keepdims=True).astype(jnp.int32)
    period = GROUP // math.gcd(capacity, GROUP)
    for piece in range(3):
        moved = index + piece
        moved = jnp.where(moved >= count, moved - count, moved)
        slot = moved * capacity + within
        row = lax.broadcasted_iota(jnp.int32, (count * capacity, surfels), 0)
        pick = (row == slot).astype(jnp.bfloat16)
        values = strips_ref[piece]
        high = values.astype(jnp.bfloat16)
        rest = values - high.astype(jnp.float32)
        middle = rest.astype(jnp.bfloat16)
        low = (rest - middle.astype(jnp.float32)).astype(jnp.bfloat16)
        rows_ref[...] = product(
            jnp.concatenate([pick, pick, pick], axis=1),
            jnp.concatenate([high, middle, low], axis=0),
            NN,
            lax.Precision.DEFAULT,
        )

        def spread(turn, carry, piece=piece):
            start = pl.multiple_of(turn * (period * capacity), GROUP)
            for tile in range(lane_tiles):
                block = rows_ref[pl.ds(start, period * capacity), WIDE * tile : WIDE * (tile + 1)]
                for member in range(period):
                    begin = (piece * lane_tiles + tile) * capacity
                    out_ref[turn * period + member, begin : begin + capacity, :] = block[
                        member * capacity : (member + 1) * capacity
                    ]
            return carry

        lax.fori_loop(0, count // period, spread, 0)


def bucketed(index_row, strips, count, capacity):
    width = strips.shape[2]
    return pl.pallas_call(
        functools.partial(bucket_kernel, count, capacity),
        out_shape=jax.ShapeDtypeStruct(
            (count, 3 * (width // WIDE) * capacity, WIDE), jnp.float32
        ),
        in_specs=[VMEM_SPEC, VMEM_SPEC],
        out_specs=VMEM_SPEC,
        scratch_shapes=[pltpu.VMEM((count * capacity, width), jnp.float32)],
        name="bucket",
    )(index_row, strips)


def regroup_kernel(capacity, in_ref, out_ref, two_ref, one_ref):
    count = in_ref.shape[0]
    width = out_ref.shape[1]
    lane_tiles = width // WIDE
    period = GROUP // math.gcd(capacity, GROUP)

    def gather(turn, carry):
        for piece in range(3):
            for tile in range(lane_tiles):
                begin = (piece * lane_tiles + tile) * capacity
                block = jnp.concatenate(
                    [
                        in_ref[turn * period + member, begin : begin + capacity, :]
                        for member in range(period)
                    ],
                    axis=0,
                )
                start = pl.multiple_of(
                    piece * count * capacity + turn * (period * capacity), GROUP
                )
                out_ref[
                    pl.ds(start, period * capacity), WIDE * tile : WIDE * (tile + 1)
                ] = block
        return carry

    lax.fori_loop(0, count // period, gather, 0)
    side = count * capacity
    two_ref[...] = out_ref[: 2 * side, :]
    one_ref[...] = out_ref[2 * side :, :]


def regrouped(chunks, capacity, width):
    side = chunks.shape[0] * capacity
    return pl.pallas_call(
        functools.partial(regroup_kernel, capacity),
        out_shape=tuple(
            jax.ShapeDtypeStruct((parts * side, width), jnp.float32) for parts in (3, 2, 1)
        ),
        in_specs=[VMEM_SPEC],
        out_specs=(VMEM_SPEC,) * 3,
        compiler_params=pltpu.CompilerParams(vmem_limit_bytes=16 << 20),
        name="regroup",
    )(chunks)


def full(value):
    return jnp.broadcast_to(value, (GROUP, TILE))


def half_factor(pair_ref, done_ref, start):
    groups = pair_ref.shape[0] // GROUP
    sub = lax.broadcasted_iota(jnp.int32, (GROUP, TILE), 0)
    rows = [pair_ref[GROUP * g : GROUP * (g + 1), :] for g in range(groups)]
    eight = range(GROUP)
    for p in range(groups):
        strip = rows[p]
        cols = [full(strip[:, GROUP * p + k : GROUP * p + k + 1]) for k in eight]
        m = [[full(cols[k][i : i + 1, :]) if k <= i else None for k in eight] for i in eight]
        r = [None] * GROUP
        u = [full(strip[j : j + 1, :]) for j in eight]
        for j in eight:
            r[j] = lax.rsqrt(m[j][j])
            for i in range(j + 1, GROUP):
                m[i][j] = m[i][j] * r[j]
            for k in range(j + 1, GROUP):
                for i in range(k, GROUP):
                    m[i][k] = m[i][k] - m[i][j] * m[k][j]
            u[j] = u[j] * r[j]
            for i in range(j + 1, GROUP):
                u[i] = u[i] - m[i][j] * u[j]
        joined = u[0]
        for j in range(1, GROUP):
            joined = jnp.where(sub == j, u[j], joined)
        done_ref[pl.ds(start + GROUP * p, GROUP), :] = joined
        for g in range(p + 1, groups):
            side = [full(rows[g][:, GROUP * p + k : GROUP * p + k + 1]) for k in eight]
            x = rows[g]
            for j in eight:
                side[j] = side[j] * r[j]
                for i in range(j + 1, GROUP):
                    side[i] = side[i] - m[i][j] * side[j]
                x = x - side[j] * u[j]
            rows[g] = x


def tile_factor(tile, pair_ref, done_ref, cross_ref, corner_ref):
    half = TILE // 2
    row = lax.broadcasted_iota(jnp.int32, (half, half), 0)
    col = lax.broadcasted_iota(jnp.int32, (half, half), 1)
    unit = jnp.where(row == col, 1.0, 0.0).astype(jnp.float32)
    zero = jnp.zeros((half, half), jnp.float32)
    pair_ref[...] = jnp.concatenate([tile[:half, :half], unit], axis=1)
    cross_ref[...] = tile[:half, half:]
    corner_ref[...] = tile[half:, half:]

    def turn(number, carry):
        half_factor(pair_ref, done_ref, pl.multiple_of(number * half, half))

        @pl.when(number == 0)
        def _():
            cross = near_product(done_ref[:half, half:], cross_ref[...], NN)
            cross_ref[...] = cross
            both = halves(cross)
            rest = corner_ref[...] - product_of_halves(both, both, TN)
            pair_ref[...] = jnp.concatenate([rest, unit], axis=1)

        return carry

    lax.fori_loop(0, 2, turn, 0)
    first, second = done_ref[:half, half:], done_ref[half:, half:]
    middle = near_product(cross_ref[...], first, TN)
    upper = jnp.concatenate(
        [
            jnp.concatenate([done_ref[:half, :half], cross_ref[...]], axis=1),
            jnp.concatenate([zero, done_ref[half:, :half]], axis=1),
        ],
        axis=0,
    )
    inverse = jnp.concatenate(
        [
            jnp.concatenate([first, zero], axis=1),
            jnp.concatenate([-near_product(second, middle, NN), second], axis=1),
        ],
        axis=0,
    )
    return upper, inverse


def halves(value):
    high = value.astype(jnp.bfloat16)
    return high, (value - high.astype(jnp.float32)).astype(jnp.bfloat16)


def product_of_halves(left, right, dims):
    total = product(left[0], right[0], dims, lax.Precision.DEFAULT)
    total = total + product(left[0], right[1], dims, lax.Precision.DEFAULT)
    return total + product(left[1], right[0], dims, lax.Precision.DEFAULT)


def lanes_at(number):
    return pl.ds(pl.multiple_of(number * WIDE, WIDE), WIDE)


def tall_product(left_refs, rows, depth, right_at, put, width):
    left = tuple(ref[:rows, :depth] for ref in left_refs)

    def block(number, carry):
        put(lanes_at(number), product_of_halves(left, halves(right_at(lanes_at(number))), NN))
        return carry

    lax.fori_loop(0, width // WIDE, block, 0)


def keep_halves(left_refs, value):
    rows, depth = value.shape
    high, low = halves(value)
    left_refs[0][:rows, :depth] = high
    left_refs[1][:rows, :depth] = low


def piece_shapes(side, lanes):
    return tuple(
        jax.ShapeDtypeStruct(((stop - start) * side, lanes), jnp.float32) for start, stop in PIECES
    )


def part_kernel(side, bounds, number, *refs):
    first, last = bounds[number], bounds[number + 1]
    final = number == len(bounds) - 2
    x_ref, start_ref = refs[:2]
    before = refs[2 : 2 + 2 * number]
    refs = refs[2 + 2 * number :]
    low_ref, outs = refs[0], refs[1:5]
    gram_refs, refs = (refs[5:7], refs[7:]) if final else ((), refs[5:])
    small_refs, refs = refs[:4], refs[4:]
    low_high_ref, low_less_ref, y_high_ref, y_less_ref = refs[:4]
    depth, width = x_ref.shape
    begin, end = first * TILE, last * TILE
    reach = end - TILE
    row = lax.broadcasted_iota(jnp.int32, (TILE, TILE), 0)
    col = lax.broadcasted_iota(jnp.int32, (TILE, TILE), 1)

    if number == 0:
        turned = refs[4:6]
        keep_halves(turned, x_ref[...].T)

        def gram(lanes, value):
            low_ref[:, lanes] = value

        tall_product(turned, width, depth, lambda lanes: x_ref[:, lanes], gram, width)
        for i in range(width // TILE):
            rows = slice(i * TILE, (i + 1) * TILE)
            low_ref[rows, rows] = low_ref[rows, rows] + jnp.where(
                row == col, jnp.broadcast_to(start_ref[:, rows], (TILE, TILE)), 0.0
            )
    else:
        low_ref[...] = start_ref[...]
        high, less = halves(start_ref[:, :begin])
        low_high_ref[:, :begin] = high
        low_less_ref[:, :begin] = less
        for k in range(number):
            lanes = slice(bounds[k] * TILE, bounds[k + 1] * TILE)
            for ref, rows in ((before[2 * k], slice(0, 2 * side)), (before[2 * k + 1], slice(2 * side, 3 * side))):
                high, less = halves(ref[...])
                y_high_ref[rows, lanes] = high
                y_less_ref[rows, lanes] = less
    for ref in (low_high_ref, low_less_ref):
        ref[:, begin:] = jnp.zeros((width, end - begin), jnp.bfloat16)
    for ref in (y_high_ref, y_less_ref):
        ref[:, begin:] = jnp.zeros((depth, end - begin), jnp.bfloat16)

    def step(j, carry):
        start = pl.multiple_of(j * TILE, TILE)
        cols = pl.ds(start, TILE)
        local = pl.ds(pl.multiple_of((j - first) * TILE, TILE), TILE)

        def reduced(value, high_ref, less_ref, rows):
            if reach == 0:
                return value
            return value - product_of_halves(
                (high_ref[rows, :reach], less_ref[rows, :reach]),
                (low_high_ref[cols, :reach], low_less_ref[cols, :reach]),
                NT,
            )

        tile = reduced(low_ref[cols, cols], low_high_ref, low_less_ref, cols)
        upper, inverse = tile_factor(tile, *small_refs)
        inverse = halves(inverse)
        for i in range(depth // side):
            rows = slice(i * side, (i + 1) * side)
            value = reduced(x_ref[rows, cols], y_high_ref, y_less_ref, rows)
            value = product_of_halves(halves(value), inverse, NT)
            for out_ref, (head, tail) in zip(outs, PIECES):
                if head <= i < tail:
                    out_ref[(i - head) * side : (i - head + 1) * side, local] = value
            high, less = halves(value)
            y_high_ref[rows, cols] = high
            y_less_ref[rows, cols] = less
        for i in range(first * TILE // WIDE, width // WIDE):
            rows = slice(i * WIDE, (i + 1) * WIDE)
            value = reduced(low_ref[rows, cols], low_high_ref, low_less_ref, rows)
            value = product_of_halves(halves(value), inverse, NT)
            place = lax.broadcasted_iota(jnp.int32, (WIDE, TILE), 0) + i * WIDE
            value = jnp.where(place >= start + TILE, value, 0.0)
            low_ref[rows, cols] = value
            high, less = halves(value)
            low_high_ref[rows, cols] = high
            low_less_ref[rows, cols] = less
        low_ref[cols, cols] = jnp.where(col <= row, upper.T, 0.0)
        return carry

    lax.fori_loop(first, last, step, 0)
    if number > 0:
        for i in range(first * TILE // WIDE):
            rows = slice(i * WIDE, (i + 1) * WIDE)
            low_ref[rows, begin:end] = jnp.zeros((WIDE, end - begin), jnp.float32)
    if final:
        for gram_ref, left, right in (
            (gram_refs[0], slice(2 * side, 3 * side), slice(0, 2 * side)),
            (gram_refs[1], slice(side, 2 * side), slice(0, side)),
        ):
            gram_ref[...] = product_of_halves(
                (y_high_ref[left, :], y_less_ref[left, :]),
                (y_high_ref[right, :], y_less_ref[right, :]),
                NT,
            )


def factored_part(x, start, before, side, bounds, number):
    depth, width = x.shape
    first, last = bounds[number], bounds[number + 1]
    final = number == len(bounds) - 2
    end = last * TILE
    shapes = [jax.ShapeDtypeStruct((width, width), jnp.float32)]
    shapes += piece_shapes(side, (last - first) * TILE)
    if final:
        shapes += [
            jax.ShapeDtypeStruct((side, 2 * side), jnp.float32),
            jax.ShapeDtypeStruct((side, side), jnp.float32),
        ]
    half = TILE // 2
    scratch = [pltpu.VMEM((half, TILE), jnp.float32), pltpu.VMEM((TILE, TILE), jnp.float32)]
    scratch += [pltpu.VMEM((half, half), jnp.float32)] * 2
    scratch += [pltpu.VMEM((width, end), jnp.bfloat16)] * 2
    scratch += [pltpu.VMEM((depth, end), jnp.bfloat16)] * 2
    if number == 0:
        scratch += [pltpu.VMEM((width, depth), jnp.bfloat16)] * 2
    return pl.pallas_call(
        functools.partial(part_kernel, side, bounds, number),
        out_shape=tuple(shapes),
        in_specs=[VMEM_SPEC] * (2 + len(before)),
        out_specs=(VMEM_SPEC,) * len(shapes),
        scratch_shapes=scratch,
        compiler_params=pltpu.CompilerParams(vmem_limit_bytes=24 << 20),
        cost_estimate=pl.CostEstimate(
            flops=20_000_000_000, bytes_accessed=3 * depth * width * 4, transcendentals=0
        ),
        name="factor_part",
    )(x, start, *before)


def near_product(left, right, dims):
    return product_of_halves(halves(left), halves(right), dims)


COUPLINGS = ((3, 0, 1), (1, 0, 2), (0, 1, 3), (2, 2, 3))


def put_coupling(side, start, y_refs, x_ref, buffer_ref, left_refs, out_ref, sems, places=range(4)):
    rows = buffer_ref.shape[1]
    width = x_ref.shape[1]
    copies = []
    for place in places:
        number, begin, end = COUPLINGS[place]
        slot = place % buffer_ref.shape[0]
        keep_halves(left_refs, y_refs[number][...].T)

        def put(lanes, value, slot=slot):
            buffer_ref[slot, :, lanes] = value

        tall_product(
            left_refs,
            rows,
            (end - begin) * side,
            lambda lanes, begin=begin, end=end: x_ref[begin * side : end * side, lanes],
            put,
            width,
        )
        copy = pltpu.make_async_copy(
            buffer_ref.at[slot], out_ref.at[place, pl.ds(start, rows), :], sems.at[place]
        )
        copy.start()
        copies.append(copy)
    return copies


def early_kernel(side, starts, x_ref, *refs):
    parts = len(starts)
    y_refs, refs = refs[: 4 * parts], refs[4 * parts :]
    out_ref, refs = refs[0], refs[1:]
    buffers, (high_ref, less_ref, sems) = refs[:parts], refs[parts:]
    copies = []
    for number, start in enumerate(starts):
        copies += put_coupling(
            side,
            start,
            y_refs[4 * number : 4 * number + 4],
            x_ref,
            buffers[number],
            (high_ref, less_ref),
            out_ref,
            sems.at[number],
        )
    for copy in copies:
        copy.wait()


def early(x, parts, starts, side):
    width = x.shape[1]
    heights = [part[0].shape[1] for part in parts]
    most = max(heights)
    return pl.pallas_call(
        functools.partial(early_kernel, side, starts),
        out_shape=jax.ShapeDtypeStruct((4, width, width), jnp.float32),
        in_specs=[VMEM_SPEC] * (1 + 4 * len(parts)),
        out_specs=ANY_SPEC,
        scratch_shapes=[pltpu.VMEM((4, height, width), jnp.float32) for height in heights]
        + [
            pltpu.VMEM((most, 2 * side), jnp.bfloat16),
            pltpu.VMEM((most, 2 * side), jnp.bfloat16),
            pltpu.SemaphoreType.DMA((len(parts), 4)),
        ],
        compiler_params=pltpu.CompilerParams(vmem_limit_bytes=24 << 20),
        cost_estimate=pl.CostEstimate(
            flops=8_000_000_000, bytes_accessed=4 * width * width * 4, transcendentals=0
        ),
        name="early",
    )(x, *[piece for part in parts for piece in part])


def before_kernel(side, flags_ref, x_ref, gram_one_ref, gram_two_ref, *refs):
    mine, refs = refs[:PARTS], refs[PARTS:]
    pieces, refs = [refs[4 * k : 4 * k + 4] for k in range(PARTS - 1)], refs[4 * PARTS - 4 :]
    rest_ref, near_ref, far_ref, high_ref, less_ref = refs
    width = x_ref.shape[1]
    own, above, second_above, under, second_under = [flags_ref[k] > 0 for k in range(5)]
    one, two, three = slice(0, side), slice(side, 2 * side), slice(2 * side, 3 * side)
    pair, tail = slice(0, 2 * side), slice(side, 3 * side)
    keep_halves((high_ref, less_ref), x_ref[...].T)
    rest_ref[...] = x_ref[...]
    near_ref[three, :] = jnp.zeros((side, width), jnp.float32)
    far_ref[two, :] = jnp.zeros((side, width), jnp.float32)

    @pl.when(own)
    def _():
        start = 0
        for ref in mine:
            lanes = slice(start, start + ref.shape[1])
            near_ref[pair, lanes] = ref[...]
            far_ref[one, lanes] = ref[side:, :]
            start += ref.shape[1]

    @pl.when(jnp.logical_not(own))
    def _():
        near_ref[pair, :] = x_ref[tail, :]
        far_ref[one, :] = x_ref[three, :]

    def weighed(number, rows):
        gram = 0.0
        for part in pieces:
            both = halves(part[number][...])
            gram = gram + product_of_halves(both, both, NT)
        return near_product(gram, x_ref[rows, :], NN)

    @pl.when(second_above)
    def _():
        rest_ref[one, :] = rest_ref[one, :] - weighed(3, one)

    @pl.when(above)
    def _():
        term = weighed(1, pair)
        rest_ref[pair, :] = rest_ref[pair, :] - term
        near_ref[one, :] = near_ref[one, :] - term[side:]

    @pl.when(under)
    def _():
        term = weighed(0, tail)
        rest_ref[tail, :] = rest_ref[tail, :] - term
        far_ref[one, :] = far_ref[one, :] - term[side:]
        far_ref[two, :] = -near_product(gram_one_ref[...], x_ref[tail, :], NN)

    @pl.when(second_under)
    def _():
        term = weighed(2, three)
        rest_ref[three, :] = rest_ref[three, :] - term
        near_ref[two, :] = near_ref[two, :] - term
        near_ref[three, :] = -near_product(gram_two_ref[...], x_ref[three, :], NN)


def before_last(flags, x, grams, mine, parts, side):
    depth, width = x.shape
    inputs = [x, *grams, *mine] + [piece for part in parts for piece in part]
    return pl.pallas_call(
        functools.partial(before_kernel, side),
        out_shape=(
            jax.ShapeDtypeStruct((depth, width), jnp.float32),
            jax.ShapeDtypeStruct((depth, width), jnp.float32),
            jax.ShapeDtypeStruct((2 * side, width), jnp.float32),
            jax.ShapeDtypeStruct((width, depth), jnp.bfloat16),
            jax.ShapeDtypeStruct((width, depth), jnp.bfloat16),
        ),
        in_specs=[SMEM_SPEC] + [VMEM_SPEC] * len(inputs),
        out_specs=(VMEM_SPEC,) * 5,
        compiler_params=pltpu.CompilerParams(vmem_limit_bytes=24 << 20),
        cost_estimate=pl.CostEstimate(
            flops=4_000_000_000, bytes_accessed=4 * width * width * 4, transcendentals=0
        ),
        name="before_last",
    )(flags, *inputs)


def late_kernel(side, cut, flags_ref, *refs):
    x_ref, shift_ref, second_ref, low_ref = refs[:4]
    lasts, ready, refs = (refs[4], None, *refs[5:7]), refs[7:12], refs[12:]
    partial_ref, schur_ref, coupling_ref, near_ref = refs[:4]
    buffer_ref, tile_ref, rest_ref, far_ref, high_ref, less_ref, sems, outs = refs[4:]
    left_refs = (high_ref, less_ref)
    width = x_ref.shape[1]
    rows = width - cut
    copies = put_coupling(
        side, cut, lasts, x_ref, buffer_ref, left_refs, coupling_ref, sems, (0, 3, 2)
    )
    own, _, second_above, under, second_under = [flags_ref[k] > 0 for k in range(5)]
    for ref, given in zip((rest_ref, near_ref, far_ref), ready):
        ref[...] = given[...]

    def take_off(flag, place, targets):
        number, begin, end = COUPLINGS[place]
        height = (end - begin) * side

        @pl.when(flag)
        def _():
            keep_halves(left_refs, lasts[number][...])

            def put(lanes, value):
                for ref, there, here, amount in targets:
                    ref[there : there + amount, lanes] = (
                        ref[there : there + amount, lanes] - value[here : here + amount]
                    )

            tall_product(
                left_refs, height, rows, lambda lanes: buffer_ref[place, :, lanes], put, width
            )

    take_off(second_above, 0, ((rest_ref, 0, 0, side),))
    take_off(under, 2, ((rest_ref, side, 0, 2 * side), (far_ref, 0, side, side)))
    take_off(second_under, 3, ((rest_ref, 2 * side, 0, side), (near_ref, side, 0, side)))

    def put(place):
        return pltpu.make_async_copy(tile_ref.at[place], schur_ref.at[place], outs.at[place])

    def fill(place, halved, depth, right_ref):
        def store(lanes, value):
            tile_ref[place, :, lanes] = value

        tall_product(halved, width, depth, lambda lanes: right_ref[:, lanes], store, width)

    def from_coupling(place, member):
        copy = pltpu.make_async_copy(
            partial_ref.at[member, pl.ds(0, cut), :],
            tile_ref.at[place, pl.ds(0, cut), :],
            outs.at[place],
        )
        copy.start()
        tile_ref[place, cut:, :] = buffer_ref[member]
        copy.wait()

    @pl.when(own)
    def _():
        tile_ref[2] = low_ref[...]

    @pl.when(jnp.logical_not(own))
    def _():
        fill(2, ready[3:], 3 * side, rest_ref)
        for i in range(width // TILE):
            rows = slice(i * TILE, (i + 1) * TILE)
            row = lax.broadcasted_iota(jnp.int32, (TILE, TILE), 0)
            col = lax.broadcasted_iota(jnp.int32, (TILE, TILE), 1)
            tile_ref[2, rows, rows] = tile_ref[2, rows, rows] + jnp.where(
                row == col, jnp.broadcast_to(shift_ref[:, rows], (TILE, TILE)), 0.0
            )

    put(2).start()

    @pl.when(under)
    def _():
        from_coupling(1, 2)

    @pl.when(under)
    def _():
        put(1).start()

    @pl.when(second_under)
    def _():
        from_coupling(0, 3)

    @pl.when(jnp.logical_not(second_under))
    def _():
        keep_halves(left_refs, second_ref[...].T)
        fill(0, left_refs, 2 * side, far_ref)

    put(0).start()

    @pl.when(under)
    def _():
        put(1).wait()

    put(2).wait()
    put(0).wait()
    for copy in copies:
        copy.wait()


def late(flags, x, shift, second, low, lasts, ready, partial, cut, side):
    depth, width = x.shape
    rows = width - cut
    inputs = [x, shift, second, low, lasts[0], *lasts[2:], *ready]
    return pl.pallas_call(
        functools.partial(late_kernel, side, cut),
        out_shape=(
            jax.ShapeDtypeStruct((3, width, width), jnp.float32),
            jax.ShapeDtypeStruct((4, width, width), jnp.float32),
            jax.ShapeDtypeStruct((depth, width), jnp.float32),
        ),
        in_specs=[SMEM_SPEC] + [VMEM_SPEC] * len(inputs) + [ANY_SPEC],
        out_specs=(ANY_SPEC, ANY_SPEC, VMEM_SPEC),
        input_output_aliases={1 + len(inputs): 1},
        scratch_shapes=[
            pltpu.VMEM((4, rows, width), jnp.float32),
            pltpu.VMEM((3, width, width), jnp.float32),
            pltpu.VMEM((depth, width), jnp.float32),
            pltpu.VMEM((2 * side, width), jnp.float32),
            pltpu.VMEM((width, depth), jnp.bfloat16),
            pltpu.VMEM((width, depth), jnp.bfloat16),
            pltpu.SemaphoreType.DMA((4,)),
            pltpu.SemaphoreType.DMA((3,)),
        ],
        compiler_params=pltpu.CompilerParams(vmem_limit_bytes=34 << 20),
        cost_estimate=pl.CostEstimate(
            flops=12_000_000_000, bytes_accessed=7 * width * width * 4, transcendentals=0
        ),
        name="late",
    )(flags, *inputs, partial)


def beside_kernel(flags_ref, direct_ref, onward_ref, extra_ref, near_ref, tiles_ref, schur_ref, tile_ref, high_ref, less_ref, sem):
    width = near_ref.shape[1]

    @pl.when(flags_ref[3] <= 0)
    def _():
        below = direct_ref[...] + onward_ref[...]
        left_refs = (high_ref, less_ref)
        keep_halves(left_refs, jnp.concatenate([below, extra_ref[...]], axis=0).T)

        def put(lanes, value):
            tile_ref[:, lanes] = value

        tall_product(
            left_refs, width, near_ref.shape[0], lambda lanes: near_ref[:, lanes], put, width
        )
        copy = pltpu.make_async_copy(tile_ref, schur_ref.at[1], sem)
        copy.start()
        copy.wait()


def beside(flags, received, near, tiles):
    depth, width = near.shape
    inputs = [*received, near]
    return pl.pallas_call(
        beside_kernel,
        out_shape=jax.ShapeDtypeStruct((3, width, width), jnp.float32),
        in_specs=[SMEM_SPEC] + [VMEM_SPEC] * len(inputs) + [ANY_SPEC],
        out_specs=ANY_SPEC,
        input_output_aliases={1 + len(inputs): 0},
        scratch_shapes=[
            pltpu.VMEM((width, width), jnp.float32),
            pltpu.VMEM((width, depth), jnp.bfloat16),
            pltpu.VMEM((width, depth), jnp.bfloat16),
            pltpu.SemaphoreType.DMA,
        ],
        compiler_params=pltpu.CompilerParams(vmem_limit_bytes=16 << 20),
        cost_estimate=pl.CostEstimate(
            flops=3_000_000_000, bytes_accessed=2 * width * width * 4, transcendentals=0
        ),
        name="beside",
    )(flags, *inputs, tiles)


def final_kernel(side, flags_ref, x_ref, direct_ref, onward_ref, y_ref, *refs):
    tiles_ref, _, schur_ref, coupling_ref = refs[:4]
    buffer_ref, tile_ref, small_ref, high_ref, less_ref, sems, ins, outs = refs[4:]
    left_refs = (high_ref, less_ref)
    rows, width = buffer_ref.shape[1:]
    above = flags_ref[1] > 0
    taken = pltpu.make_async_copy(tiles_ref.at[2], tile_ref.at[1], ins.at[1])
    taken_beside = pltpu.make_async_copy(tiles_ref.at[1], tile_ref.at[0], ins.at[0])
    back = pltpu.make_async_copy(tile_ref.at[1], schur_ref.at[2], outs.at[1])
    beside = pltpu.make_async_copy(tile_ref.at[0], schur_ref.at[1], outs.at[0])

    @pl.when(above)
    def _():
        taken.start()
        taken_beside.start()

    copies = put_coupling(
        side,
        width - rows,
        (None, y_ref, None, None),
        x_ref,
        buffer_ref,
        left_refs,
        coupling_ref,
        sems,
        (1,),
    )

    @pl.when(above)
    def _():
        keep_halves(left_refs, y_ref[side:, :])

        def put_small(lanes, value):
            small_ref[:, lanes] = value

        tall_product(left_refs, side, rows, lambda lanes: buffer_ref[0, :, lanes], put_small, width)
        keep_halves(left_refs, buffer_ref[0].T)
        taken.wait()

        def put_diag(lanes, value):
            tile_ref[1, :, lanes] = tile_ref[1, :, lanes] - value

        tall_product(left_refs, width, rows, lambda lanes: buffer_ref[0, :, lanes], put_diag, width)
        back.start()
        keep_halves(left_refs, (direct_ref[:side, :] + onward_ref[:side, :]).T)
        taken_beside.wait()

        def put_beside(lanes, value):
            tile_ref[0, :, lanes] = tile_ref[0, :, lanes] - value

        tall_product(left_refs, width, side, lambda lanes: small_ref[:, lanes], put_beside, width)
        beside.start()
        beside.wait()

    @pl.when(above)
    def _():
        back.wait()

    for copy in copies:
        copy.wait()


def final(flags, x, received, y, tiles, coupling, side):
    depth, width = x.shape
    rows = y.shape[1]
    inputs = [x, *received, y]
    return pl.pallas_call(
        functools.partial(final_kernel, side),
        out_shape=(
            jax.ShapeDtypeStruct((3, width, width), jnp.float32),
            jax.ShapeDtypeStruct((4, width, width), jnp.float32),
        ),
        in_specs=[SMEM_SPEC] + [VMEM_SPEC] * len(inputs) + [ANY_SPEC] * 2,
        out_specs=(ANY_SPEC, ANY_SPEC),
        input_output_aliases={1 + len(inputs): 0, 2 + len(inputs): 1},
        scratch_shapes=[
            pltpu.VMEM((1, rows, width), jnp.float32),
            pltpu.VMEM((2, width, width), jnp.float32),
            pltpu.VMEM((side, width), jnp.float32),
            pltpu.VMEM((width, depth), jnp.bfloat16),
            pltpu.VMEM((width, depth), jnp.bfloat16),
            pltpu.SemaphoreType.DMA((4,)),
            pltpu.SemaphoreType.DMA((2,)),
            pltpu.SemaphoreType.DMA((2,)),
        ],
        compiler_params=pltpu.CompilerParams(vmem_limit_bytes=24 << 20),
        cost_estimate=pl.CostEstimate(
            flops=4_000_000_000, bytes_accessed=4 * width * width * 4, transcendentals=0
        ),
        name="final",
    )(flags, *inputs, tiles, coupling)


def local(weighted_jacobian_strips, leading_pose_index, levenberg_shift, removal_flags):
    count = lax.axis_size(AXES)
    own = lax.axis_index(AXES)
    surfels, _, width = weighted_jacobian_strips.shape
    capacity = max(2, (3 * surfels + 2 * count - 1) // (2 * count))
    side = count * capacity
    tiles = width // TILE
    bounds = tuple(tiles * k // PARTS for k in range(PARTS + 1))
    starts = tuple(bound * TILE for bound in bounds[:-1])
    flags = removal_flags[(own + jnp.array((0, 1, 2, -1, -2), jnp.int32)) % count]

    chunks = bucketed(
        leading_pose_index.reshape(1, surfels),
        weighted_jacobian_strips.transpose(1, 0, 2),
        count,
        capacity,
    )
    chunks = lax.all_to_all(chunks, AXES, split_axis=0, concat_axis=0, tiled=True)
    x, two, last = regrouped(chunks, capacity, width)

    def sent_parts(parts):
        return [passed_along(part, steps) for part, steps in zip(parts, (1, -1, 2, -2))]

    direct = lax.ppermute(two, AXES, [(k, k + 1) for k in range(0, count, 2)])
    second = passed_along(two, 2)

    def solved(number, start, known):
        before = [part[k] for part in known for k in (0, 3)]
        return factored_part(x, start, before, side, bounds, number)

    low, *part = solved(0, levenberg_shift, ())
    known = [part]
    parts = [sent_parts(part)]
    for number in range(1, PARTS - 1):
        low, *part = solved(number, low, known)
        known.append(part)
        parts.append(sent_parts(part))
    onward = lax.ppermute(second, AXES, [(k + 1, k) for k in range(0, count, 2)])
    extra = passed_along(last, 1)
    low, *part, gram_one, gram_two = solved(PARTS - 1, low, known)
    known.append(part)
    parts.append(sent_parts(part))
    grams = (passed_along(gram_one, 1), passed_along(gram_two, 2))
    partial = early(x, parts[:-1], starts[:-1], side)
    ready = before_last(flags, x, grams, [part[1] for part in known], parts[:-1], side)
    schur, coupling, near = late(
        flags, x, levenberg_shift, second, low, parts[-1], ready, partial, starts[-1], side
    )
    schur = beside(flags, (direct, onward, extra), near, schur)
    schur, coupling = final(flags, x, (direct, onward), parts[-1][1], schur, coupling, side)
    return schur[None], coupling[None]


def solution(mesh):
    in_specs = (P(AXES, None, None), P(AXES, None), P(AXES, None), P())
    out_specs = (P(AXES, None, None, None), P(AXES, None, None, None))

    return jax.shard_map(local, mesh=mesh, in_specs=in_specs, out_specs=out_specs, check_vma=False)
```
